256 devices in a mesh: macro: 4 (over x), micro: 64 (over y, z, core).
Axes of the slice: x: 4, y: 4, z: 8, core: 2. Of those that a mesh axis runs over, the one named last changes fastest.
Arguments:
- displacement: float32 [3, 8, 128, 256], P(None, 'macro', 'micro'), may hold values from -6 to 6
- load: float32 [3, 8, 128, 256], P(None, 'macro', 'micro'), may hold values from -6 to 6
- routes: int32 [4, 64, 1024, 1], P('macro', 'micro'), may hold values from 0 to 63; in each aligned block of 1024 rows (0 to 1023, 1024 to 2047, ..., all dimensions but the last counted through in order) at most 32 rows name the same one
- counts: int32 [4, 64, 1024], P('macro', 'micro'), may hold values from 1 to 4
- stiffness: bfloat16 [64, 512, 512], P('micro'), may hold values from -0.5 to 2.5, as said below
- precond: bfloat16 [64, 512, 512], P('micro'), may hold values from -0.5 to 2.5, as said below
- forcing: bfloat16 [64, 6, 512], P('micro'), may hold values from -2.5 to 2.5
- coupling: bfloat16 [64, 512, 6], P('micro'), may hold values from -0.25 to 0.25
- lame_first: float32 [64], P('micro'), may hold values from 0.5 to 2
- lame_shear: float32 [64], P('micro'), may hold values from 0.5 to 2
Outputs:
- increment: float32 [3, 8, 128, 256], P(None, 'macro', 'micro')
- residual: float32 [3, 8, 128, 256], P(None, 'macro', 'micro')
The draws below stay inside these ranges and needn't reach their ends.
Inputs may be any that keep to these rules, and one draw needn't show every extreme that they name: `routes`: among the points of one block (one device's points), no owner is named by more than 32 points, a bound that some block reaches. `stiffness`: Symmetric. `precond`: Symmetric.
All inputs are finite; a program needn't handle non-finite values.
Results may differ from the reference program's by a relative error of at most 0.002.
Values sent between devices are 32-bit elements; how exact they have to be, the bound alone decides.
No kernel may reach another device: no remote copies, remote signals or barrier semaphores. Data moves between devices by JAX's collectives and lax.ppermute only.
A program may use at most 64 MiB of HBM per device.

```python
import math
import jax
import jax.numpy as jnp
import numpy as np
from jax import lax

CX = 2
CY = 2
MODES = 512
ITMAX = 4
ITERS = 5
P_DEV = 1024
CAP = 32
MODELS = 64
NX = 8
NY = 128
NZ = 256
N_MACRO = 4
N_MICRO = 64


def model_scale(key):
    return jnp.exp(jax.random.uniform(jax.random.fold_in(key, 7), (MODELS,), jnp.float32, math.log(0.7), math.log(1.4)))


def model_matrix(key, scale):
    gauss = jax.random.truncated_normal(key, -4.0, 4.0, (MODELS, MODES, MODES), jnp.float32) / jnp.sqrt(MODES * 1.0)
    symmetric = (gauss + jnp.swapaxes(gauss, 1, 2)) / 2.9
    identity = jnp.eye(MODES, dtype=jnp.float32)
    return scale[:, None, None] * (identity[None] + 0.45 * symmetric)


def draw_stiffness(key, part):
    scale = model_scale(key)
    return model_matrix(jax.random.fold_in(key, 11), scale).astype(jnp.bfloat16)


def draw_precond(key, part):
    scale = model_scale(key)
    return model_matrix(jax.random.fold_in(key, 13), 1.0 / scale).astype(jnp.bfloat16)


def plant(values, stream_key, least, top_value):
    shape = values.shape
    spot = [jax.random.randint(jax.random.fold_in(stream_key, axis), (), 0, shape[axis]) for axis in range(len(shape))]
    values = values.at[tuple(spot)].set(least)
    longest = shape.index(max(shape))
    spot[longest] = (spot[longest] + 1) % shape[longest]
    return values.at[tuple(spot)].set(top_value)


def block_levels(key, shape, pieces, smallest, largest):
    def one(axis_at, shards_of):
        heights = jax.random.uniform(jax.random.fold_in(jax.random.fold_in(key, 6), axis_at), (shards_of,), jnp.float32, smallest / len(pieces), largest / len(pieces))
        return jnp.repeat(jnp.exp(heights), shape[axis_at] // shards_of).reshape((-1,) + (1,) * (len(shape) - axis_at - 1))

    loudness = one(*pieces[0])
    for cut in pieces[1:]:
        loudness = loudness * one(*cut)
    return loudness


def deal_out(key, own, number, rows, amount, top, reach, lean):
    sequence = jax.random.permutation(key, amount)
    packed, common = shares(amount, rows * top, reach, lean, True), shares(amount, rows * top, reach, lean, False)
    places = jnp.arange(amount)

    def named(sizes, rotation):
        used = int((sizes > 0).sum())
        fixed = max(1, used // 4)
        shifted = fixed + (places - fixed + rotation * (used - fixed)) % max(1, amount - fixed)
        return jnp.zeros((amount,), jnp.int32).at[sequence[jnp.where(places < fixed, places, shifted)]].set(jnp.asarray(sizes, jnp.int32))

    sizes = jnp.where(number % 4 == 0, named(packed, number // 4), named(common, number - number // 4 - 1))
    mixed = jax.random.permutation(jax.random.fold_in(own, 3), amount)
    source_of, taker = mixed[0:amount // 2 * 2:2], mixed[1:amount // 2 * 2:2]
    room = jnp.minimum(sizes[source_of] - 1, reach - sizes[taker]) // 2
    room = jnp.where((source_of == sequence[0]) | (taker == sequence[0]) | (sizes[taker] == 0), 0, jnp.maximum(room, 0))
    shifted = jax.random.randint(jax.random.fold_in(own, 4), (amount // 2,), 0, 1 << 20) % (room + 1)
    sizes = sizes.at[source_of].add(-shifted).at[taker].add(shifted)
    members = jnp.searchsorted(jnp.cumsum(sizes), jnp.arange(rows * top), side="right").astype(jnp.int32)
    table = members.reshape(top, rows).T
    table = table[jax.random.permutation(jax.random.fold_in(own, 1), rows)]
    rotation = jax.random.randint(jax.random.fold_in(own, 2), (rows, 1), 0, top)
    return jnp.take_along_axis(table, (jnp.arange(top)[None, :] + rotation) % top, axis=1)


def shares(amount, total, reach, lean, full):
    loads = [(1 << 20) // math.isqrt(grade ** lean) + 1 for grade in range(1, amount + 1)]
    largest = reach if full else min(reach, max(-(-total // amount), total * loads[0] // sum(loads)))
    least = 1 if total - largest >= amount - 1 else 0
    holding, spare = [largest] + [least] * (amount - 1), total - largest - least * (amount - 1)
    while spare > 0:
        candidates = [i for i in range(1, amount) if holding[i] < largest] or [i for i in range(1, amount) if holding[i] < reach]
        whole, budget = sum([loads[i] for i in candidates]), spare
        for i in candidates:
            more = min(reach - holding[i], max(1, budget * loads[i] // whole), spare)
            holding[i] = holding[i] + more
            spare = spare - more
    return np.array(holding)


def normal_values(key, dims, spread, reach, cuts=(), held_as=jnp.bfloat16):
    values = jax.random.normal(key, dims, jnp.float32) * spread
    if len(cuts) > 0:
        values = block_levels(key, dims, cuts, -0.22, 0.18) * values
    return jnp.clip(values, min=-reach, max=reach).astype(held_as)


def setup_inputs(seed: int = 0) -> dict:
    keys = jax.random.split(jax.random.key(seed), 11)
    displacement = normal_values(keys[0], (3, NX, NY, NZ), 1.0, 6.0, ((1, 4), (2, 64)), jnp.float32)
    load = normal_values(keys[1], (3, NX, NY, NZ), 1.0, 6.0, ((1, 4), (2, 64)), jnp.float32)
    routes_keys = jax.random.split(jax.random.fold_in(keys[2], 1), N_MACRO * N_MICRO * P_DEV // P_DEV)
    routes_turns = jax.random.permutation(jax.random.fold_in(keys[2], 3), N_MACRO * N_MICRO * P_DEV // P_DEV)
    routes = jax.vmap(lambda own, number: deal_out(jax.random.fold_in(keys[2], 2), own, number, P_DEV, N_MICRO, 1, CAP, 2))(routes_keys, routes_turns).reshape((N_MACRO, N_MICRO, P_DEV, 1))
    counts = plant(jax.random.randint(keys[3], (N_MACRO, N_MICRO, P_DEV), 1, ITMAX + 1), jax.random.fold_in(keys[3], 1), 1, ITMAX).astype(jnp.int32)
    stiffness = draw_stiffness(jax.random.fold_in(keys[10], 71), 0)
    precond = draw_precond(jax.random.fold_in(keys[10], 71), 0)
    forcing = normal_values(keys[6], (MODELS, 6, MODES), 6 ** -0.5, 2.5, ((0, 64),))
    coupling = normal_values(keys[7], (MODELS, MODES, 6), MODES ** -0.5, 0.25, ((0, 64),))
    lame_first = jnp.clip(jnp.exp(math.log(2.0) - 1.3862944 * jax.random.uniform(keys[8], (MODELS,), jnp.float32) ** block_levels(keys[8], (MODELS,), ((0, 64),), -0.2, 0.2)), 0.5, 2.0)
    lame_shear = jnp.clip(jnp.exp(math.log(2.0) - 1.3862944 * jax.random.uniform(keys[9], (MODELS,), jnp.float32) ** block_levels(keys[9], (MODELS,), ((0, 64),), -0.2, 0.2)), 0.5, 2.0)
    return {"displacement": displacement, "load": load, "routes": routes, "counts": counts, "stiffness": stiffness, "precond": precond, "forcing": forcing, "coupling": coupling, "lame_first": lame_first, "lame_shear": lame_shear}


BETA = 0.1
OMEGA = 0.8
MASS = 0.1
VOIGT = ((0, 5, 4), (5, 1, 3), (4, 3, 2))
ALL_PAIRS = tuple((first_axis, second_axis) for first_axis in range(6) for second_axis in range(6))


def element_strain(nodes):
    count_x = nodes.shape[1] - 1
    count_y = nodes.shape[2] - 1
    count_z = nodes.shape[3]
    padded = jnp.pad(nodes, ((0, 0), (0, 0), (0, 0), (0, 1)))
    zeros = jnp.zeros((3, count_x, count_y, count_z), jnp.float32)
    grad_x, grad_y, grad_z = zeros, zeros, zeros
    for corner_x in (0, 1):
        for corner_y in (0, 1):
            for corner_z in (0, 1):
                piece = padded[:, corner_x:corner_x + count_x, corner_y:corner_y + count_y, corner_z:corner_z + count_z]
                grad_x = grad_x + (0.25 * (2 * corner_x - 1)) * piece
                grad_y = grad_y + (0.25 * (2 * corner_y - 1)) * piece
                grad_z = grad_z + (0.25 * (2 * corner_z - 1)) * piece
    return jnp.stack([grad_x[0], grad_y[1], grad_z[2], grad_z[1] + grad_y[2], grad_z[0] + grad_x[2], grad_y[0] + grad_x[1]])


def node_force(stress):
    count_x, count_y, count_z = stress.shape[1], stress.shape[2], stress.shape[3]
    forces = jnp.zeros((3, count_x + 1, count_y + 1, count_z + 1), jnp.float32)
    for corner_x in (0, 1):
        for corner_y in (0, 1):
            for corner_z in (0, 1):
                signs = (2 * corner_x - 1, 2 * corner_y - 1, 2 * corner_z - 1)
                parts = []
                for component in range(3):
                    table = VOIGT[component]
                    parts.append(0.25 * (signs[0] * stress[table[0]] + signs[1] * stress[table[1]] + signs[2] * stress[table[2]]))
                contrib = jnp.stack(parts)
                forces = forces + jnp.pad(contrib, ((0, 0), (corner_x, 1 - corner_x), (corner_y, 1 - corner_y), (corner_z, 1 - corner_z)))
    return forces


def micro_solve(strain, sweeps, stiffness, precond, forcing, coupling, lame_first, lame_shear, pairs):
    strain_half = strain.astype(jnp.bfloat16)
    modal_load = lax.dot_general(strain_half, forcing, (((0,), (0,)), ((), ())), preferred_element_type=jnp.float32)
    modes = jnp.zeros_like(modal_load)
    for sweep in range(ITMAX):
        misfit = jnp.dot(modes.astype(jnp.bfloat16), stiffness, preferred_element_type=jnp.float32) + BETA * jnp.tanh(modes) - modal_load
        update = modes - OMEGA * jnp.dot(misfit.astype(jnp.bfloat16), precond, preferred_element_type=jnp.float32)
        modes = jnp.where((sweeps[0] > sweep)[:, None], update, modes)
    trace = strain[0] + strain[1] + strain[2]
    elastic = jnp.stack([lame_first * trace + 2.0 * lame_shear * strain[0], lame_first * trace + 2.0 * lame_shear * strain[1], lame_first * trace + 2.0 * lame_shear * strain[2], lame_shear * strain[3], lame_shear * strain[4], lame_shear * strain[5]])
    stress = elastic + lax.dot_general(coupling, modes.astype(jnp.bfloat16), (((0,), (1,)), ((), ())), preferred_element_type=jnp.float32)
    slope = 1.0 - jnp.tanh(modes) ** 2
    wide = coupling.astype(jnp.float32)
    products = jnp.stack([wide[:, pair[0]] * wide[:, pair[1]] for pair in pairs], axis=1)
    extra = lax.dot_general(products, slope, (((0,), (1,)), ((), ())), precision=lax.Precision.HIGHEST, preferred_element_type=jnp.float32)
    base = jnp.stack([lame_first * float(pair[0] < 3 and pair[1] < 3) + lame_shear * (2.0 * float(pair[0] == pair[1] and pair[0] < 3) + float(pair[0] == pair[1] and pair[0] >= 3)) for pair in pairs])
    return jnp.concatenate([stress, extra + base[:, None]], axis=0)


def operate(field, tangent):
    padded = jnp.pad(field, ((0, 0), (0, 1), (0, 1), (0, 0)))
    strain = element_strain(padded)
    stress = jnp.sum(tangent * strain[None], axis=1)
    return MASS * field + node_force(stress)[:, :-1, :-1, :-1]


def reference(displacement, load, routes, counts, stiffness, precond, forcing, coupling, lame_first, lame_shear):
    strain_all = element_strain(jnp.pad(displacement, ((0, 0), (0, 1), (0, 1), (0, 0))))
    points = strain_all.reshape(6, N_MACRO, CX, N_MICRO, CY, NZ).transpose(0, 1, 3, 2, 4, 5).reshape(6, N_MACRO, N_MICRO, P_DEV)
    owner_of = routes[..., 0]
    onehot = (owner_of[..., None] == jnp.arange(N_MICRO, dtype=jnp.int32)).astype(jnp.int32)
    ranks = jnp.sum((jnp.cumsum(onehot, axis=2) - 1) * onehot, axis=-1)
    target = (owner_of * CAP + ranks).astype(jnp.int32)
    macro_index = jnp.arange(N_MACRO, dtype=jnp.int32)[:, None, None]
    source_index = jnp.arange(N_MICRO, dtype=jnp.int32)[None, :, None]
    strain_buffer = jnp.zeros((6, N_MACRO, N_MICRO, N_MICRO * CAP), jnp.float32).at[:, macro_index, source_index, target].set(points)
    sweep_buffer = jnp.zeros((N_MACRO, N_MICRO, N_MICRO * CAP), jnp.int32).at[macro_index, source_index, target].set(counts)
    strain_owner = strain_buffer.reshape(6, N_MACRO, N_MICRO, N_MICRO, CAP).transpose(3, 0, 1, 2, 4).reshape(N_MICRO, 6, N_MACRO * N_MICRO * CAP)
    sweep_owner = sweep_buffer.reshape(N_MACRO, N_MICRO, N_MICRO, CAP).transpose(2, 0, 1, 3).reshape(N_MICRO, 1, N_MACRO * N_MICRO * CAP)

    def solve_owner(bundle):
        return micro_solve(bundle[0], bundle[1], bundle[2], bundle[3], bundle[4], bundle[5], bundle[6], bundle[7], ALL_PAIRS)

    results = lax.map(solve_owner, (strain_owner, sweep_owner, stiffness, precond, forcing, coupling, lame_first, lame_shear))
    back = results.reshape(N_MICRO, 42, N_MACRO, N_MICRO, CAP).transpose(1, 2, 3, 0, 4).reshape(42, N_MACRO, N_MICRO, N_MICRO * CAP)
    picked = jnp.take_along_axis(back, target[None], axis=3)
    values = picked.reshape(42, N_MACRO, N_MICRO, CX, CY, NZ).transpose(0, 1, 3, 2, 4, 5).reshape(42, NX, NY, NZ)
    stress = values[:6]
    tangent = values[6:].reshape(6, 6, NX, NY, NZ)
    rhs = load - node_force(stress)[:, :-1, :-1, :-1]
    increment = jnp.zeros_like(rhs)
    residual, direction = rhs, rhs
    norm_now = jnp.sum(residual * residual)
    for step in range(ITERS):
        image = operate(direction, tangent)
        alpha = norm_now / jnp.sum(direction * image)
        increment = increment + alpha * direction
        residual = residual - alpha * image
        norm_next = jnp.sum(residual * residual)
        direction = residual + (norm_next / norm_now) * direction
        norm_now = norm_next
    return increment, residual
```

```python
import jax
import jax.numpy as jnp
from jax import lax
from jax.experimental import pallas as pl
from jax.experimental.pallas import tpu as pltpu
from jax.sharding import Mesh
from jax.sharding import PartitionSpec as P

ITMAX = 4
MICRO = ("micro_0", "micro_1", "micro_2")

BETA = 0.1
OMEGA = 0.8
MASS = 0.1
VOIGT = ((0, 5, 4), (5, 1, 3), (4, 3, 2))
PAIRS = tuple((i, j) for i in range(6) for j in range(i, 6))
TANGENT = {}
for number, (i, j) in enumerate(PAIRS):
    TANGENT[i, j] = TANGENT[j, i] = 6 + number
ROWS = 27
LOAD = 27
FIELDS = 30
DOTS = 128
F32 = jnp.float32
BF16 = jnp.bfloat16


def micro_kernel(strain_ref, stiff_ref, pre_ref, force_ref, maps_ref, cols_ref, out_ref):
    stiff = stiff_ref[...]
    pre = pre_ref[...]
    halves = 2
    width = strain_ref.shape[1] // halves
    loads, modes, sweeps = [], [], []
    for h in range(halves):
        part = strain_ref[:, h * width : (h + 1) * width]
        load = jnp.dot(force_ref[...], part.astype(BF16), preferred_element_type=F32)
        loads.append(load)
        sweeps.append(part[6:7])
    for h in range(halves):
        modes.append(OMEGA * jnp.dot(pre, loads[h].astype(BF16), preferred_element_type=F32))
    for sweep in range(1, ITMAX):
        misfits = []
        for h in range(halves):
            misfit = (
                jnp.dot(stiff, modes[h].astype(BF16), preferred_element_type=F32)
                + BETA * jnp.tanh(modes[h])
                - loads[h]
            )
            misfits.append(misfit.astype(BF16))
        for h in range(halves):
            update = modes[h] - OMEGA * jnp.dot(pre, misfits[h], preferred_element_type=F32)
            modes[h] = jnp.where(sweeps[h] > sweep, update, modes[h])
    couple, high, low = maps_ref[0], maps_ref[1], maps_ref[2]
    cols = cols_ref[...]
    for h in range(halves):
        at = slice(h * width, (h + 1) * width)
        bent = jnp.tanh(modes[h])
        slope = 1.0 - bent * bent
        slope_high = slope.astype(BF16)
        slope_low = (slope - slope_high.astype(F32)).astype(BF16)
        rows = (
            jnp.dot(couple, modes[h].astype(BF16), preferred_element_type=F32)
            + jnp.dot(high, slope_high, preferred_element_type=F32)
            + jnp.dot(low, slope_high, preferred_element_type=F32)
            + jnp.dot(high, slope_low, preferred_element_type=F32)
            + cols[:, 0:1]
        )
        part = strain_ref[:, at]
        trace = part[0:1] + part[1:2] + part[2:3]
        elastic = cols[:8, 1:2] * trace + cols[:8, 2:3] * part
        out_ref[:8, at] = rows[:8] + elastic
        out_ref[8:, at] = rows[8:]


def micro_solve(points, stiffness, precond, forcing, coupling, lame_first, lame_shear):
    modes = stiffness.shape[0]
    count = points.shape[1]
    tile = 512
    force = jnp.pad(forcing, ((0, 2), (0, 0))).T
    wide = coupling.astype(F32).T
    products = jnp.stack([wide[i] * wide[j] for i, j in PAIRS])
    high = products.astype(BF16)
    low = (products - high.astype(F32)).astype(BF16)
    maps = jnp.stack(
        [
            jnp.pad(coupling.T, ((0, 26), (0, 0))),
            jnp.pad(high, ((6, 5), (0, 0))),
            jnp.pad(low, ((6, 5), (0, 0))),
        ]
    )
    base_first = [0.0] * 6 + [float(i < 3 and j < 3) for i, j in PAIRS] + [0.0] * 5
    base_shear = (
        [0.0] * 6
        + [2.0 * float(i == j and i < 3) + float(i == j and i >= 3) for i, j in PAIRS]
        + [0.0] * 5
    )
    on_trace = [1.0] * 3 + [0.0] * 29
    on_strain = [2.0] * 3 + [1.0] * 3 + [0.0] * 26
    cols = jnp.stack(
        [
            lame_first * jnp.array(base_first, F32) + lame_shear * jnp.array(base_shear, F32),
            lame_first * jnp.array(on_trace, F32),
            lame_shear * jnp.array(on_strain, F32),
        ]
        + [jnp.zeros((32,), F32)] * 5,
        axis=1,
    )
    whole = lambda *shape: pl.BlockSpec(shape, lambda step: (0,) * len(shape))
    return pl.pallas_call(
        micro_kernel,
        grid=(count // tile,),
        in_specs=[
            pl.BlockSpec((8, tile), lambda step: (0, step)),
            whole(modes, modes),
            whole(modes, modes),
            whole(modes, 8),
            whole(3, 32, modes),
            whole(32, 8),
        ],
        out_specs=pl.BlockSpec((32, tile), lambda step: (0, step)),
        out_shape=jax.ShapeDtypeStruct((32, count), F32),
        compiler_params=pltpu.CompilerParams(vmem_limit_bytes=48 * 1024 * 1024),
        name="micro_solve",
    )(points, stiffness, precond, force, maps, cols)


def shifts(shape):
    plane = lax.broadcasted_iota(jnp.int32, shape, 0)
    column = lax.broadcasted_iota(jnp.int32, shape, 1)
    planes, columns = shape

    def next_x(v):
        return jnp.where(plane == planes - 1, 0.0, pltpu.roll(v, planes - 1, 0))

    def prev_x(v):
        return jnp.where(plane == 0, 0.0, pltpu.roll(v, 1, 0))

    def next_z(v):
        return jnp.where(column == columns - 1, 0.0, pltpu.roll(v, columns - 1, 1))

    def prev_z(v):
        return jnp.where(column == 0, 0.0, pltpu.roll(v, 1, 1))

    return next_x, prev_x, next_z, prev_z


def strain_rows(nodes, lower, upper, moves):
    next_x, _, next_z, _ = moves
    sums, diffs = {}, {}
    for y in range(lower, upper + 2):
        for c in range(3):
            v = nodes[y][c]
            w = next_z(v)
            sums[y, c] = v + w
            diffs[y, c] = w - v
    strain = {}
    for y in range(lower, upper + 1):
        grad = []
        for c in range(3):
            both = sums[y, c] + sums[y + 1, c]
            rise = sums[y + 1, c] - sums[y, c]
            turn = diffs[y, c] + diffs[y + 1, c]
            grad.append(
                (
                    0.25 * (next_x(both) - both),
                    0.25 * (next_x(rise) + rise),
                    0.25 * (next_x(turn) + turn),
                )
            )
        strain[y] = (
            grad[0][0],
            grad[1][1],
            grad[2][2],
            grad[1][2] + grad[2][1],
            grad[0][2] + grad[2][0],
            grad[0][1] + grad[1][0],
        )
    return strain


def force_rows(stress, lower, upper, moves):
    _, prev_x, _, prev_z = moves
    xs = {}
    for y in range(lower - 1, upper + 1):
        for c in range(3):
            a, b, d = (stress[y][VOIGT[c][k]] for k in range(3))
            xs[y, c] = (prev_x(a) - a, prev_x(b) + b, prev_x(d) + d)
    force = {}
    for y in range(lower, upper + 1):
        parts = []
        for c in range(3):
            a0, b0, d0 = xs[y - 1, c]
            a1, b1, d1 = xs[y, c]
            flat = (a0 + a1) + (b0 - b1)
            deep = d0 + d1
            parts.append(0.25 * (prev_z(flat + deep) + (flat - deep)))
        force[y] = tuple(parts)
    return force


def apply_rows(nodes, tangent, lower, upper, moves):
    strain = strain_rows(nodes, lower - 1, upper, moves)
    stress = {}
    for y in range(lower - 1, upper + 1):
        rows = []
        for i in range(6):
            total = tangent(y, TANGENT[i, 0]) * strain[y][0]
            for j in range(1, 6):
                total = total + tangent(y, TANGENT[i, j]) * strain[y][j]
            rows.append(total)
        stress[y] = tuple(rows)
    force = force_rows(stress, lower, upper, moves)
    return {
        y: tuple(MASS * nodes[y][c] + force[y][c] for c in range(3))
        for y in range(lower, upper + 1)
    }


def value_reader(low_ref, own_ref, high_ref):
    def read(y, c):
        if y < 0:
            return low_ref[c, y + 2]
        if y < 2:
            return own_ref[c, y]
        return high_ref[c, y - 2]

    return read


def read_rows(ref, lower, count):
    return {lower + k: tuple(ref[c, k] for c in range(3)) for k in range(count)}


def inside(rows, y, last_ref):
    keep = jnp.where(last_ref[0] == 1, 0.0, 1.0)
    rows[y] = tuple(v * keep for v in rows[y])


def write_rows(ref, rows, lower, count):
    for k in range(count):
        for c in range(3):
            ref[c, k] = rows[lower + k][c]


def row_dot(first, second):
    total = None
    for y in (0, 1):
        for c in range(3):
            term = first[y][c] * second[y][c]
            total = term if total is None else total + term
    return total


def pack_dots(ref, products):
    lane = lax.broadcasted_iota(jnp.int32, (1, DOTS), 1)
    packed = jnp.zeros((1, DOTS), F32)
    for k, product in enumerate(products):
        total = jnp.sum(jnp.sum(product, axis=0, keepdims=True), axis=1, keepdims=True)
        packed = packed + jnp.where(lane == k, total, 0.0)
    ref[...] = packed


def unpack_dots(ref, count):
    row = jnp.sum(ref[...], axis=0, keepdims=True)
    lane = lax.broadcasted_iota(jnp.int32, (1, DOTS), 1)
    return [
        jnp.sum(jnp.where(lane == k, row, 0.0), axis=1, keepdims=True) for k in range(count)
    ]


def first_kernel(last_ref, low_ref, own_ref, high_ref, v0_ref, v1_ref):
    read = value_reader(low_ref, own_ref, high_ref)
    moves = shifts(own_ref.shape[2:])
    stress = {y: tuple(read(y, i) for i in range(6)) for y in range(-2, 3)}
    force = force_rows(stress, -1, 2, moves)
    v0 = {y: tuple(read(y, LOAD + c) - force[y][c] for c in range(3)) for y in range(-1, 3)}
    inside(v0, 2, last_ref)
    v1 = apply_rows(v0, read, 0, 1, moves)
    write_rows(v0_ref, v0, -1, 4)
    write_rows(v1_ref, v1, 0, 2)


def second_kernel(
    last_ref, low_ref, own_ref, high_ref, v0_ref, v1_low_ref, v1_ref, v1_high_ref, v2_ref, dots_ref
):
    read = value_reader(low_ref, own_ref, high_ref)
    moves = shifts(own_ref.shape[2:])
    v1 = read_rows(v1_low_ref, -2, 2) | read_rows(v1_ref, 0, 2) | read_rows(v1_high_ref, 2, 2)
    v2 = apply_rows(v1, read, -1, 2, moves)
    inside(v2, 2, last_ref)
    v0 = read_rows(v0_ref, -1, 4)
    write_rows(v2_ref, v2, -1, 4)
    pack_dots(
        dots_ref,
        [
            row_dot(a, b)
            for a, b in ((v0, v0), (v0, v1), (v0, v2), (v1, v1), (v1, v2))
        ],
    )


def third_kernel(
    low_ref,
    own_ref,
    high_ref,
    v0_ref,
    v1_low_ref,
    v1_ref,
    v1_high_ref,
    v2_ref,
    sums_ref,
    r1_ref,
    r2_ref,
    w3_ref,
    coef_ref,
):
    read = value_reader(low_ref, own_ref, high_ref)
    moves = shifts(own_ref.shape[2:])
    m00, m01, m02, m11, m12 = unpack_dots(sums_ref, 5)
    a0 = m00 / m01
    n1 = m00 - 2.0 * a0 * m01 + a0 * a0 * m11
    b0 = n1 / m00
    e = 1.0 + b0
    a1 = n1 / (e * e * m01 - e * a0 * (m02 + m11) + a0 * a0 * m12)
    center = 0.5 * (1.0 / a0 + 1.0 / a1 + b0 / a0)
    v0 = read_rows(v0_ref, -1, 4)
    v1 = read_rows(v1_low_ref, -2, 2) | read_rows(v1_ref, 0, 2) | read_rows(v1_high_ref, 2, 2)
    v2 = read_rows(v2_ref, -1, 4)
    along, twice = a0 + a1 * e, a1 * a0
    r2 = {
        y: tuple(v0[y][c] - along * v1[y][c] + twice * v2[y][c] for c in range(3))
        for y in range(-1, 3)
    }
    image = apply_rows(r2, read, 0, 1, moves)
    scale = 1.0 / center
    w3 = {y: tuple(image[y][c] * scale - r2[y][c] for c in range(3)) for y in (0, 1)}
    r1 = {y: tuple(v0[y][c] - a0 * v1[y][c] for c in range(3)) for y in (0, 1)}
    write_rows(r1_ref, r1, 0, 2)
    write_rows(r2_ref, r2, 0, 2)
    write_rows(w3_ref, w3, 0, 2)
    lane = lax.broadcasted_iota(jnp.int32, (1, DOTS), 1)
    packed = jnp.zeros((1, DOTS), F32)
    for k, value in enumerate((a0, b0, a1, n1, center)):
        packed = packed + jnp.where(lane == k, value, 0.0)
    coef_ref[...] = packed


def basis_pairs():
    return [(i, j) for i in range(6) for j in range(i, 6)]


def fourth_kernel(
    last_ref,
    low_ref,
    own_ref,
    high_ref,
    coef_ref,
    v0_ref,
    r1_ref,
    r2_ref,
    w3_low_ref,
    w3_ref,
    w3_high_ref,
    w4_ref,
    w5_ref,
    dots_ref,
):
    read = value_reader(low_ref, own_ref, high_ref)
    moves = shifts(own_ref.shape[2:])
    scale = 1.0 / unpack_dots(coef_ref, 5)[4]
    w3 = read_rows(w3_low_ref, -2, 2) | read_rows(w3_ref, 0, 2) | read_rows(w3_high_ref, 2, 2)
    image = apply_rows(w3, read, -1, 2, moves)
    w4 = {y: tuple(image[y][c] * scale - w3[y][c] for c in range(3)) for y in range(-1, 3)}
    inside(w4, 2, last_ref)
    image = apply_rows(w4, read, 0, 1, moves)
    w5 = {y: tuple(image[y][c] * scale - w4[y][c] for c in range(3)) for y in (0, 1)}
    write_rows(w4_ref, w4, 0, 2)
    write_rows(w5_ref, w5, 0, 2)
    v0 = read_rows(v0_ref, -1, 4)
    basis = [v0, read_rows(r1_ref, 0, 2), read_rows(r2_ref, 0, 2), w3, w4, w5]
    pack_dots(dots_ref, [row_dot(basis[i], basis[j]) for i, j in basis_pairs()])


def total_of(terms):
    total = None
    for term in terms:
        total = term if total is None else total + term
    return total


def fifth_kernel(
    coef_ref, sums_ref, v0_ref, r1_ref, r2_ref, w3_ref, w4_ref, w5_ref, increment_ref, residual_ref
):
    a0, b0, a1, n1, center = unpack_dots(coef_ref, 5)
    dots = unpack_dots(sums_ref, 21)
    gram = {}
    for k, (i, j) in enumerate(basis_pairs()):
        gram[i, j] = gram[j, i] = dots[k]
    zero = jnp.zeros((1, 1), F32)
    one = jnp.ones((1, 1), F32)
    i0, i1 = 1.0 / a0, 1.0 / a1

    def image_of(p):
        return [
            i0 * p[0] - b0 * i0 * p[1],
            (i1 + b0 * i0) * p[1] - i0 * p[0],
            center * p[2] - i1 * p[1],
            center * (p[2] + p[3]),
            center * (p[3] + p[4]),
            center * p[4],
        ]

    def product(p, q):
        return total_of(
            p[i] * total_of(gram[i, j] * q[j] for j in range(6)) for i in range(6)
        )

    solved = [a0 + a1 * b0, a1, zero, zero, zero, zero]
    left = [zero, zero, one, zero, zero, zero]
    norm = gram[2, 2]
    ratio = norm / n1
    course = [ratio * b0, ratio, one, zero, zero, zero]
    for step in range(3):
        image = image_of(course)
        alpha = norm / product(course, image)
        solved = [s + alpha * p for s, p in zip(solved, course)]
        left = [r - alpha * q for r, q in zip(left, image)]
        if step < 2:
            fresh = product(left, left)
            ratio = fresh / norm
            course = [r + ratio * p for r, p in zip(left, course)]
            norm = fresh
    v0 = read_rows(v0_ref, -1, 4)
    basis = [v0] + [read_rows(ref, 0, 2) for ref in (r1_ref, r2_ref, w3_ref, w4_ref, w5_ref)]
    for y in (0, 1):
        for c in range(3):
            increment_ref[c, y] = total_of(solved[k] * basis[k][y][c] for k in range(6))
            residual_ref[c, y] = total_of(left[k] * basis[k][y][c] for k in range(6))


def local_call(kernel, outs, name, *args, flag=None):
    specs = [pl.BlockSpec(memory_space=pltpu.VMEM)] * len(args)
    if flag is not None:
        specs = [pl.BlockSpec(memory_space=pltpu.SMEM)] + specs
        args = (flag,) + args
    return pl.pallas_call(
        kernel,
        in_specs=specs,
        out_specs=[pl.BlockSpec(memory_space=pltpu.VMEM)] * len(outs),
        out_shape=[jax.ShapeDtypeStruct(shape, F32) for shape in outs],
        compiler_params=pltpu.CompilerParams(vmem_limit_bytes=48 * 1024 * 1024),
        name=name,
    )(*args)


def up_and_down(up, down):
    count = lax.axis_size(MICRO)
    forward = [(k, k + 1) for k in range(count - 1)]
    backward = [(k + 1, k) for k in range(count - 1)]
    return lax.ppermute(up, MICRO, forward), lax.ppermute(down, MICRO, backward)


def summands(packed):
    count = lax.axis_size(MICRO)
    sent = jnp.broadcast_to(packed[None], (count, 1, DOTS))
    got = lax.all_to_all(sent, MICRO, split_axis=0, concat_axis=0, tiled=True)
    return got.reshape(count, DOTS)


def gather_planes(block):
    count = lax.axis_size("macro")
    pieces = [block] + [
        lax.ppermute(block, "macro", [(k, (k - shift) % count) for k in range(count)])
        for shift in range(1, count)
    ]
    planes = block.shape[2]
    twice = jnp.concatenate(pieces + pieces[:-1], axis=2)
    start = (count - lax.axis_index("macro")) % count * planes
    return lax.dynamic_slice_in_dim(twice, start, count * planes, axis=2)


def element_strain(nodes):
    padded = jnp.pad(nodes, ((0, 0), (0, 0), (0, 0), (0, 1)))

    def pair(v, axis):
        size = v.shape[axis] - 1
        first = lax.slice_in_dim(v, 0, size, axis=axis)
        second = lax.slice_in_dim(v, 1, size + 1, axis=axis)
        return first + second, second - first

    sum_z, diff_z = pair(padded, 3)
    sum_yz, diff_yz = pair(sum_z, 2)
    sum_yd, _ = pair(diff_z, 2)
    grad_x = 0.25 * pair(sum_yz, 1)[1]
    grad_y = 0.25 * pair(diff_yz, 1)[0]
    grad_z = 0.25 * pair(sum_yd, 1)[0]
    return jnp.stack(
        [
            grad_x[0],
            grad_y[1],
            grad_z[2],
            grad_z[1] + grad_y[2],
            grad_z[0] + grad_x[2],
            grad_y[0] + grad_x[1],
        ]
    )


def with_next(block, axis, dim):
    count = lax.axis_size(axis)
    high = lax.ppermute(
        lax.slice_in_dim(block, 0, 1, axis=dim), axis, [(k + 1, k) for k in range(count - 1)]
    )
    return jnp.concatenate([block, high], axis=dim)


def shards(
    displacement,
    load,
    routes,
    counts,
    stiffness,
    precond,
    forcing,
    coupling,
    lame_first,
    lame_shear,
):
    planes, width, depth = displacement.shape[1:]
    points = planes * width * depth
    owners = lax.axis_size(MICRO)
    capacity = max(2, 2 * points // owners)
    slots = owners * capacity

    owner_of = routes.reshape(points)
    chosen = owner_of[:, None] == jnp.arange(owners, dtype=jnp.int32)[None, :]
    before = jnp.tri(points, points, -1, dtype=BF16)
    earlier = jnp.dot(before, chosen.astype(BF16), preferred_element_type=F32)
    ranks = jnp.sum(jnp.where(chosen, earlier, 0.0), axis=1).astype(jnp.int32)
    target = owner_of * capacity + ranks

    strain = element_strain(with_next(with_next(displacement, "macro", 1), MICRO, 2))
    leaving = jnp.concatenate(
        [strain.reshape(6, points), counts.reshape(1, points).astype(F32)], axis=0
    )
    send = jnp.zeros((7, slots), F32).at[:, target].set(
        leaving, unique_indices=True, mode="promise_in_bounds"
    )
    send = send.reshape(7, owners, capacity).transpose(1, 0, 2).reshape(owners, 1, 7 * capacity)
    got = lax.all_to_all(send, MICRO, split_axis=0, concat_axis=0, tiled=True)
    got = got.reshape(owners, 7, capacity).transpose(1, 0, 2).reshape(7, slots)
    rows = micro_solve(
        jnp.pad(got, ((0, 1), (0, 0))),
        stiffness[0],
        precond[0],
        forcing[0],
        coupling[0],
        lame_first[0],
        lame_shear[0],
    )
    back = rows[:ROWS].reshape(ROWS, owners, capacity).transpose(1, 0, 2)
    back = lax.all_to_all(
        back.reshape(owners, 1, ROWS * capacity), MICRO, split_axis=0, concat_axis=0, tiled=True
    )
    back = back.reshape(owners, ROWS, capacity).transpose(1, 0, 2).reshape(ROWS, slots)
    picked = jnp.take(back, target, axis=1, mode="clip")
    values = jnp.concatenate([picked.reshape(ROWS, planes, width, depth), load], axis=0)
    own = gather_planes(values.transpose(0, 2, 1, 3))
    low, high = up_and_down(own, own[:, :1])
    sets = (low, own, high)
    last = (lax.axis_index(MICRO) == owners - 1).astype(jnp.int32).reshape(1)
    whole = own.shape[2]
    two = (3, 2, whole, depth)
    four = (3, 4, whole, depth)
    line = (1, DOTS)
    v0, v1 = local_call(first_kernel, (four, two), "first_rows", *sets, flag=last)
    v1_low, v1_high = up_and_down(v1, v1)
    v2, dots = local_call(
        second_kernel, (four, line), "second_rows", *sets, v0, v1_low, v1, v1_high, flag=last
    )
    r1, r2, w3, coef = local_call(
        third_kernel,
        (two, two, two, line),
        "third_rows",
        *sets,
        v0,
        v1_low,
        v1,
        v1_high,
        v2,
        summands(dots),
    )
    w3_low, w3_high = up_and_down(w3, w3)
    w4, w5, dots = local_call(
        fourth_kernel,
        (two, two, line),
        "fourth_rows",
        *sets,
        coef,
        v0,
        r1,
        r2,
        w3_low,
        w3,
        w3_high,
        flag=last,
    )
    increment, residual = local_call(
        fifth_kernel, (two, two), "fifth_rows", coef, summands(dots), v0, r1, r2, w3, w4, w5
    )
    start = lax.axis_index("macro") * planes

    def mine(field):
        return lax.dynamic_slice_in_dim(field, start, planes, axis=2).transpose(0, 2, 1, 3)

    return (mine(increment), mine(residual))


def solution(mesh):
    split = Mesh(
        mesh.devices.reshape(mesh.shape["macro"], 4, 8, 2),
        ("macro", "micro_0", "micro_1", "micro_2"),
    )
    placed = (
        P(None, "macro", MICRO, None),
        P(None, "macro", MICRO, None),
        P("macro", MICRO, None, None),
        P("macro", MICRO, None),
        P(MICRO, None, None),
        P(MICRO, None, None),
        P(MICRO, None, None),
        P(MICRO, None, None),
        P(MICRO),
        P(MICRO),
    )
    return jax.shard_map(
        shards,
        mesh=split,
        in_specs=placed,
        out_specs=(P(None, "macro", MICRO, None), P(None, "macro", MICRO, None)),
        check_vma=False,
    )
```

```python
import jax
import jax.numpy as jnp
import numpy as np
from jax import lax
from jax.experimental import pallas as pl
from jax.experimental.pallas import tpu as pltpu
from jax.sharding import Mesh
from jax.sharding import PartitionSpec as P

ITMAX = 4
MICRO = ("micro_0", "micro_1", "micro_2")

BETA = 0.1
OMEGA = 0.8
MASS = 0.1
VOIGT = ((0, 5, 4), (5, 1, 3), (4, 3, 2))
PAIRS = tuple((i, j) for i in range(6) for j in range(i, 6))
TANGENT = {}
for number, (i, j) in enumerate(PAIRS):
    TANGENT[i, j] = TANGENT[j, i] = 6 + number
ROWS = 27
LOAD = 27
FIELDS = 30
DOTS = 128
BASIS = 3.2
MARK = 7 * 32 - 128
F32 = jnp.float32
BF16 = jnp.bfloat16


def three_parts(value):
    high = value.astype(BF16)
    rest = value - high.astype(F32)
    middle = rest.astype(BF16)
    return high, middle, (rest - middle.astype(F32)).astype(BF16)


def hot_rows(count, index):
    return lax.broadcasted_iota(jnp.int32, (count, index.shape[1]), 0) == index


def dispatch_kernel(
    mark_ref, routes_ref, counts_ref, own_ref, right_ref, above_ref, corner_ref, send_ref, place_ref
):
    owners = send_ref.shape[0]
    depth = own_ref.shape[3]
    capacity = 32
    column = lax.broadcasted_iota(jnp.int32, (3, depth), 1)
    sums, diffs = {}, {}
    for x in range(3):
        for y in range(3):
            ref = ((own_ref, above_ref), (right_ref, corner_ref))[x // 2][y // 2]
            node = ref[:, x % 2, y % 2, :]
            after = jnp.where(column == depth - 1, 0.0, pltpu.roll(node, depth - 1, 1))
            sums[x, y] = node + after
            diffs[x, y] = after - node
    blocks = []
    for x in range(2):
        for y in range(2):
            s00, s01, s10, s11 = sums[x, y], sums[x, y + 1], sums[x + 1, y], sums[x + 1, y + 1]
            grad_x = 0.25 * ((s10 + s11) - (s00 + s01))
            grad_y = 0.25 * ((s01 + s11) - (s00 + s10))
            grad_z = 0.25 * (
                (diffs[x, y] + diffs[x, y + 1]) + (diffs[x + 1, y] + diffs[x + 1, y + 1])
            )
            blocks.append(
                jnp.concatenate(
                    [
                        grad_x[0:1],
                        grad_y[1:2],
                        grad_z[2:3],
                        grad_z[1:2] + grad_y[2:3],
                        grad_z[0:1] + grad_x[2:3],
                        grad_y[0:1] + grad_x[1:2],
                    ],
                    axis=0,
                )
            )
    values = jnp.concatenate(blocks, axis=1)
    owner = routes_ref[...]
    chosen = jnp.where(hot_rows(owners, owner), 1.0, 0.0)
    pieces = [chosen[:, k * depth : (k + 1) * depth] for k in range(4)]
    earlier = lax.broadcasted_iota(jnp.int32, (depth, depth), 0) < lax.broadcasted_iota(
        jnp.int32, (depth, depth), 1
    )
    within = jnp.dot(
        jnp.concatenate(pieces, axis=0).astype(BF16),
        jnp.where(earlier, 1.0, 0.0).astype(BF16),
        preferred_element_type=F32,
    )
    running = jnp.zeros((owners, 1), F32)
    ranks = []
    for k in range(4):
        seen = within[k * owners : (k + 1) * owners] + running
        ranks.append(jnp.sum(pieces[k] * seen, axis=0, keepdims=True))
        running = running + jnp.sum(pieces[k], axis=1, keepdims=True)
    rank = jnp.concatenate(ranks, axis=1).astype(jnp.int32)
    place_ref[0:1] = owner
    place_ref[1:2] = rank
    at_rank = hot_rows(capacity, rank)
    leaving = jnp.concatenate([values, counts_ref[...].astype(F32)], axis=0)
    chosen = chosen.astype(BF16)
    total = None
    for part in three_parts(leaving):
        part = part.astype(F32)
        spread = [jnp.where(at_rank, part[c : c + 1], 0.0) for c in range(7)]
        spread.append(jnp.zeros_like(spread[0]))
        term = lax.dot_general(
            chosen,
            jnp.concatenate(spread, axis=0).astype(BF16),
            (((1,), (1,)), ((), ())),
            preferred_element_type=F32,
        )
        total = term if total is None else total + term
    lane = lax.broadcasted_iota(jnp.int32, (owners, 128), 1)
    send_ref[:, 0, :] = total[:, :128]
    send_ref[:, 1, :] = jnp.where(lane >= MARK, mark_ref[...], total[:, 128:])


def micro_kernel(
    got_ref,
    stiff_ref,
    pre_ref,
    force_ref,
    couple_ref,
    products_ref,
    cols_ref,
    out_ref,
    marks_ref,
    points_ref,
):
    tile = pl.program_id(0)
    owners = got_ref.shape[0]

    @pl.when(tile == 0)
    def _():
        points_ref[:128] = got_ref[:, 0, :].T
        second = got_ref[:, 1, :]
        points_ref[128:] = second.T
        marks_ref[...] = jnp.sum(second, axis=0, keepdims=True)

    stiff = stiff_ref[...]
    pre = pre_ref[...]
    halves = 2
    parts, loads, modes, sweeps = [], [], [], []
    for h in range(halves):
        part = jnp.concatenate(
            [points_ref[pl.ds(tile * 8 + h * 4 + k, 8, stride=32), :] for k in range(4)], axis=1
        )
        parts.append(part)
        loads.append(jnp.dot(force_ref[...], part.astype(BF16), preferred_element_type=F32))
        sweeps.append(part[6:7])
    for h in range(halves):
        modes.append(OMEGA * jnp.dot(pre, loads[h].astype(BF16), preferred_element_type=F32))
    for sweep in range(1, ITMAX):
        misfits = []
        for h in range(halves):
            misfit = (
                jnp.dot(stiff, modes[h].astype(BF16), preferred_element_type=F32)
                + BETA * jnp.tanh(modes[h])
                - loads[h]
            )
            misfits.append(misfit.astype(BF16))
        for h in range(halves):
            update = modes[h] - OMEGA * jnp.dot(pre, misfits[h], preferred_element_type=F32)
            modes[h] = jnp.where(sweeps[h] > sweep, update, modes[h])
    couple = couple_ref[...]
    products = products_ref[...]
    high = products.astype(BF16)
    low = (products - high.astype(F32)).astype(BF16)
    cols = cols_ref[...]
    for h in range(halves):
        bent = jnp.tanh(modes[h])
        slope = 1.0 - bent * bent
        slope_high = slope.astype(BF16)
        slope_low = (slope - slope_high.astype(F32)).astype(BF16)
        rows = (
            jnp.dot(couple, modes[h].astype(BF16), preferred_element_type=F32)
            + jnp.dot(high, slope_high, preferred_element_type=F32)
            + jnp.dot(low, slope_high, preferred_element_type=F32)
            + jnp.dot(high, slope_low, preferred_element_type=F32)
            + cols[:, 0:1]
        )
        part = parts[h]
        trace = part[0:1] + part[1:2] + part[2:3]
        elastic = cols[:8, 1:2] * trace + cols[:8, 2:3] * part
        rows = jnp.concatenate([rows[:8] + elastic, rows[8:]], axis=0)
        turned = []
        for k in range(2):
            pair = rows[:, k * 2 * owners : (k + 1) * 2 * owners].T
            turned += [pair[:owners], pair[owners:]]
        out_ref[:, pl.ds(tile * 2 + h, 1), :] = jnp.concatenate(turned, axis=1)[:, None, :]


def micro_solve(got, stiffness, precond, forcing, coupling, lame_first, lame_shear):
    modes = stiffness.shape[0]
    owners = got.shape[0]
    force = jnp.pad(forcing, ((0, 2), (0, 0))).T
    wide = coupling.astype(F32).T
    products = jnp.pad(jnp.stack([wide[i] * wide[j] for i, j in PAIRS]), ((6, 5), (0, 0)))
    couple = jnp.pad(coupling.T, ((0, 26), (0, 0)))
    base_first = [0.0] * 6 + [float(i < 3 and j < 3) for i, j in PAIRS] + [0.0] * 5
    base_shear = (
        [0.0] * 6
        + [2.0 * float(i == j and i < 3) + float(i == j and i >= 3) for i, j in PAIRS]
        + [0.0] * 5
    )
    on_trace = [1.0] * 3 + [0.0] * 29
    on_strain = [2.0] * 3 + [1.0] * 3 + [0.0] * 26
    firsts = np.zeros((32, 8), np.float32)
    shears = np.zeros((32, 8), np.float32)
    firsts[:, 0], firsts[:, 1] = base_first, on_trace
    shears[:, 0], shears[:, 2] = base_shear, on_strain
    cols = lame_first * firsts + lame_shear * shears
    whole = lambda *shape: pl.BlockSpec(shape, lambda step: (0,) * len(shape))
    return pl.pallas_call(
        micro_kernel,
        grid=(4,),
        in_specs=[
            whole(owners, 2, 128),
            whole(modes, modes),
            whole(modes, modes),
            whole(modes, 8),
            whole(32, modes),
            whole(32, modes),
            whole(32, 8),
        ],
        out_specs=[whole(owners, 8, 128), whole(1, 128)],
        out_shape=[
            jax.ShapeDtypeStruct((owners, 8, 128), F32),
            jax.ShapeDtypeStruct((1, 128), F32),
        ],
        scratch_shapes=[pltpu.VMEM((256, owners), F32)],
        compiler_params=pltpu.CompilerParams(vmem_limit_bytes=48 * 1024 * 1024),
        name="micro_solve",
    )(got, stiffness, precond, force, couple, products, cols)


def pick_kernel(back_ref, place_ref, load_ref, out_ref):
    owners = back_ref.shape[0]
    depth = out_ref.shape[3]
    owner = place_ref[0:1]
    rank = place_ref[1:2]
    chosen = jnp.where(hot_rows(owners, owner), 1.0, 0.0).astype(BF16)
    chosen = jnp.concatenate([chosen] * 3, axis=0)
    total = jnp.zeros((32, owner.shape[1]), F32)
    for s in range(8):
        turned = back_ref[:, s, :].T
        split = jnp.concatenate(three_parts(turned), axis=1)
        candidates = jnp.dot(split, chosen, preferred_element_type=F32)
        for k in range(4):
            total = total + jnp.where(
                rank == s * 4 + k, candidates[k * 32 : (k + 1) * 32], 0.0
            )
    for x in range(2):
        for y in range(2):
            at = (x * 2 + y) * depth
            out_ref[:ROWS, y, x, :] = total[:ROWS, at : at + depth]
            out_ref[ROWS:, y, x, :] = load_ref[:, x, y, :]


def shifts(shape):
    plane = lax.broadcasted_iota(jnp.int32, shape, 0)
    column = lax.broadcasted_iota(jnp.int32, shape, 1)
    planes, columns = shape

    def next_x(v):
        return jnp.where(plane == planes - 1, 0.0, pltpu.roll(v, planes - 1, 0))

    def prev_x(v):
        return jnp.where(plane == 0, 0.0, pltpu.roll(v, 1, 0))

    def next_z(v):
        return jnp.where(column == columns - 1, 0.0, pltpu.roll(v, columns - 1, 1))

    def prev_z(v):
        return jnp.where(column == 0, 0.0, pltpu.roll(v, 1, 1))

    return next_x, prev_x, next_z, prev_z


def strain_rows(nodes, lower, upper, moves):
    next_x, _, next_z, _ = moves
    sums, diffs = {}, {}
    for y in range(lower, upper + 2):
        for c in range(3):
            v = nodes[y][c]
            w = next_z(v)
            sums[y, c] = v + w
            diffs[y, c] = w - v
    strain = {}
    for y in range(lower, upper + 1):
        grad = []
        for c in range(3):
            both = sums[y, c] + sums[y + 1, c]
            rise = sums[y + 1, c] - sums[y, c]
            turn = diffs[y, c] + diffs[y + 1, c]
            grad.append(
                (
                    0.25 * (next_x(both) - both),
                    0.25 * (next_x(rise) + rise),
                    0.25 * (next_x(turn) + turn),
                )
            )
        strain[y] = (
            grad[0][0],
            grad[1][1],
            grad[2][2],
            grad[1][2] + grad[2][1],
            grad[0][2] + grad[2][0],
            grad[0][1] + grad[1][0],
        )
    return strain


def force_rows(stress, lower, upper, moves):
    _, prev_x, _, prev_z = moves
    xs = {}
    for y in range(lower - 1, upper + 1):
        for c in range(3):
            a, b, d = (stress[y][VOIGT[c][k]] for k in range(3))
            xs[y, c] = (prev_x(a) - a, prev_x(b) + b, prev_x(d) + d)
    force = {}
    for y in range(lower, upper + 1):
        parts = []
        for c in range(3):
            a0, b0, d0 = xs[y - 1, c]
            a1, b1, d1 = xs[y, c]
            flat = (a0 + a1) + (b0 - b1)
            deep = d0 + d1
            parts.append(0.25 * (prev_z(flat + deep) + (flat - deep)))
        force[y] = tuple(parts)
    return force


def apply_rows(nodes, tangent, lower, upper, moves):
    strain = strain_rows(nodes, lower - 1, upper, moves)
    stress = {}
    for y in range(lower - 1, upper + 1):
        rows = []
        for i in range(6):
            total = tangent(y, TANGENT[i, 0]) * strain[y][0]
            for j in range(1, 6):
                total = total + tangent(y, TANGENT[i, j]) * strain[y][j]
            rows.append(total)
        stress[y] = tuple(rows)
    force = force_rows(stress, lower, upper, moves)
    return {
        y: tuple(MASS * nodes[y][c] + force[y][c] for c in range(3))
        for y in range(lower, upper + 1)
    }


def value_reader(low_ref, own_ref, high_ref):
    def read(y, c):
        if y < 0:
            return low_ref[c, y + 2]
        if y < 2:
            return own_ref[c, y]
        return high_ref[c, y - 2]

    return read


def read_rows(ref, lower, count):
    return {lower + k: tuple(ref[c, k] for c in range(3)) for k in range(count)}


def inside(rows, y, last_ref):
    keep = jnp.where(last_ref[0] == 1, 0.0, 1.0)
    rows[y] = tuple(v * keep for v in rows[y])


def write_rows(ref, rows, lower, count):
    for k in range(count):
        for c in range(3):
            ref[c, k] = rows[lower + k][c]


def row_dot(first, second):
    total = None
    for y in (0, 1):
        for c in range(3):
            term = first[y][c] * second[y][c]
            total = term if total is None else total + term
    return total


def pack_dots(ref, products):
    lane = lax.broadcasted_iota(jnp.int32, (1, DOTS), 1)
    packed = jnp.zeros((1, DOTS), F32)
    for k, product in enumerate(products):
        total = jnp.sum(jnp.sum(product, axis=0, keepdims=True), axis=1, keepdims=True)
        packed = packed + jnp.where(lane == k, total, 0.0)
    ref[...] = jnp.broadcast_to(packed[None], ref.shape)


def unpack_dots(ref, count):
    row = jnp.sum(ref[...], axis=0)
    lane = lax.broadcasted_iota(jnp.int32, (1, DOTS), 1)
    return [
        jnp.sum(jnp.where(lane == k, row, 0.0), axis=1, keepdims=True) for k in range(count)
    ]


def basis_steps(marks_ref):
    lane = lax.broadcasted_iota(jnp.int32, (1, DOTS), 1)
    mark = jnp.sum(jnp.where(lane == MARK, marks_ref[...], 0.0), axis=1, keepdims=True)
    reach = 0.5 * BASIS * mark
    return MASS + reach, reach


def chebyshev(image, now, before, center, half):
    scale = 2.0 / half
    return {
        y: tuple((image[y][c] - center * now[y][c]) * scale - before[y][c] for c in range(3))
        for y in image
    }


def first_kernel(flags_ref, marks_ref, low_ref, own_ref, high_ref, v0_ref, v1_ref):
    read = value_reader(low_ref, own_ref, high_ref)
    moves = shifts(own_ref.shape[2:])
    center, half = basis_steps(marks_ref)
    stress = {y: tuple(read(y, i) for i in range(6)) for y in range(-2, 3)}
    force = force_rows(stress, -1, 2, moves)
    v0 = {y: tuple(read(y, LOAD + c) - force[y][c] for c in range(3)) for y in range(-1, 3)}
    inside(v0, 2, flags_ref)
    image = apply_rows(v0, read, 0, 1, moves)
    scale = 1.0 / half
    v1 = {y: tuple((image[y][c] - center * v0[y][c]) * scale for c in range(3)) for y in (0, 1)}
    write_rows(v0_ref, v0, -1, 4)
    write_rows(v1_ref, v1, 0, 2)


def next_two(flags_ref, marks_ref, read, moves, before, low_ref, own_ref, high_ref):
    center, half = basis_steps(marks_ref)
    now = read_rows(low_ref, -2, 2) | read_rows(own_ref, 0, 2) | read_rows(high_ref, 2, 2)
    after = chebyshev(apply_rows(now, read, -1, 2, moves), now, before, center, half)
    inside(after, 2, flags_ref)
    last = chebyshev(apply_rows(after, read, 0, 1, moves), after, now, center, half)
    return now, after, last


def second_kernel(
    flags_ref,
    marks_ref,
    low_ref,
    own_ref,
    high_ref,
    v0_ref,
    v1_low_ref,
    v1_ref,
    v1_high_ref,
    v2_ref,
    v3_ref,
):
    read = value_reader(low_ref, own_ref, high_ref)
    moves = shifts(own_ref.shape[2:])
    _, v2, v3 = next_two(
        flags_ref,
        marks_ref,
        read,
        moves,
        read_rows(v0_ref, -1, 4),
        v1_low_ref,
        v1_ref,
        v1_high_ref,
    )
    write_rows(v2_ref, v2, -1, 4)
    write_rows(v3_ref, v3, 0, 2)


def basis_pairs():
    return [(i, j) for i in range(6) for j in range(i, 6)]


def third_kernel(
    flags_ref,
    marks_ref,
    low_ref,
    own_ref,
    high_ref,
    v0_ref,
    v1_ref,
    v2_ref,
    v3_low_ref,
    v3_ref,
    v3_high_ref,
    v4_ref,
    v5_ref,
    dots_ref,
):
    read = value_reader(low_ref, own_ref, high_ref)
    moves = shifts(own_ref.shape[2:])
    v2 = read_rows(v2_ref, -1, 4)
    v3, v4, v5 = next_two(
        flags_ref, marks_ref, read, moves, v2, v3_low_ref, v3_ref, v3_high_ref
    )
    write_rows(v4_ref, v4, 0, 2)
    write_rows(v5_ref, v5, 0, 2)
    basis = [read_rows(v0_ref, -1, 4), read_rows(v1_ref, 0, 2), v2, v3, v4, v5]
    pack_dots(dots_ref, [row_dot(basis[i], basis[j]) for i, j in basis_pairs()])


def total_of(terms):
    total = None
    for term in terms:
        total = term if total is None else total + term
    return total


def fourth_kernel(
    flags_ref,
    marks_ref,
    sums_ref,
    v0_ref,
    v1_ref,
    v2_ref,
    v3_ref,
    v4_ref,
    v5_ref,
    increment_ref,
    residual_ref,
    rows_ref,
):
    center, half = basis_steps(marks_ref)
    dots = unpack_dots(sums_ref, 21)
    gram = {}
    for k, (i, j) in enumerate(basis_pairs()):
        gram[i, j] = gram[j, i] = dots[k]

    def image_of(p):
        count = len(p)
        image = []
        for i in range(count + 1):
            terms = []
            if i < count:
                terms.append(center * p[i])
            if i > 0:
                terms.append((half if i == 1 else 0.5 * half) * p[i - 1])
            if i + 1 < count:
                terms.append(0.5 * half * p[i + 1])
            image.append(total_of(terms))
        return image

    def product(p, q):
        return total_of(
            p[i] * total_of(gram[i, j] * q[j] for j in range(len(q))) for i in range(len(p))
        )

    def combine(p, factor, q):
        longer = max(len(p), len(q))
        return [
            (p[k] + factor * q[k] if k < len(p) else factor * q[k]) if k < len(q) else p[k]
            for k in range(longer)
        ]

    solved = []
    left = [jnp.ones((1, 1), F32)]
    course = left
    norm = gram[0, 0]
    for step in range(5):
        image = image_of(course)
        alpha = norm / product(course, image)
        solved = combine(solved, alpha, course)
        left = combine(left, -alpha, image)
        if step < 4:
            fresh = product(left, left)
            course = combine(left, fresh / norm, course)
            norm = fresh
    basis = [
        read_rows(v0_ref, -1, 4),
        read_rows(v1_ref, 0, 2),
        read_rows(v2_ref, -1, 4),
        read_rows(v3_ref, 0, 2),
        read_rows(v4_ref, 0, 2),
        read_rows(v5_ref, 0, 2),
    ]
    first = flags_ref[1]
    for ref, weights in ((increment_ref, solved), (residual_ref, left)):
        for y in (0, 1):
            for c in range(3):
                rows_ref[...] = total_of(w * basis[k][y][c] for k, w in enumerate(weights))
                for x in (0, 1):
                    ref[c, x, pl.ds(y, 1), :] = rows_ref[pl.ds(first + x, 1), :]


def local_call(kernel, outs, name, *args, flags=None, scratch=()):
    specs = [pl.BlockSpec(memory_space=pltpu.VMEM)] * len(args)
    if flags is not None:
        specs = [pl.BlockSpec(memory_space=pltpu.SMEM)] + specs
        args = (flags,) + args
    return pl.pallas_call(
        kernel,
        in_specs=specs,
        out_specs=[pl.BlockSpec(memory_space=pltpu.VMEM)] * len(outs),
        out_shape=[jax.ShapeDtypeStruct(*out) if isinstance(out[0], tuple) else jax.ShapeDtypeStruct(out, F32) for out in outs],
        scratch_shapes=scratch,
        compiler_params=pltpu.CompilerParams(vmem_limit_bytes=48 * 1024 * 1024),
        name=name,
    )(*args)


def up_and_down(up, down):
    count = lax.axis_size(MICRO)
    forward = [(k, k + 1) for k in range(count - 1)]
    backward = [(k + 1, k) for k in range(count - 1)]
    return lax.ppermute(up, MICRO, forward), lax.ppermute(down, MICRO, backward)


def swapped(block):
    return lax.all_to_all(block, MICRO, split_axis=0, concat_axis=0, tiled=True)


def gather_planes(block):
    count = lax.axis_size("macro")
    pieces = [block] + [
        lax.ppermute(block, "macro", [(k, (k - shift) % count) for k in range(count)])
        for shift in range(1, count)
    ]
    planes = block.shape[2]
    twice = jnp.concatenate(pieces + pieces[:-1], axis=2)
    start = (count - lax.axis_index("macro")) % count * planes
    return lax.dynamic_slice_in_dim(twice, start, count * planes, axis=2)


def shards(
    displacement,
    load,
    routes,
    counts,
    stiffness,
    precond,
    forcing,
    coupling,
    lame_first,
    lame_shear,
):
    planes, width, depth = displacement.shape[1:]
    points = planes * width * depth
    rows_x = lax.axis_size("macro")
    owners = lax.axis_size(MICRO)
    stretch = jnp.sum(jnp.square(coupling[0, :, :3].astype(F32)))
    mark = ((lame_first[0] + 2.0 * lame_shear[0] + stretch / 6.0) / owners).reshape(1, 1)
    right = lax.ppermute(displacement, "macro", [(a + 1, a) for a in range(rows_x - 1)])
    above = lax.ppermute(displacement, MICRO, [(b + 1, b) for b in range(owners - 1)])
    corner = lax.ppermute(
        displacement,
        ("macro",) + MICRO,
        [
            ((a + 1) * owners + b + 1, a * owners + b)
            for a in range(rows_x - 1)
            for b in range(owners - 1)
        ],
    )
    send, place = local_call(
        dispatch_kernel,
        ((owners, 2, 128), ((8, points), jnp.int32)),
        "dispatch",
        mark,
        routes.reshape(1, points),
        counts.reshape(1, points),
        displacement,
        right,
        above,
        corner,
    )
    back, marks = micro_solve(
        swapped(send),
        stiffness[0],
        precond[0],
        forcing[0],
        coupling[0],
        lame_first[0],
        lame_shear[0],
    )
    (values,) = local_call(
        pick_kernel, ((FIELDS, width, planes, depth),), "pick", swapped(back), place, load
    )
    own = gather_planes(values)
    low, high = up_and_down(own, own[:, :1])
    flags = jnp.stack(
        [
            (lax.axis_index(MICRO) == owners - 1).astype(jnp.int32),
            (lax.axis_index("macro") * planes).astype(jnp.int32),
        ]
    )
    sets = (marks, low, own, high)
    whole = own.shape[2]
    two = (3, 2, whole, depth)
    four = (3, 4, whole, depth)
    v0, v1 = local_call(first_kernel, (four, two), "first_rows", *sets, flags=flags)
    v1_low, v1_high = up_and_down(v1, v1)
    v2, v3 = local_call(
        second_kernel, (four, two), "second_rows", *sets, v0, v1_low, v1, v1_high, flags=flags
    )
    v3_low, v3_high = up_and_down(v3, v3)
    v4, v5, dots = local_call(
        third_kernel,
        (two, two, (owners, 1, DOTS)),
        "third_rows",
        *sets,
        v0,
        v1,
        v2,
        v3_low,
        v3,
        v3_high,
        flags=flags,
    )
    mine = (3, planes, width, depth)
    return tuple(
        local_call(
            fourth_kernel,
            (mine, mine),
            "fourth_rows",
            marks,
            swapped(dots),
            v0,
            v1,
            v2,
            v3,
            v4,
            v5,
            flags=flags,
            scratch=[pltpu.VMEM((whole, depth), F32)],
        )
    )


def solution(mesh):
    split = Mesh(
        mesh.devices.reshape(mesh.shape["macro"], 4, 8, 2),
        ("macro", "micro_0", "micro_1", "micro_2"),
    )
    placed = (
        P(None, "macro", MICRO, None),
        P(None, "macro", MICRO, None),
        P("macro", MICRO, None, None),
        P("macro", MICRO, None),
        P(MICRO, None, None),
        P(MICRO, None, None),
        P(MICRO, None, None),
        P(MICRO, None, None),
        P(MICRO),
        P(MICRO),
    )
    return jax.shard_map(
        shards,
        mesh=split,
        in_specs=placed,
        out_specs=(P(None, "macro", MICRO, None), P(None, "macro", MICRO, None)),
        check_vma=False,
    )
```

```python
import jax
import jax.numpy as jnp
import numpy as np
from jax import lax
from jax.experimental import pallas as pl
from jax.experimental.pallas import tpu as pltpu
from jax.sharding import Mesh
from jax.sharding import PartitionSpec as P

ITMAX = 4
MICRO = ("micro_0", "micro_1", "micro_2")

BETA = 0.1
OMEGA = 0.8
MASS = 0.1
VOIGT = ((0, 5, 4), (5, 1, 3), (4, 3, 2))
PAIRS = tuple((i, j) for i in range(6) for j in range(i, 6))
TANGENT = {}
for number, (i, j) in enumerate(PAIRS):
    TANGENT[i, j] = TANGENT[j, i] = 6 + number
ROWS = 27
LOAD = 27
FIELDS = 30
DOTS = 128
BASIS = 3.5
TRUST = 2e4
MARK = 7 * 32 - 128
F32 = jnp.float32
BF16 = jnp.bfloat16


def three_parts(value):
    high = value.astype(BF16)
    rest = value - high.astype(F32)
    middle = rest.astype(BF16)
    return high, middle, (rest - middle.astype(F32)).astype(BF16)


def hot_rows(count, index):
    return lax.broadcasted_iota(jnp.int32, (count, index.shape[1]), 0) == index


def dispatch_kernel(
    first_ref, shear_ref, couple_ref, routes_ref, counts_ref, own_ref, right_ref, above_ref, corner_ref, send_ref, place_ref
):
    owners = send_ref.shape[0]
    depth = own_ref.shape[3]
    capacity = 32
    column = lax.broadcasted_iota(jnp.int32, (3, depth), 1)
    sums, diffs = {}, {}
    for x in range(3):
        for y in range(3):
            ref = ((own_ref, above_ref), (right_ref, corner_ref))[x // 2][y // 2]
            node = ref[:, x % 2, y % 2, :]
            after = jnp.where(column == depth - 1, 0.0, pltpu.roll(node, depth - 1, 1))
            sums[x, y] = node + after
            diffs[x, y] = after - node
    blocks = []
    for x in range(2):
        for y in range(2):
            s00, s01, s10, s11 = sums[x, y], sums[x, y + 1], sums[x + 1, y], sums[x + 1, y + 1]
            grad_x = 0.25 * ((s10 + s11) - (s00 + s01))
            grad_y = 0.25 * ((s01 + s11) - (s00 + s10))
            grad_z = 0.25 * (
                (diffs[x, y] + diffs[x, y + 1]) + (diffs[x + 1, y] + diffs[x + 1, y + 1])
            )
            blocks.append(
                jnp.concatenate(
                    [
                        grad_x[0:1],
                        grad_y[1:2],
                        grad_z[2:3],
                        grad_z[1:2] + grad_y[2:3],
                        grad_z[0:1] + grad_x[2:3],
                        grad_y[0:1] + grad_x[1:2],
                    ],
                    axis=0,
                )
            )
    values = jnp.concatenate(blocks, axis=1)
    owner = routes_ref[...]
    chosen = jnp.where(hot_rows(owners, owner), 1.0, 0.0)
    pieces = [chosen[:, k * depth : (k + 1) * depth] for k in range(4)]
    earlier = lax.broadcasted_iota(jnp.int32, (depth, depth), 0) < lax.broadcasted_iota(
        jnp.int32, (depth, depth), 1
    )
    within = jnp.dot(
        jnp.concatenate(pieces, axis=0).astype(BF16),
        jnp.where(earlier, 1.0, 0.0).astype(BF16),
        preferred_element_type=F32,
    )
    running = jnp.zeros((owners, 1), F32)
    ranks = []
    for k in range(4):
        seen = within[k * owners : (k + 1) * owners] + running
        ranks.append(jnp.sum(pieces[k] * seen, axis=0, keepdims=True))
        running = running + jnp.sum(pieces[k], axis=1, keepdims=True)
    rank = jnp.concatenate(ranks, axis=1).astype(jnp.int32)
    place_ref[0:1] = owner
    place_ref[1:2] = rank
    at_rank = hot_rows(capacity, rank)
    leaving = jnp.concatenate([values, counts_ref[...].astype(F32)], axis=0)
    chosen = chosen.astype(BF16)
    total = None
    for part in three_parts(leaving):
        part = part.astype(F32)
        spread = [jnp.where(at_rank, part[c : c + 1], 0.0) for c in range(7)]
        spread.append(jnp.zeros_like(spread[0]))
        term = lax.dot_general(
            chosen,
            jnp.concatenate(spread, axis=0).astype(BF16),
            (((1,), (1,)), ((), ())),
            preferred_element_type=F32,
        )
        total = term if total is None else total + term
    lane = lax.broadcasted_iota(jnp.int32, (owners, 128), 1)
    send_ref[:, 0, :] = total[:, :128]
    axial = couple_ref[...].astype(F32)[:3]
    stretch = jnp.sum(jnp.sum(axial * axial, axis=0, keepdims=True), axis=1, keepdims=True)
    mark = (first_ref[...] + 2.0 * shear_ref[...] + stretch / 6.0) / owners
    send_ref[:, 1, :] = jnp.where(lane >= MARK, mark, total[:, 128:])


def micro_kernel(
    got_ref,
    stiff_ref,
    pre_ref,
    force_ref,
    couple_ref,
    products_ref,
    cols_ref,
    out_ref,
    marks_ref,
    points_ref,
):
    tile = pl.program_id(0)
    owners = got_ref.shape[0]

    @pl.when(tile == 0)
    def _():
        points_ref[:128] = got_ref[:, 0, :].T
        second = got_ref[:, 1, :]
        points_ref[128:] = second.T
        marks_ref[...] = jnp.sum(second, axis=0, keepdims=True)

    stiff = stiff_ref[...]
    pre = pre_ref[...]
    halves = 4
    parts, loads, modes, sweeps = [], [], [], []
    for h in range(halves):
        part = jnp.concatenate(
            [points_ref[pl.ds(tile * 16 + h * 4 + k, 8, stride=32), :] for k in range(4)], axis=1
        )
        parts.append(part)
        loads.append(jnp.dot(force_ref[...], part.astype(BF16), preferred_element_type=F32))
        sweeps.append(part[6:7])
    for h in range(halves):
        modes.append(OMEGA * jnp.dot(pre, loads[h].astype(BF16), preferred_element_type=F32))
    for sweep in range(1, ITMAX):
        misfits = []
        for h in range(halves):
            misfit = (
                jnp.dot(stiff, modes[h].astype(BF16), preferred_element_type=F32)
                + BETA * jnp.tanh(modes[h])
                - loads[h]
            )
            misfits.append(misfit.astype(BF16))
        for h in range(halves):
            update = modes[h] - OMEGA * jnp.dot(pre, misfits[h], preferred_element_type=F32)
            modes[h] = jnp.where(sweeps[h] > sweep, update, modes[h])
    couple = couple_ref[...]
    products = products_ref[...]
    high = products.astype(BF16)
    low = (products - high.astype(F32)).astype(BF16)
    cols = cols_ref[...]
    for h in range(halves):
        bent = jnp.tanh(modes[h])
        slope = 1.0 - bent * bent
        slope_high = slope.astype(BF16)
        slope_low = (slope - slope_high.astype(F32)).astype(BF16)
        rows = (
            jnp.dot(couple, modes[h].astype(BF16), preferred_element_type=F32)
            + jnp.dot(high, slope_high, preferred_element_type=F32)
            + jnp.dot(low, slope_high, preferred_element_type=F32)
            + jnp.dot(high, slope_low, preferred_element_type=F32)
            + cols[:, 0:1]
        )
        part = parts[h]
        trace = part[0:1] + part[1:2] + part[2:3]
        elastic = cols[:8, 1:2] * trace + cols[:8, 2:3] * part
        rows = jnp.concatenate([rows[:8] + elastic, rows[8:]], axis=0)
        turned = []
        for k in range(2):
            pair = rows[:, k * 2 * owners : (k + 1) * 2 * owners].T
            turned += [pair[:owners], pair[owners:]]
        out_ref[:, pl.ds(tile * 4 + h, 1), :] = jnp.concatenate(turned, axis=1)[:, None, :]


def micro_solve(got, stiffness, precond, forcing, coupling, lame_first, lame_shear):
    modes = stiffness.shape[0]
    owners = got.shape[0]
    force = jnp.pad(forcing, ((0, 2), (0, 0))).T
    wide = coupling.astype(F32).T
    products = jnp.pad(jnp.stack([wide[i] * wide[j] for i, j in PAIRS]), ((6, 5), (0, 0)))
    couple = jnp.pad(coupling.T, ((0, 26), (0, 0)))
    base_first = [0.0] * 6 + [float(i < 3 and j < 3) for i, j in PAIRS] + [0.0] * 5
    base_shear = (
        [0.0] * 6
        + [2.0 * float(i == j and i < 3) + float(i == j and i >= 3) for i, j in PAIRS]
        + [0.0] * 5
    )
    on_trace = [1.0] * 3 + [0.0] * 29
    on_strain = [2.0] * 3 + [1.0] * 3 + [0.0] * 26
    firsts = np.zeros((32, 8), np.float32)
    shears = np.zeros((32, 8), np.float32)
    firsts[:, 0], firsts[:, 1] = base_first, on_trace
    shears[:, 0], shears[:, 2] = base_shear, on_strain
    cols = lame_first * firsts + lame_shear * shears
    whole = lambda *shape: pl.BlockSpec(shape, lambda step: (0,) * len(shape))
    return pl.pallas_call(
        micro_kernel,
        grid=(2,),
        in_specs=[
            whole(owners, 2, 128),
            whole(modes, modes),
            whole(modes, modes),
            whole(modes, 8),
            whole(32, modes),
            whole(32, modes),
            whole(32, 8),
        ],
        out_specs=[whole(owners, 8, 128), whole(1, 128)],
        out_shape=[
            jax.ShapeDtypeStruct((owners, 8, 128), F32),
            jax.ShapeDtypeStruct((1, 128), F32),
        ],
        scratch_shapes=[pltpu.VMEM((256, owners), F32)],
        compiler_params=pltpu.CompilerParams(vmem_limit_bytes=48 * 1024 * 1024),
        name="micro_solve",
    )(got, stiffness, precond, force, couple, products, cols)


def pick_kernel(back_ref, place_ref, load_ref, out_ref):
    owners = back_ref.shape[0]
    depth = out_ref.shape[3]
    owner = place_ref[0:1]
    rank = place_ref[1:2]
    chosen = jnp.where(hot_rows(owners, owner), 1.0, 0.0).astype(BF16)
    chosen = jnp.concatenate([chosen] * 3, axis=0)
    total = jnp.zeros((32, owner.shape[1]), F32)
    for s in range(8):
        turned = back_ref[:, s, :].T
        split = jnp.concatenate(three_parts(turned), axis=1)
        candidates = jnp.dot(split, chosen, preferred_element_type=F32)
        for k in range(4):
            total = total + jnp.where(
                rank == s * 4 + k, candidates[k * 32 : (k + 1) * 32], 0.0
            )
    for x in range(2):
        for y in range(2):
            at = (x * 2 + y) * depth
            out_ref[:ROWS, y, x, :] = total[:ROWS, at : at + depth]
            out_ref[ROWS:, y, x, :] = load_ref[:, x, y, :]


def shifts(shape):
    plane = lax.broadcasted_iota(jnp.int32, shape, 0)
    column = lax.broadcasted_iota(jnp.int32, shape, 1)
    planes, columns = shape

    def next_x(v):
        return jnp.where(plane == planes - 1, 0.0, pltpu.roll(v, planes - 1, 0))

    def prev_x(v):
        return jnp.where(plane == 0, 0.0, pltpu.roll(v, 1, 0))

    def next_z(v):
        return jnp.where(column == columns - 1, 0.0, pltpu.roll(v, columns - 1, 1))

    def prev_z(v):
        return jnp.where(column == 0, 0.0, pltpu.roll(v, 1, 1))

    return next_x, prev_x, next_z, prev_z


def strain_rows(nodes, lower, upper, moves):
    next_x, _, next_z, _ = moves
    sums, diffs = {}, {}
    for y in range(lower, upper + 2):
        for c in range(3):
            v = nodes[y][c]
            w = next_z(v)
            sums[y, c] = v + w
            diffs[y, c] = w - v
    strain = {}
    for y in range(lower, upper + 1):
        grad = []
        for c in range(3):
            both = sums[y, c] + sums[y + 1, c]
            rise = sums[y + 1, c] - sums[y, c]
            turn = diffs[y, c] + diffs[y + 1, c]
            grad.append(
                (
                    0.25 * (next_x(both) - both),
                    0.25 * (next_x(rise) + rise),
                    0.25 * (next_x(turn) + turn),
                )
            )
        strain[y] = (
            grad[0][0],
            grad[1][1],
            grad[2][2],
            grad[1][2] + grad[2][1],
            grad[0][2] + grad[2][0],
            grad[0][1] + grad[1][0],
        )
    return strain


def force_rows(stress, lower, upper, moves):
    _, prev_x, _, prev_z = moves
    xs = {}
    for y in range(lower - 1, upper + 1):
        for c in range(3):
            a, b, d = (stress[y][VOIGT[c][k]] for k in range(3))
            xs[y, c] = (prev_x(a) - a, prev_x(b) + b, prev_x(d) + d)
    force = {}
    for y in range(lower, upper + 1):
        parts = []
        for c in range(3):
            a0, b0, d0 = xs[y - 1, c]
            a1, b1, d1 = xs[y, c]
            flat = (a0 + a1) + (b0 - b1)
            deep = d0 + d1
            parts.append(0.25 * (prev_z(flat + deep) + (flat - deep)))
        force[y] = tuple(parts)
    return force


def apply_rows(nodes, tangent, lower, upper, moves):
    strain = strain_rows(nodes, lower - 1, upper, moves)
    stress = {}
    for y in range(lower - 1, upper + 1):
        rows = []
        for i in range(6):
            total = tangent(y, TANGENT[i, 0]) * strain[y][0]
            for j in range(1, 6):
                total = total + tangent(y, TANGENT[i, j]) * strain[y][j]
            rows.append(total)
        stress[y] = tuple(rows)
    force = force_rows(stress, lower, upper, moves)
    return {
        y: tuple(MASS * nodes[y][c] + force[y][c] for c in range(3))
        for y in range(lower, upper + 1)
    }


def value_reader(low_ref, own_ref, high_ref):
    def read(y, c):
        if y < 0:
            return low_ref[c, y + 2]
        if y < 2:
            return own_ref[c, y]
        return high_ref[c, y - 2]

    return read


def read_rows(ref, lower, count):
    return {lower + k: tuple(ref[c, k] for c in range(3)) for k in range(count)}


def inside(rows, y, last_ref):
    keep = jnp.where(last_ref[0] == 1, 0.0, 1.0)
    rows[y] = tuple(v * keep for v in rows[y])


def write_rows(ref, rows, lower, count):
    for k in range(count):
        for c in range(3):
            ref[c, k] = rows[lower + k][c]


def row_dot(first, second):
    total = None
    for y in (0, 1):
        for c in range(3):
            term = first[y][c] * second[y][c]
            total = term if total is None else total + term
    return total


def pack_dots(ref, products):
    lane = lax.broadcasted_iota(jnp.int32, (1, DOTS), 1)
    packed = jnp.zeros((1, DOTS), F32)
    for k, product in enumerate(products):
        total = jnp.sum(jnp.sum(product, axis=0, keepdims=True), axis=1, keepdims=True)
        packed = packed + jnp.where(lane == k, total, 0.0)
    ref[...] = jnp.broadcast_to(packed[None], ref.shape)


def unpack_dots(ref, count):
    row = jnp.sum(ref[...].reshape(-1, DOTS), axis=0, keepdims=True)
    lane = lax.broadcasted_iota(jnp.int32, (1, DOTS), 1)
    return [
        jnp.sum(jnp.where(lane == k, row, 0.0), axis=1, keepdims=True) for k in range(count)
    ]


def basis_steps(marks_ref):
    lane = lax.broadcasted_iota(jnp.int32, (1, DOTS), 1)
    mark = jnp.sum(jnp.where(lane == MARK, marks_ref[...], 0.0), axis=1, keepdims=True)
    reach = 0.5 * BASIS * mark
    return MASS + reach, reach


def chebyshev(image, now, before, center, half):
    scale = 2.0 / half
    return {
        y: tuple((image[y][c] - center * now[y][c]) * scale - before[y][c] for c in range(3))
        for y in image
    }


def first_kernel(flags_ref, marks_ref, low_ref, own_ref, high_ref, v0_ref, v1_ref):
    read = value_reader(low_ref, own_ref, high_ref)
    moves = shifts(own_ref.shape[2:])
    center, half = basis_steps(marks_ref)
    stress = {y: tuple(read(y, i) for i in range(6)) for y in range(-2, 3)}
    force = force_rows(stress, -1, 2, moves)
    v0 = {y: tuple(read(y, LOAD + c) - force[y][c] for c in range(3)) for y in range(-1, 3)}
    inside(v0, 2, flags_ref)
    image = apply_rows(v0, read, 0, 1, moves)
    scale = 1.0 / half
    v1 = {y: tuple((image[y][c] - center * v0[y][c]) * scale for c in range(3)) for y in (0, 1)}
    write_rows(v0_ref, v0, -1, 4)
    write_rows(v1_ref, v1, 0, 2)


def next_two(flags_ref, marks_ref, read, moves, before, low_ref, own_ref, high_ref):
    center, half = basis_steps(marks_ref)
    now = read_rows(low_ref, -2, 2) | read_rows(own_ref, 0, 2) | read_rows(high_ref, 2, 2)
    after = chebyshev(apply_rows(now, read, -1, 2, moves), now, before, center, half)
    inside(after, 2, flags_ref)
    last = chebyshev(apply_rows(after, read, 0, 1, moves), after, now, center, half)
    return now, after, last


def second_kernel(
    flags_ref,
    marks_ref,
    low_ref,
    own_ref,
    high_ref,
    v0_ref,
    v1_low_ref,
    v1_ref,
    v1_high_ref,
    v2_ref,
    v3_ref,
):
    read = value_reader(low_ref, own_ref, high_ref)
    moves = shifts(own_ref.shape[2:])
    _, v2, v3 = next_two(
        flags_ref,
        marks_ref,
        read,
        moves,
        read_rows(v0_ref, -1, 4),
        v1_low_ref,
        v1_ref,
        v1_high_ref,
    )
    write_rows(v2_ref, v2, -1, 4)
    write_rows(v3_ref, v3, 0, 2)


def basis_pairs():
    return [(i, j) for i in range(6) for j in range(i, 6)]


def third_kernel(
    flags_ref,
    marks_ref,
    low_ref,
    own_ref,
    high_ref,
    v0_ref,
    v1_ref,
    v2_ref,
    v3_low_ref,
    v3_ref,
    v3_high_ref,
    v4_ref,
    v5_ref,
    dots_ref,
):
    read = value_reader(low_ref, own_ref, high_ref)
    moves = shifts(own_ref.shape[2:])
    v2 = read_rows(v2_ref, -1, 4)
    v3, v4, v5 = next_two(
        flags_ref, marks_ref, read, moves, v2, v3_low_ref, v3_ref, v3_high_ref
    )
    write_rows(v4_ref, v4, 0, 2)
    write_rows(v5_ref, v5, 0, 2)
    basis = [read_rows(v0_ref, -1, 4), read_rows(v1_ref, 0, 2), v2, v3, v4, v5]
    pack_dots(dots_ref, [row_dot(basis[i], basis[j]) for i, j in basis_pairs()])


def total_of(terms):
    total = None
    for term in terms:
        total = term if total is None else total + term
    return total


def place_planes(increment_ref, residual_ref, solved, left, basis, rows_ref, first):
    for ref, weights in ((increment_ref, solved), (residual_ref, left)):
        for y in (0, 1):
            for c in range(3):
                rows_ref[...] = total_of(w * basis[k][y][c] for k, w in enumerate(weights))
                for x in (0, 1):
                    ref[c, x, pl.ds(y, 1), :] = rows_ref[pl.ds(first + x, 1), :]


def fourth_kernel(
    flags_ref,
    marks_ref,
    sums_ref,
    v0_ref,
    v1_ref,
    v2_ref,
    v3_ref,
    v4_ref,
    v5_ref,
    increment_ref,
    residual_ref,
    trust_ref,
    rows_ref,
):
    center, half = basis_steps(marks_ref)
    dots = unpack_dots(sums_ref, 21)
    gram = {}
    for k, (i, j) in enumerate(basis_pairs()):
        gram[i, j] = gram[j, i] = dots[k]

    def image_of(p):
        count = len(p)
        image = []
        for i in range(count + 1):
            terms = []
            if i < count:
                terms.append(center * p[i])
            if i > 0:
                terms.append((half if i == 1 else 0.5 * half) * p[i - 1])
            if i + 1 < count:
                terms.append(0.5 * half * p[i + 1])
            image.append(total_of(terms))
        return image

    def product(p, q):
        return total_of(
            p[i] * total_of(gram[i, j] * q[j] for j in range(len(q))) for i in range(len(p))
        )

    def size(p, q):
        return total_of(
            jnp.abs(p[i]) * total_of(jnp.abs(gram[i, j]) * jnp.abs(q[j]) for j in range(len(q)))
            for i in range(len(p))
        )

    def combine(p, factor, q):
        longer = max(len(p), len(q))
        return [
            (p[k] + factor * q[k] if k < len(p) else factor * q[k]) if k < len(q) else p[k]
            for k in range(longer)
        ]

    solved = []
    left = [jnp.ones((1, 1), F32)]
    course = left
    norm = gram[0, 0]
    for step in range(5):
        image = image_of(course)
        bend = product(course, image)
        if step == 4:
            spread = size(course, image) / bend
            trusted = jnp.where((spread > 0.0) & (spread < TRUST) & trusted, 1, 0)
        alpha = norm / bend
        solved = combine(solved, alpha, course)
        left = combine(left, -alpha, image)
        if step < 4:
            fresh = product(left, left)
            if step == 3:
                spread = size(left, left) / fresh
                trusted = (spread > 0.0) & (spread < TRUST)
            course = combine(left, fresh / norm, course)
            norm = fresh
    basis = [
        read_rows(v0_ref, -1, 4),
        read_rows(v1_ref, 0, 2),
        read_rows(v2_ref, -1, 4),
        read_rows(v3_ref, 0, 2),
        read_rows(v4_ref, 0, 2),
        read_rows(v5_ref, 0, 2),
    ]
    trust_ref[...] = trusted
    place_planes(increment_ref, residual_ref, solved, left, basis, rows_ref, flags_ref[1])


def careful_first(low_ref, own_ref, high_ref, v0_ref, v1_ref):
    read = value_reader(low_ref, own_ref, high_ref)
    moves = shifts(own_ref.shape[2:])
    write_rows(v1_ref, apply_rows(read_rows(v0_ref, -1, 4), read, 0, 1, moves), 0, 2)


def careful_second(
    last_ref, low_ref, own_ref, high_ref, v0_ref, v1_low_ref, v1_ref, v1_high_ref, v2_ref, dots_ref
):
    read = value_reader(low_ref, own_ref, high_ref)
    moves = shifts(own_ref.shape[2:])
    v1 = read_rows(v1_low_ref, -2, 2) | read_rows(v1_ref, 0, 2) | read_rows(v1_high_ref, 2, 2)
    v2 = apply_rows(v1, read, -1, 2, moves)
    inside(v2, 2, last_ref)
    v0 = read_rows(v0_ref, -1, 4)
    write_rows(v2_ref, v2, -1, 4)
    pack_dots(
        dots_ref,
        [
            row_dot(a, b)
            for a, b in ((v0, v0), (v0, v1), (v0, v2), (v1, v1), (v1, v2))
        ],
    )


def careful_third(
    low_ref,
    own_ref,
    high_ref,
    v0_ref,
    v1_low_ref,
    v1_ref,
    v1_high_ref,
    v2_ref,
    sums_ref,
    r1_ref,
    r2_ref,
    w3_ref,
    coef_ref,
):
    read = value_reader(low_ref, own_ref, high_ref)
    moves = shifts(own_ref.shape[2:])
    m00, m01, m02, m11, m12 = unpack_dots(sums_ref, 5)
    a0 = m00 / m01
    n1 = m00 - 2.0 * a0 * m01 + a0 * a0 * m11
    b0 = n1 / m00
    e = 1.0 + b0
    a1 = n1 / (e * e * m01 - e * a0 * (m02 + m11) + a0 * a0 * m12)
    center = 0.5 * (1.0 / a0 + 1.0 / a1 + b0 / a0)
    v0 = read_rows(v0_ref, -1, 4)
    v1 = read_rows(v1_low_ref, -2, 2) | read_rows(v1_ref, 0, 2) | read_rows(v1_high_ref, 2, 2)
    v2 = read_rows(v2_ref, -1, 4)
    along, twice = a0 + a1 * e, a1 * a0
    r2 = {
        y: tuple(v0[y][c] - along * v1[y][c] + twice * v2[y][c] for c in range(3))
        for y in range(-1, 3)
    }
    image = apply_rows(r2, read, 0, 1, moves)
    scale = 1.0 / center
    w3 = {y: tuple(image[y][c] * scale - r2[y][c] for c in range(3)) for y in (0, 1)}
    r1 = {y: tuple(v0[y][c] - a0 * v1[y][c] for c in range(3)) for y in (0, 1)}
    write_rows(r1_ref, r1, 0, 2)
    write_rows(r2_ref, r2, 0, 2)
    write_rows(w3_ref, w3, 0, 2)
    lane = lax.broadcasted_iota(jnp.int32, (1, DOTS), 1)
    packed = jnp.zeros((1, DOTS), F32)
    for k, value in enumerate((a0, b0, a1, n1, center)):
        packed = packed + jnp.where(lane == k, value, 0.0)
    coef_ref[...] = packed


def careful_fourth(
    last_ref,
    low_ref,
    own_ref,
    high_ref,
    coef_ref,
    v0_ref,
    r1_ref,
    r2_ref,
    w3_low_ref,
    w3_ref,
    w3_high_ref,
    w4_ref,
    w5_ref,
    dots_ref,
):
    read = value_reader(low_ref, own_ref, high_ref)
    moves = shifts(own_ref.shape[2:])
    scale = 1.0 / unpack_dots(coef_ref, 5)[4]
    w3 = read_rows(w3_low_ref, -2, 2) | read_rows(w3_ref, 0, 2) | read_rows(w3_high_ref, 2, 2)
    image = apply_rows(w3, read, -1, 2, moves)
    w4 = {y: tuple(image[y][c] * scale - w3[y][c] for c in range(3)) for y in range(-1, 3)}
    inside(w4, 2, last_ref)
    image = apply_rows(w4, read, 0, 1, moves)
    w5 = {y: tuple(image[y][c] * scale - w4[y][c] for c in range(3)) for y in (0, 1)}
    write_rows(w4_ref, w4, 0, 2)
    write_rows(w5_ref, w5, 0, 2)
    v0 = read_rows(v0_ref, -1, 4)
    basis = [v0, read_rows(r1_ref, 0, 2), read_rows(r2_ref, 0, 2), w3, w4, w5]
    pack_dots(dots_ref, [row_dot(basis[i], basis[j]) for i, j in basis_pairs()])


def careful_fifth(
    flags_ref,
    coef_ref,
    sums_ref,
    v0_ref,
    r1_ref,
    r2_ref,
    w3_ref,
    w4_ref,
    w5_ref,
    increment_ref,
    residual_ref,
    rows_ref,
):
    a0, b0, a1, n1, center = unpack_dots(coef_ref, 5)
    dots = unpack_dots(sums_ref, 21)
    gram = {}
    for k, (i, j) in enumerate(basis_pairs()):
        gram[i, j] = gram[j, i] = dots[k]
    zero = jnp.zeros((1, 1), F32)
    one = jnp.ones((1, 1), F32)
    i0, i1 = 1.0 / a0, 1.0 / a1

    def image_of(p):
        return [
            i0 * p[0] - b0 * i0 * p[1],
            (i1 + b0 * i0) * p[1] - i0 * p[0],
            center * p[2] - i1 * p[1],
            center * (p[2] + p[3]),
            center * (p[3] + p[4]),
            center * p[4],
        ]

    def product(p, q):
        return total_of(
            p[i] * total_of(gram[i, j] * q[j] for j in range(6)) for i in range(6)
        )

    solved = [a0 + a1 * b0, a1, zero, zero, zero, zero]
    left = [zero, zero, one, zero, zero, zero]
    norm = gram[2, 2]
    ratio = norm / n1
    course = [ratio * b0, ratio, one, zero, zero, zero]
    for step in range(3):
        image = image_of(course)
        alpha = norm / product(course, image)
        solved = [s + alpha * p for s, p in zip(solved, course)]
        left = [r - alpha * q for r, q in zip(left, image)]
        if step < 2:
            fresh = product(left, left)
            ratio = fresh / norm
            course = [r + ratio * p for r, p in zip(left, course)]
            norm = fresh
    v0 = read_rows(v0_ref, -1, 4)
    basis = [v0] + [read_rows(ref, 0, 2) for ref in (r1_ref, r2_ref, w3_ref, w4_ref, w5_ref)]
    place_planes(increment_ref, residual_ref, solved, left, basis, rows_ref, flags_ref[1])


def local_call(kernel, outs, name, *args, flags=None, scratch=()):
    typed = [out if isinstance(out[0], tuple) else (out, F32) for out in outs]
    specs = [pl.BlockSpec(memory_space=pltpu.VMEM)] * len(args)
    if flags is not None:
        specs = [pl.BlockSpec(memory_space=pltpu.SMEM)] + specs
        args = (flags,) + args
    return pl.pallas_call(
        kernel,
        in_specs=specs,
        out_specs=[pl.BlockSpec(memory_space=pltpu.VMEM)] * len(outs),
        out_shape=[jax.ShapeDtypeStruct(*out) for out in typed],
        scratch_shapes=scratch,
        compiler_params=pltpu.CompilerParams(vmem_limit_bytes=48 * 1024 * 1024),
        name=name,
    )(*args)


def up_and_down(up, down):
    count = lax.axis_size(MICRO)
    forward = [(k, k + 1) for k in range(count - 1)]
    backward = [(k + 1, k) for k in range(count - 1)]
    return lax.ppermute(up, MICRO, forward), lax.ppermute(down, MICRO, backward)


def swapped(block):
    return lax.all_to_all(block, MICRO, split_axis=0, concat_axis=0, tiled=True)


def gather_planes(block):
    count = lax.axis_size("macro")
    pieces = [block] + [
        lax.ppermute(block, "macro", [(k, (k - shift) % count) for k in range(count)])
        for shift in range(1, count)
    ]
    planes = block.shape[2]
    twice = jnp.concatenate(pieces + pieces[:-1], axis=2)
    start = (count - lax.axis_index("macro")) % count * planes
    return lax.dynamic_slice_in_dim(twice, start, count * planes, axis=2)


def shards(
    displacement,
    load,
    routes,
    counts,
    stiffness,
    precond,
    forcing,
    coupling,
    lame_first,
    lame_shear,
):
    planes, width, depth = displacement.shape[1:]
    points = planes * width * depth
    rows_x = lax.axis_size("macro")
    owners = lax.axis_size(MICRO)
    right = lax.ppermute(displacement, "macro", [(a + 1, a) for a in range(rows_x - 1)])
    above = lax.ppermute(displacement, MICRO, [(b + 1, b) for b in range(owners - 1)])
    corner = lax.ppermute(
        displacement,
        ("macro",) + MICRO,
        [
            ((a + 1) * owners + b + 1, a * owners + b)
            for a in range(rows_x - 1)
            for b in range(owners - 1)
        ],
    )
    send, place = local_call(
        dispatch_kernel,
        ((owners, 2, 128), ((8, points), jnp.int32)),
        "dispatch",
        lame_first.reshape(1, 1),
        lame_shear.reshape(1, 1),
        coupling[0].T,
        routes.reshape(1, points),
        counts.reshape(1, points),
        displacement,
        right,
        above,
        corner,
    )
    back, marks = micro_solve(
        swapped(send),
        stiffness[0],
        precond[0],
        forcing[0],
        coupling[0],
        lame_first[0],
        lame_shear[0],
    )
    (values,) = local_call(
        pick_kernel, ((FIELDS, width, planes, depth),), "pick", swapped(back), place, load
    )
    own = gather_planes(values)
    low, high = up_and_down(own, own[:, :1])
    flags = jnp.stack(
        [
            (lax.axis_index(MICRO) == owners - 1).astype(jnp.int32),
            (lax.axis_index("macro") * planes).astype(jnp.int32),
        ]
    )
    sets = (marks, low, own, high)
    whole = own.shape[2]
    two = (3, 2, whole, depth)
    four = (3, 4, whole, depth)
    v0, v1 = local_call(first_kernel, (four, two), "first_rows", *sets, flags=flags)
    v1_low, v1_high = up_and_down(v1, v1)
    v2, v3 = local_call(
        second_kernel, (four, two), "second_rows", *sets, v0, v1_low, v1, v1_high, flags=flags
    )
    v3_low, v3_high = up_and_down(v3, v3)
    v4, v5, dots = local_call(
        third_kernel,
        (two, two, (owners, 1, DOTS)),
        "third_rows",
        *sets,
        v0,
        v1,
        v2,
        v3_low,
        v3,
        v3_high,
        flags=flags,
    )
    mine = (3, planes, width, depth)
    scratch = [pltpu.VMEM((whole, depth), F32)]
    increment, residual, trust = local_call(
        fourth_kernel,
        (mine, mine, ((1, 1), jnp.int32)),
        "fourth_rows",
        marks,
        swapped(dots),
        v0,
        v1,
        v2,
        v3,
        v4,
        v5,
        flags=flags,
        scratch=scratch,
    )

    def careful():
        sets = (low, own, high)
        line = (1, DOTS)
        (u1,) = local_call(careful_first, (two,), "careful_first", *sets, v0)
        u1_low, u1_high = up_and_down(u1, u1)
        u2, dots = local_call(
            careful_second,
            (four, (owners, 1, DOTS)),
            "careful_second",
            *sets,
            v0,
            u1_low,
            u1,
            u1_high,
            flags=flags,
        )
        r1, r2, w3, coef = local_call(
            careful_third,
            (two, two, two, line),
            "careful_third",
            *sets,
            v0,
            u1_low,
            u1,
            u1_high,
            u2,
            swapped(dots),
        )
        w3_low, w3_high = up_and_down(w3, w3)
        w4, w5, dots = local_call(
            careful_fourth,
            (two, two, (owners, 1, DOTS)),
            "careful_fourth",
            *sets,
            coef,
            v0,
            r1,
            r2,
            w3_low,
            w3,
            w3_high,
            flags=flags,
        )
        return tuple(
            local_call(
                careful_fifth,
                (mine, mine),
                "careful_fifth",
                coef,
                swapped(dots),
                v0,
                r1,
                r2,
                w3,
                w4,
                w5,
                flags=flags,
                scratch=scratch,
            )
        )

    return lax.cond(trust[0, 0] == 1, lambda: (increment, residual), careful)


def solution(mesh):
    split = Mesh(
        mesh.devices.reshape(mesh.shape["macro"], 4, 8, 2),
        ("macro", "micro_0", "micro_1", "micro_2"),
    )
    placed = (
        P(None, "macro", MICRO, None),
        P(None, "macro", MICRO, None),
        P("macro", MICRO, None, None),
        P("macro", MICRO, None),
        P(MICRO, None, None),
        P(MICRO, None, None),
        P(MICRO, None, None),
        P(MICRO, None, None),
        P(MICRO),
        P(MICRO),
    )
    return jax.shard_map(
        shards,
        mesh=split,
        in_specs=placed,
        out_specs=(P(None, "macro", MICRO, None), P(None, "macro", MICRO, None)),
        check_vma=False,
    )
```

```python
import functools

import jax
import jax.numpy as jnp
import numpy as np
from jax import lax
from jax.experimental import pallas as pl
from jax.experimental.pallas import tpu as pltpu
from jax.sharding import Mesh
from jax.sharding import PartitionSpec as P

ITMAX = 4
MICRO = ("micro_0", "micro_1", "micro_2")

BETA = 0.1
OMEGA = 0.8
MASS = 0.1
VOIGT = ((0, 5, 4), (5, 1, 3), (4, 3, 2))
PAIRS = tuple((i, j) for i in range(6) for j in range(i, 6))
TANGENT = {}
for number, (i, j) in enumerate(PAIRS):
    TANGENT[i, j] = TANGENT[j, i] = 6 + number
ROWS = 27
LOAD = 27
FIELDS = 30
DOTS = 128
BASIS = 3.5
TRUST = 2e4
MARK = 7 * 32 - 128
F32 = jnp.float32
BF16 = jnp.bfloat16


def three_parts(value):
    high = value.astype(BF16)
    rest = value - high.astype(F32)
    middle = rest.astype(BF16)
    return high, middle, (rest - middle.astype(F32)).astype(BF16)


def hot_rows(count, index):
    return lax.broadcasted_iota(jnp.int32, (count, index.shape[1]), 0) == index


def rank_kernel(
    owners, first_ref, shear_ref, couple_ref, routes_ref, counts_ref, here_ref, place_ref, mark_ref, own_ref
):
    depth = here_ref.shape[3]
    own_ref[...] = here_ref[...]
    owner = routes_ref[...]
    chosen = jnp.where(hot_rows(owners, owner), 1.0, 0.0)
    pieces = [chosen[:, k * depth : (k + 1) * depth] for k in range(4)]
    earlier = lax.broadcasted_iota(jnp.int32, (depth, depth), 0) < lax.broadcasted_iota(
        jnp.int32, (depth, depth), 1
    )
    within = jnp.dot(
        jnp.concatenate(pieces, axis=0).astype(BF16),
        jnp.where(earlier, 1.0, 0.0).astype(BF16),
        preferred_element_type=F32,
    )
    running = jnp.zeros((owners, 1), F32)
    ranks = []
    for k in range(4):
        seen = within[k * owners : (k + 1) * owners] + running
        ranks.append(jnp.sum(pieces[k] * seen, axis=0, keepdims=True))
        running = running + jnp.sum(pieces[k], axis=1, keepdims=True)
    rank = jnp.concatenate(ranks, axis=1).astype(jnp.int32)
    place_ref[0:1] = owner
    place_ref[1:2] = rank
    place_ref[2:3] = counts_ref[...]
    axial = couple_ref[...].astype(F32)[:3]
    stretch = jnp.sum(jnp.sum(axial * axial, axis=0, keepdims=True), axis=1, keepdims=True)
    mark = (first_ref[...] + 2.0 * shear_ref[...] + stretch / 6.0) / owners
    mark_ref[...] = mark


def dispatch_kernel(
    place_ref, mark_ref, own_ref, right_ref, above_ref, corner_ref, send_ref
):
    owners = send_ref.shape[0]
    depth = own_ref.shape[3]
    capacity = 32
    column = lax.broadcasted_iota(jnp.int32, (3, depth), 1)
    sums, diffs = {}, {}
    for x in range(3):
        for y in range(3):
            ref = ((own_ref, above_ref), (right_ref, corner_ref))[x // 2][y // 2]
            node = ref[:, x % 2, y % 2, :]
            after = jnp.where(column == depth - 1, 0.0, pltpu.roll(node, depth - 1, 1))
            sums[x, y] = node + after
            diffs[x, y] = after - node
    blocks = []
    for x in range(2):
        for y in range(2):
            s00, s01, s10, s11 = sums[x, y], sums[x, y + 1], sums[x + 1, y], sums[x + 1, y + 1]
            grad_x = 0.25 * ((s10 + s11) - (s00 + s01))
            grad_y = 0.25 * ((s01 + s11) - (s00 + s10))
            grad_z = 0.25 * (
                (diffs[x, y] + diffs[x, y + 1]) + (diffs[x + 1, y] + diffs[x + 1, y + 1])
            )
            blocks.append(
                jnp.concatenate(
                    [
                        grad_x[0:1],
                        grad_y[1:2],
                        grad_z[2:3],
                        grad_z[1:2] + grad_y[2:3],
                        grad_z[0:1] + grad_x[2:3],
                        grad_y[0:1] + grad_x[1:2],
                    ],
                    axis=0,
                )
            )
    values = jnp.concatenate(blocks, axis=1)
    chosen = jnp.where(hot_rows(owners, place_ref[0:1]), 1.0, 0.0)
    rank = place_ref[1:2]
    at_rank = hot_rows(capacity, rank)
    leaving = jnp.concatenate([values, place_ref[2:3].astype(F32)], axis=0)
    chosen = chosen.astype(BF16)
    total = None
    for part in three_parts(leaving):
        part = part.astype(F32)
        spread = [jnp.where(at_rank, part[c : c + 1], 0.0) for c in range(7)]
        spread.append(jnp.zeros_like(spread[0]))
        term = lax.dot_general(
            chosen,
            jnp.concatenate(spread, axis=0).astype(BF16),
            (((1,), (1,)), ((), ())),
            preferred_element_type=F32,
        )
        total = term if total is None else total + term
    lane = lax.broadcasted_iota(jnp.int32, (owners, 128), 1)
    send_ref[:, 0, :] = total[:, :128]
    send_ref[:, 1, :] = jnp.where(lane >= MARK, mark_ref[...], total[:, 128:])


def micro_kernel(
    got_ref,
    stiff_ref,
    pre_ref,
    force_ref,
    couple_ref,
    products_ref,
    cols_ref,
    out_ref,
    marks_ref,
    points_ref,
):
    tile = pl.program_id(0)
    owners = got_ref.shape[0]

    @pl.when(tile == 0)
    def _():
        points_ref[:128] = got_ref[:, 0, :].T
        second = got_ref[:, 1, :]
        points_ref[128:] = second.T
        marks_ref[...] = jnp.sum(second, axis=0, keepdims=True)

    stiff = stiff_ref[...]
    pre = pre_ref[...]
    halves = 4
    parts, loads, modes, sweeps = [], [], [], []
    for h in range(halves):
        part = jnp.concatenate(
            [points_ref[pl.ds(tile * 16 + h * 4 + k, 8, stride=32), :] for k in range(4)], axis=1
        )
        parts.append(part)
        loads.append(jnp.dot(force_ref[...], part.astype(BF16), preferred_element_type=F32))
        sweeps.append(part[6:7])
    for h in range(halves):
        modes.append(OMEGA * jnp.dot(pre, loads[h].astype(BF16), preferred_element_type=F32))
    for sweep in range(1, ITMAX):
        misfits = []
        for h in range(halves):
            misfit = (
                jnp.dot(stiff, modes[h].astype(BF16), preferred_element_type=F32)
                + BETA * jnp.tanh(modes[h])
                - loads[h]
            )
            misfits.append(misfit.astype(BF16))
        for h in range(halves):
            update = modes[h] - OMEGA * jnp.dot(pre, misfits[h], preferred_element_type=F32)
            modes[h] = jnp.where(sweeps[h] > sweep, update, modes[h])
    couple = couple_ref[...]
    products = products_ref[...]
    high = products.astype(BF16)
    low = (products - high.astype(F32)).astype(BF16)
    cols = cols_ref[...]
    for h in range(halves):
        bent = jnp.tanh(modes[h])
        slope = 1.0 - bent * bent
        slope_high = slope.astype(BF16)
        slope_low = (slope - slope_high.astype(F32)).astype(BF16)
        rows = (
            jnp.dot(couple, modes[h].astype(BF16), preferred_element_type=F32)
            + jnp.dot(high, slope_high, preferred_element_type=F32)
            + jnp.dot(low, slope_high, preferred_element_type=F32)
            + jnp.dot(high, slope_low, preferred_element_type=F32)
            + cols[:, 0:1]
        )
        part = parts[h]
        trace = part[0:1] + part[1:2] + part[2:3]
        elastic = cols[:8, 1:2] * trace + cols[:8, 2:3] * part
        rows = jnp.concatenate([rows[:8] + elastic, rows[8:]], axis=0)
        turned = []
        for k in range(2):
            pair = rows[:, k * 2 * owners : (k + 1) * 2 * owners].T
            turned += [pair[:owners], pair[owners:]]
        out_ref[:, pl.ds(tile * 4 + h, 1), :] = jnp.concatenate(turned, axis=1)[:, None, :]


def micro_solve(got, stiffness, precond, forcing, coupling, lame_first, lame_shear):
    modes = stiffness.shape[0]
    owners = got.shape[0]
    force = jnp.pad(forcing, ((0, 2), (0, 0))).T
    wide = coupling.astype(F32).T
    products = jnp.pad(jnp.stack([wide[i] * wide[j] for i, j in PAIRS]), ((6, 5), (0, 0)))
    couple = jnp.pad(coupling.T, ((0, 26), (0, 0)))
    base_first = [0.0] * 6 + [float(i < 3 and j < 3) for i, j in PAIRS] + [0.0] * 5
    base_shear = (
        [0.0] * 6
        + [2.0 * float(i == j and i < 3) + float(i == j and i >= 3) for i, j in PAIRS]
        + [0.0] * 5
    )
    on_trace = [1.0] * 3 + [0.0] * 29
    on_strain = [2.0] * 3 + [1.0] * 3 + [0.0] * 26
    firsts = np.zeros((32, 8), np.float32)
    shears = np.zeros((32, 8), np.float32)
    firsts[:, 0], firsts[:, 1] = base_first, on_trace
    shears[:, 0], shears[:, 2] = base_shear, on_strain
    cols = lame_first * firsts + lame_shear * shears
    whole = lambda *shape: pl.BlockSpec(shape, lambda step: (0,) * len(shape))
    return pl.pallas_call(
        micro_kernel,
        grid=(2,),
        in_specs=[
            whole(owners, 2, 128),
            whole(modes, modes),
            whole(modes, modes),
            whole(modes, 8),
            whole(32, modes),
            whole(32, modes),
            whole(32, 8),
        ],
        out_specs=[whole(owners, 8, 128), whole(1, 128)],
        out_shape=[
            jax.ShapeDtypeStruct((owners, 8, 128), F32),
            jax.ShapeDtypeStruct((1, 128), F32),
        ],
        scratch_shapes=[pltpu.VMEM((256, owners), F32)],
        compiler_params=pltpu.CompilerParams(vmem_limit_bytes=48 * 1024 * 1024),
        name="micro_solve",
    )(got, stiffness, precond, force, couple, products, cols)


def pick_kernel(back_ref, place_ref, load_ref, out_ref):
    owners = back_ref.shape[0]
    depth = out_ref.shape[3]
    owner = place_ref[0:1]
    rank = place_ref[1:2]
    chosen = jnp.where(hot_rows(owners, owner), 1.0, 0.0).astype(BF16)
    chosen = jnp.concatenate([chosen] * 3, axis=0)
    total = jnp.zeros((32, owner.shape[1]), F32)
    for s in range(8):
        turned = back_ref[:, s, :].T
        split = jnp.concatenate(three_parts(turned), axis=1)
        candidates = jnp.dot(split, chosen, preferred_element_type=F32)
        for k in range(4):
            total = total + jnp.where(
                rank == s * 4 + k, candidates[k * 32 : (k + 1) * 32], 0.0
            )
    for x in range(2):
        for y in range(2):
            at = (x * 2 + y) * depth
            out_ref[:ROWS, y, x, :] = total[:ROWS, at : at + depth]
            out_ref[ROWS:, y, x, :] = load_ref[:, x, y, :]


def shifts(shape):
    plane = lax.broadcasted_iota(jnp.int32, shape, 0)
    column = lax.broadcasted_iota(jnp.int32, shape, 1)
    planes, columns = shape

    def next_x(v):
        return jnp.where(plane == planes - 1, 0.0, pltpu.roll(v, planes - 1, 0))

    def prev_x(v):
        return jnp.where(plane == 0, 0.0, pltpu.roll(v, 1, 0))

    def next_z(v):
        return jnp.where(column == columns - 1, 0.0, pltpu.roll(v, columns - 1, 1))

    def prev_z(v):
        return jnp.where(column == 0, 0.0, pltpu.roll(v, 1, 1))

    return next_x, prev_x, next_z, prev_z


def strain_rows(nodes, lower, upper, moves):
    next_x, _, next_z, _ = moves
    sums, diffs = {}, {}
    for y in range(lower, upper + 2):
        for c in range(3):
            v = nodes[y][c]
            w = next_z(v)
            sums[y, c] = v + w
            diffs[y, c] = w - v
    strain = {}
    for y in range(lower, upper + 1):
        grad = []
        for c in range(3):
            both = sums[y, c] + sums[y + 1, c]
            rise = sums[y + 1, c] - sums[y, c]
            turn = diffs[y, c] + diffs[y + 1, c]
            grad.append(
                (
                    0.25 * (next_x(both) - both),
                    0.25 * (next_x(rise) + rise),
                    0.25 * (next_x(turn) + turn),
                )
            )
        strain[y] = (
            grad[0][0],
            grad[1][1],
            grad[2][2],
            grad[1][2] + grad[2][1],
            grad[0][2] + grad[2][0],
            grad[0][1] + grad[1][0],
        )
    return strain


def force_rows(stress, lower, upper, moves):
    _, prev_x, _, prev_z = moves
    xs = {}
    for y in range(lower - 1, upper + 1):
        for c in range(3):
            a, b, d = (stress[y][VOIGT[c][k]] for k in range(3))
            xs[y, c] = (prev_x(a) - a, prev_x(b) + b, prev_x(d) + d)
    force = {}
    for y in range(lower, upper + 1):
        parts = []
        for c in range(3):
            a0, b0, d0 = xs[y - 1, c]
            a1, b1, d1 = xs[y, c]
            flat = (a0 + a1) + (b0 - b1)
            deep = d0 + d1
            parts.append(0.25 * (prev_z(flat + deep) + (flat - deep)))
        force[y] = tuple(parts)
    return force


def apply_rows(nodes, tangent, lower, upper, moves):
    strain = strain_rows(nodes, lower - 1, upper, moves)
    stress = {}
    for y in range(lower - 1, upper + 1):
        rows = []
        for i in range(6):
            total = tangent(y, TANGENT[i, 0]) * strain[y][0]
            for j in range(1, 6):
                total = total + tangent(y, TANGENT[i, j]) * strain[y][j]
            rows.append(total)
        stress[y] = tuple(rows)
    force = force_rows(stress, lower, upper, moves)
    return {
        y: tuple(MASS * nodes[y][c] + force[y][c] for c in range(3))
        for y in range(lower, upper + 1)
    }


def value_reader(low_ref, own_ref, high_ref):
    def read(y, c):
        if y < 0:
            return low_ref[c, y + 2]
        if y < 2:
            return own_ref[c, y]
        return high_ref[c, y - 2]

    return read


def read_rows(ref, lower, count):
    return {lower + k: tuple(ref[c, k] for c in range(3)) for k in range(count)}


def inside(rows, y, last_ref):
    keep = jnp.where(last_ref[0] == 1, 0.0, 1.0)
    rows[y] = tuple(v * keep for v in rows[y])


def write_rows(ref, rows, lower, count):
    for k in range(count):
        for c in range(3):
            ref[c, k] = rows[lower + k][c]


def row_dot(first, second):
    total = None
    for y in (0, 1):
        for c in range(3):
            term = first[y][c] * second[y][c]
            total = term if total is None else total + term
    return total


def pack_dots(ref, products):
    lane = lax.broadcasted_iota(jnp.int32, (1, DOTS), 1)
    packed = jnp.zeros((1, DOTS), F32)
    for k, product in enumerate(products):
        total = jnp.sum(jnp.sum(product, axis=0, keepdims=True), axis=1, keepdims=True)
        packed = packed + jnp.where(lane == k, total, 0.0)
    ref[...] = jnp.broadcast_to(packed[None], ref.shape)


def unpack_dots(ref, count):
    row = jnp.sum(ref[...].reshape(-1, DOTS), axis=0, keepdims=True)
    lane = lax.broadcasted_iota(jnp.int32, (1, DOTS), 1)
    return [
        jnp.sum(jnp.where(lane == k, row, 0.0), axis=1, keepdims=True) for k in range(count)
    ]


def basis_steps(marks_ref):
    lane = lax.broadcasted_iota(jnp.int32, (1, DOTS), 1)
    mark = jnp.sum(jnp.where(lane == MARK, marks_ref[...], 0.0), axis=1, keepdims=True)
    reach = 0.5 * BASIS * mark
    return MASS + reach, reach


def chebyshev(image, now, before, center, half):
    scale = 2.0 / half
    return {
        y: tuple((image[y][c] - center * now[y][c]) * scale - before[y][c] for c in range(3))
        for y in image
    }


def first_kernel(flags_ref, marks_ref, low_ref, own_ref, high_ref, v0_ref, v1_ref):
    read = value_reader(low_ref, own_ref, high_ref)
    moves = shifts(own_ref.shape[2:])
    center, half = basis_steps(marks_ref)
    stress = {y: tuple(read(y, i) for i in range(6)) for y in range(-2, 3)}
    force = force_rows(stress, -1, 2, moves)
    v0 = {y: tuple(read(y, LOAD + c) - force[y][c] for c in range(3)) for y in range(-1, 3)}
    inside(v0, 2, flags_ref)
    image = apply_rows(v0, read, 0, 1, moves)
    scale = 1.0 / half
    v1 = {y: tuple((image[y][c] - center * v0[y][c]) * scale for c in range(3)) for y in (0, 1)}
    write_rows(v0_ref, v0, -1, 4)
    write_rows(v1_ref, v1, 0, 2)


def next_two(flags_ref, marks_ref, read, moves, before, low_ref, own_ref, high_ref):
    center, half = basis_steps(marks_ref)
    now = read_rows(low_ref, -2, 2) | read_rows(own_ref, 0, 2) | read_rows(high_ref, 2, 2)
    after = chebyshev(apply_rows(now, read, -1, 2, moves), now, before, center, half)
    inside(after, 2, flags_ref)
    last = chebyshev(apply_rows(after, read, 0, 1, moves), after, now, center, half)
    return now, after, last


def second_kernel(
    flags_ref,
    marks_ref,
    low_ref,
    own_ref,
    high_ref,
    v0_ref,
    v1_low_ref,
    v1_ref,
    v1_high_ref,
    v2_ref,
    v3_ref,
):
    read = value_reader(low_ref, own_ref, high_ref)
    moves = shifts(own_ref.shape[2:])
    _, v2, v3 = next_two(
        flags_ref,
        marks_ref,
        read,
        moves,
        read_rows(v0_ref, -1, 4),
        v1_low_ref,
        v1_ref,
        v1_high_ref,
    )
    write_rows(v2_ref, v2, -1, 4)
    write_rows(v3_ref, v3, 0, 2)


def basis_pairs():
    return [(i, j) for i in range(6) for j in range(i, 6)]


def third_kernel(
    flags_ref,
    marks_ref,
    low_ref,
    own_ref,
    high_ref,
    v0_ref,
    v1_ref,
    v2_ref,
    v3_low_ref,
    v3_ref,
    v3_high_ref,
    v4_ref,
    v5_ref,
    dots_ref,
):
    read = value_reader(low_ref, own_ref, high_ref)
    moves = shifts(own_ref.shape[2:])
    v2 = read_rows(v2_ref, -1, 4)
    v3, v4, v5 = next_two(
        flags_ref, marks_ref, read, moves, v2, v3_low_ref, v3_ref, v3_high_ref
    )
    write_rows(v4_ref, v4, 0, 2)
    write_rows(v5_ref, v5, 0, 2)
    basis = [read_rows(v0_ref, -1, 4), read_rows(v1_ref, 0, 2), v2, v3, v4, v5]
    pack_dots(dots_ref, [row_dot(basis[i], basis[j]) for i, j in basis_pairs()])


def total_of(terms):
    total = None
    for term in terms:
        total = term if total is None else total + term
    return total


def place_planes(increment_ref, residual_ref, solved, left, basis, rows_ref, first):
    for ref, weights in ((increment_ref, solved), (residual_ref, left)):
        for y in (0, 1):
            for c in range(3):
                rows_ref[...] = total_of(w * basis[k][y][c] for k, w in enumerate(weights))
                for x in (0, 1):
                    ref[c, x, pl.ds(y, 1), :] = rows_ref[pl.ds(first + x, 1), :]


def fourth_kernel(
    flags_ref,
    marks_ref,
    sums_ref,
    v0_ref,
    v1_ref,
    v2_ref,
    v3_ref,
    v4_ref,
    v5_ref,
    increment_ref,
    residual_ref,
    trust_ref,
    rows_ref,
):
    center, half = basis_steps(marks_ref)
    dots = unpack_dots(sums_ref, 21)
    gram = {}
    for k, (i, j) in enumerate(basis_pairs()):
        gram[i, j] = gram[j, i] = dots[k]

    def image_of(p):
        count = len(p)
        image = []
        for i in range(count + 1):
            terms = []
            if i < count:
                terms.append(center * p[i])
            if i > 0:
                terms.append((half if i == 1 else 0.5 * half) * p[i - 1])
            if i + 1 < count:
                terms.append(0.5 * half * p[i + 1])
            image.append(total_of(terms))
        return image

    def product(p, q):
        return total_of(
            p[i] * total_of(gram[i, j] * q[j] for j in range(len(q))) for i in range(len(p))
        )

    def size(p, q):
        return total_of(
            jnp.abs(p[i]) * total_of(jnp.abs(gram[i, j]) * jnp.abs(q[j]) for j in range(len(q)))
            for i in range(len(p))
        )

    def combine(p, factor, q):
        longer = max(len(p), len(q))
        return [
            (p[k] + factor * q[k] if k < len(p) else factor * q[k]) if k < len(q) else p[k]
            for k in range(longer)
        ]

    solved = []
    left = [jnp.ones((1, 1), F32)]
    course = left
    norm = gram[0, 0]
    for step in range(5):
        image = image_of(course)
        bend = product(course, image)
        if step == 4:
            spread = size(course, image) / bend
            trusted = jnp.where((spread > 0.0) & (spread < TRUST) & trusted, 1, 0)
        alpha = norm / bend
        solved = combine(solved, alpha, course)
        left = combine(left, -alpha, image)
        if step < 4:
            fresh = product(left, left)
            if step == 3:
                spread = size(left, left) / fresh
                trusted = (spread > 0.0) & (spread < TRUST)
            course = combine(left, fresh / norm, course)
            norm = fresh
    basis = [
        read_rows(v0_ref, -1, 4),
        read_rows(v1_ref, 0, 2),
        read_rows(v2_ref, -1, 4),
        read_rows(v3_ref, 0, 2),
        read_rows(v4_ref, 0, 2),
        read_rows(v5_ref, 0, 2),
    ]
    trust_ref[...] = trusted
    place_planes(increment_ref, residual_ref, solved, left, basis, rows_ref, flags_ref[1])


def careful_first(low_ref, own_ref, high_ref, v0_ref, v1_ref):
    read = value_reader(low_ref, own_ref, high_ref)
    moves = shifts(own_ref.shape[2:])
    write_rows(v1_ref, apply_rows(read_rows(v0_ref, -1, 4), read, 0, 1, moves), 0, 2)


def careful_second(
    last_ref, low_ref, own_ref, high_ref, v0_ref, v1_low_ref, v1_ref, v1_high_ref, v2_ref, dots_ref
):
    read = value_reader(low_ref, own_ref, high_ref)
    moves = shifts(own_ref.shape[2:])
    v1 = read_rows(v1_low_ref, -2, 2) | read_rows(v1_ref, 0, 2) | read_rows(v1_high_ref, 2, 2)
    v2 = apply_rows(v1, read, -1, 2, moves)
    inside(v2, 2, last_ref)
    v0 = read_rows(v0_ref, -1, 4)
    write_rows(v2_ref, v2, -1, 4)
    pack_dots(
        dots_ref,
        [
            row_dot(a, b)
            for a, b in ((v0, v0), (v0, v1), (v0, v2), (v1, v1), (v1, v2))
        ],
    )


def careful_third(
    low_ref,
    own_ref,
    high_ref,
    v0_ref,
    v1_low_ref,
    v1_ref,
    v1_high_ref,
    v2_ref,
    sums_ref,
    r1_ref,
    r2_ref,
    w3_ref,
    coef_ref,
):
    read = value_reader(low_ref, own_ref, high_ref)
    moves = shifts(own_ref.shape[2:])
    m00, m01, m02, m11, m12 = unpack_dots(sums_ref, 5)
    a0 = m00 / m01
    n1 = m00 - 2.0 * a0 * m01 + a0 * a0 * m11
    b0 = n1 / m00
    e = 1.0 + b0
    a1 = n1 / (e * e * m01 - e * a0 * (m02 + m11) + a0 * a0 * m12)
    center = 0.5 * (1.0 / a0 + 1.0 / a1 + b0 / a0)
    v0 = read_rows(v0_ref, -1, 4)
    v1 = read_rows(v1_low_ref, -2, 2) | read_rows(v1_ref, 0, 2) | read_rows(v1_high_ref, 2, 2)
    v2 = read_rows(v2_ref, -1, 4)
    along, twice = a0 + a1 * e, a1 * a0
    r2 = {
        y: tuple(v0[y][c] - along * v1[y][c] + twice * v2[y][c] for c in range(3))
        for y in range(-1, 3)
    }
    image = apply_rows(r2, read, 0, 1, moves)
    scale = 1.0 / center
    w3 = {y: tuple(image[y][c] * scale - r2[y][c] for c in range(3)) for y in (0, 1)}
    r1 = {y: tuple(v0[y][c] - a0 * v1[y][c] for c in range(3)) for y in (0, 1)}
    write_rows(r1_ref, r1, 0, 2)
    write_rows(r2_ref, r2, 0, 2)
    write_rows(w3_ref, w3, 0, 2)
    lane = lax.broadcasted_iota(jnp.int32, (1, DOTS), 1)
    packed = jnp.zeros((1, DOTS), F32)
    for k, value in enumerate((a0, b0, a1, n1, center)):
        packed = packed + jnp.where(lane == k, value, 0.0)
    coef_ref[...] = packed


def careful_fourth(
    last_ref,
    low_ref,
    own_ref,
    high_ref,
    coef_ref,
    v0_ref,
    r1_ref,
    r2_ref,
    w3_low_ref,
    w3_ref,
    w3_high_ref,
    w4_ref,
    w5_ref,
    dots_ref,
):
    read = value_reader(low_ref, own_ref, high_ref)
    moves = shifts(own_ref.shape[2:])
    scale = 1.0 / unpack_dots(coef_ref, 5)[4]
    w3 = read_rows(w3_low_ref, -2, 2) | read_rows(w3_ref, 0, 2) | read_rows(w3_high_ref, 2, 2)
    image = apply_rows(w3, read, -1, 2, moves)
    w4 = {y: tuple(image[y][c] * scale - w3[y][c] for c in range(3)) for y in range(-1, 3)}
    inside(w4, 2, last_ref)
    image = apply_rows(w4, read, 0, 1, moves)
    w5 = {y: tuple(image[y][c] * scale - w4[y][c] for c in range(3)) for y in (0, 1)}
    write_rows(w4_ref, w4, 0, 2)
    write_rows(w5_ref, w5, 0, 2)
    v0 = read_rows(v0_ref, -1, 4)
    basis = [v0, read_rows(r1_ref, 0, 2), read_rows(r2_ref, 0, 2), w3, w4, w5]
    pack_dots(dots_ref, [row_dot(basis[i], basis[j]) for i, j in basis_pairs()])


def careful_fifth(
    flags_ref,
    coef_ref,
    sums_ref,
    v0_ref,
    r1_ref,
    r2_ref,
    w3_ref,
    w4_ref,
    w5_ref,
    increment_ref,
    residual_ref,
    rows_ref,
):
    a0, b0, a1, n1, center = unpack_dots(coef_ref, 5)
    dots = unpack_dots(sums_ref, 21)
    gram = {}
    for k, (i, j) in enumerate(basis_pairs()):
        gram[i, j] = gram[j, i] = dots[k]
    zero = jnp.zeros((1, 1), F32)
    one = jnp.ones((1, 1), F32)
    i0, i1 = 1.0 / a0, 1.0 / a1

    def image_of(p):
        return [
            i0 * p[0] - b0 * i0 * p[1],
            (i1 + b0 * i0) * p[1] - i0 * p[0],
            center * p[2] - i1 * p[1],
            center * (p[2] + p[3]),
            center * (p[3] + p[4]),
            center * p[4],
        ]

    def product(p, q):
        return total_of(
            p[i] * total_of(gram[i, j] * q[j] for j in range(6)) for i in range(6)
        )

    solved = [a0 + a1 * b0, a1, zero, zero, zero, zero]
    left = [zero, zero, one, zero, zero, zero]
    norm = gram[2, 2]
    ratio = norm / n1
    course = [ratio * b0, ratio, one, zero, zero, zero]
    for step in range(3):
        image = image_of(course)
        alpha = norm / product(course, image)
        solved = [s + alpha * p for s, p in zip(solved, course)]
        left = [r - alpha * q for r, q in zip(left, image)]
        if step < 2:
            fresh = product(left, left)
            ratio = fresh / norm
            course = [r + ratio * p for r, p in zip(left, course)]
            norm = fresh
    v0 = read_rows(v0_ref, -1, 4)
    basis = [v0] + [read_rows(ref, 0, 2) for ref in (r1_ref, r2_ref, w3_ref, w4_ref, w5_ref)]
    place_planes(increment_ref, residual_ref, solved, left, basis, rows_ref, flags_ref[1])


def local_call(kernel, outs, name, *args, flags=None, scratch=()):
    typed = [out if isinstance(out[0], tuple) else (out, F32) for out in outs]
    specs = [pl.BlockSpec(memory_space=pltpu.VMEM)] * len(args)
    if flags is not None:
        specs = [pl.BlockSpec(memory_space=pltpu.SMEM)] + specs
        args = (flags,) + args
    return pl.pallas_call(
        kernel,
        in_specs=specs,
        out_specs=[pl.BlockSpec(memory_space=pltpu.VMEM)] * len(outs),
        out_shape=[jax.ShapeDtypeStruct(*out) for out in typed],
        scratch_shapes=scratch,
        compiler_params=pltpu.CompilerParams(vmem_limit_bytes=48 * 1024 * 1024),
        name=name,
    )(*args)


def up_and_down(up, down):
    count = lax.axis_size(MICRO)
    forward = [(k, k + 1) for k in range(count - 1)]
    backward = [(k + 1, k) for k in range(count - 1)]
    return lax.ppermute(up, MICRO, forward), lax.ppermute(down, MICRO, backward)


def swapped(block):
    return lax.all_to_all(block, MICRO, split_axis=0, concat_axis=0, tiled=True)


def gather_planes(block):
    count = lax.axis_size("macro")
    pieces = [block] + [
        lax.ppermute(block, "macro", [(k, (k - shift) % count) for k in range(count)])
        for shift in range(1, count)
    ]
    planes = block.shape[2]
    twice = jnp.concatenate(pieces + pieces[:-1], axis=2)
    start = (count - lax.axis_index("macro")) % count * planes
    return lax.dynamic_slice_in_dim(twice, start, count * planes, axis=2)


def shards(
    displacement,
    load,
    routes,
    counts,
    stiffness,
    precond,
    forcing,
    coupling,
    lame_first,
    lame_shear,
):
    planes, width, depth = displacement.shape[1:]
    points = planes * width * depth
    rows_x = lax.axis_size("macro")
    owners = lax.axis_size(MICRO)
    right = lax.ppermute(displacement, "macro", [(a + 1, a) for a in range(rows_x - 1)])
    above = lax.ppermute(displacement, MICRO, [(b + 1, b) for b in range(owners - 1)])
    corner = lax.ppermute(
        displacement,
        ("macro",) + MICRO,
        [
            ((a + 1) * owners + b + 1, a * owners + b)
            for a in range(rows_x - 1)
            for b in range(owners - 1)
        ],
    )
    place, mark, kept = local_call(
        functools.partial(rank_kernel, owners),
        (((8, points), jnp.int32), (1, 1), displacement.shape),
        "rank",
        lame_first.reshape(1, 1),
        lame_shear.reshape(1, 1),
        coupling[0].T,
        routes.reshape(1, points),
        counts.reshape(1, points),
        displacement,
    )
    (send,) = local_call(
        dispatch_kernel,
        ((owners, 2, 128),),
        "dispatch",
        place,
        mark,
        kept,
        right,
        above,
        corner,
    )
    back, marks = micro_solve(
        swapped(send),
        stiffness[0],
        precond[0],
        forcing[0],
        coupling[0],
        lame_first[0],
        lame_shear[0],
    )
    (values,) = local_call(
        pick_kernel, ((FIELDS, width, planes, depth),), "pick", swapped(back), place, load
    )
    own = gather_planes(values)
    low, high = up_and_down(own, own[:, :1])
    flags = jnp.stack(
        [
            (lax.axis_index(MICRO) == owners - 1).astype(jnp.int32),
            (lax.axis_index("macro") * planes).astype(jnp.int32),
        ]
    )
    sets = (marks, low, own, high)
    whole = own.shape[2]
    two = (3, 2, whole, depth)
    four = (3, 4, whole, depth)
    v0, v1 = local_call(first_kernel, (four, two), "first_rows", *sets, flags=flags)
    v1_low, v1_high = up_and_down(v1, v1)
    v2, v3 = local_call(
        second_kernel, (four, two), "second_rows", *sets, v0, v1_low, v1, v1_high, flags=flags
    )
    v3_low, v3_high = up_and_down(v3, v3)
    v4, v5, dots = local_call(
        third_kernel,
        (two, two, (owners, 1, DOTS)),
        "third_rows",
        *sets,
        v0,
        v1,
        v2,
        v3_low,
        v3,
        v3_high,
        flags=flags,
    )
    mine = (3, planes, width, depth)
    scratch = [pltpu.VMEM((whole, depth), F32)]
    increment, residual, trust = local_call(
        fourth_kernel,
        (mine, mine, ((1, 1), jnp.int32)),
        "fourth_rows",
        marks,
        swapped(dots),
        v0,
        v1,
        v2,
        v3,
        v4,
        v5,
        flags=flags,
        scratch=scratch,
    )

    def careful():
        sets = (low, own, high)
        line = (1, DOTS)
        (u1,) = local_call(careful_first, (two,), "careful_first", *sets, v0)
        u1_low, u1_high = up_and_down(u1, u1)
        u2, dots = local_call(
            careful_second,
            (four, (owners, 1, DOTS)),
            "careful_second",
            *sets,
            v0,
            u1_low,
            u1,
            u1_high,
            flags=flags,
        )
        r1, r2, w3, coef = local_call(
            careful_third,
            (two, two, two, line),
            "careful_third",
            *sets,
            v0,
            u1_low,
            u1,
            u1_high,
            u2,
            swapped(dots),
        )
        w3_low, w3_high = up_and_down(w3, w3)
        w4, w5, dots = local_call(
            careful_fourth,
            (two, two, (owners, 1, DOTS)),
            "careful_fourth",
            *sets,
            coef,
            v0,
            r1,
            r2,
            w3_low,
            w3,
            w3_high,
            flags=flags,
        )
        return tuple(
            local_call(
                careful_fifth,
                (mine, mine),
                "careful_fifth",
                coef,
                swapped(dots),
                v0,
                r1,
                r2,
                w3,
                w4,
                w5,
                flags=flags,
                scratch=scratch,
            )
        )

    return lax.cond(trust[0, 0] == 1, lambda: (increment, residual), careful)


def solution(mesh):
    split = Mesh(
        mesh.devices.reshape(mesh.shape["macro"], 4, 8, 2),
        ("macro", "micro_0", "micro_1", "micro_2"),
    )
    placed = (
        P(None, "macro", MICRO, None),
        P(None, "macro", MICRO, None),
        P("macro", MICRO, None, None),
        P("macro", MICRO, None),
        P(MICRO, None, None),
        P(MICRO, None, None),
        P(MICRO, None, None),
        P(MICRO, None, None),
        P(MICRO),
        P(MICRO),
    )
    return jax.shard_map(
        shards,
        mesh=split,
        in_specs=placed,
        out_specs=(P(None, "macro", MICRO, None), P(None, "macro", MICRO, None)),
        check_vma=False,
    )
```

```python
import functools

import jax
import jax.numpy as jnp
import numpy as np
from jax import lax
from jax.experimental import pallas as pl
from jax.experimental.pallas import tpu as pltpu
from jax.sharding import Mesh
from jax.sharding import PartitionSpec as P

ITMAX = 4
MICRO = ("micro_0", "micro_1", "micro_2")

BETA = 0.1
OMEGA = 0.8
MASS = 0.1
VOIGT = ((0, 5, 4), (5, 1, 3), (4, 3, 2))
PAIRS = tuple((i, j) for i in range(6) for j in range(i, 6))
TANGENT = {}
for number, (i, j) in enumerate(PAIRS):
    TANGENT[i, j] = TANGENT[j, i] = 6 + number
ROWS = 27
LOAD = 27
FIELDS = 30
DOTS = 128
BASIS = 3.5
TRUST = 2e4
MARK = 7 * 32 - 128
F32 = jnp.float32
BF16 = jnp.bfloat16


def three_parts(value):
    high = value.astype(BF16)
    rest = value - high.astype(F32)
    middle = rest.astype(BF16)
    return high, middle, (rest - middle.astype(F32)).astype(BF16)


def hot_rows(count, index):
    return lax.broadcasted_iota(jnp.int32, (count, index.shape[1]), 0) == index


def rank_kernel(
    owners, first_ref, shear_ref, couple_ref, routes_ref, counts_ref, here_ref, place_ref, mark_ref, own_ref
):
    depth = here_ref.shape[3]
    own_ref[...] = here_ref[...]
    owner = routes_ref[...]
    chosen = jnp.where(hot_rows(owners, owner), 1.0, 0.0)
    pieces = [chosen[:, k * depth : (k + 1) * depth] for k in range(4)]
    earlier = lax.broadcasted_iota(jnp.int32, (depth, depth), 0) < lax.broadcasted_iota(
        jnp.int32, (depth, depth), 1
    )
    within = jnp.dot(
        jnp.concatenate(pieces, axis=0).astype(BF16),
        jnp.where(earlier, 1.0, 0.0).astype(BF16),
        preferred_element_type=F32,
    )
    running = jnp.zeros((owners, 1), F32)
    ranks = []
    for k in range(4):
        seen = within[k * owners : (k + 1) * owners] + running
        ranks.append(jnp.sum(pieces[k] * seen, axis=0, keepdims=True))
        running = running + jnp.sum(pieces[k], axis=1, keepdims=True)
    rank = jnp.concatenate(ranks, axis=1).astype(jnp.int32)
    place_ref[0:1] = owner
    place_ref[1:2] = rank
    place_ref[2:3] = counts_ref[...]
    axial = couple_ref[...].astype(F32)[:3]
    stretch = jnp.sum(jnp.sum(axial * axial, axis=0, keepdims=True), axis=1, keepdims=True)
    mark = (first_ref[...] + 2.0 * shear_ref[...] + stretch / 6.0) / owners
    mark_ref[...] = mark


def dispatch_kernel(
    place_ref, mark_ref, own_ref, right_ref, above_ref, corner_ref, send_ref
):
    owners = send_ref.shape[0]
    depth = own_ref.shape[3]
    capacity = 32
    column = lax.broadcasted_iota(jnp.int32, (3, depth), 1)
    sums, diffs = {}, {}
    for x in range(3):
        for y in range(3):
            ref = ((own_ref, above_ref), (right_ref, corner_ref))[x // 2][y // 2]
            node = ref[:, x % 2, y % 2, :]
            after = jnp.where(column == depth - 1, 0.0, pltpu.roll(node, depth - 1, 1))
            sums[x, y] = node + after
            diffs[x, y] = after - node
    blocks = []
    for x in range(2):
        for y in range(2):
            s00, s01, s10, s11 = sums[x, y], sums[x, y + 1], sums[x + 1, y], sums[x + 1, y + 1]
            grad_x = 0.25 * ((s10 + s11) - (s00 + s01))
            grad_y = 0.25 * ((s01 + s11) - (s00 + s10))
            grad_z = 0.25 * (
                (diffs[x, y] + diffs[x, y + 1]) + (diffs[x + 1, y] + diffs[x + 1, y + 1])
            )
            blocks.append(
                jnp.concatenate(
                    [
                        grad_x[0:1],
                        grad_y[1:2],
                        grad_z[2:3],
                        grad_z[1:2] + grad_y[2:3],
                        grad_z[0:1] + grad_x[2:3],
                        grad_y[0:1] + grad_x[1:2],
                    ],
                    axis=0,
                )
            )
    values = jnp.concatenate(blocks, axis=1)
    chosen = jnp.where(hot_rows(owners, place_ref[0:1]), 1.0, 0.0)
    rank = place_ref[1:2]
    at_rank = hot_rows(capacity, rank)
    leaving = jnp.concatenate([values, place_ref[2:3].astype(F32)], axis=0)
    chosen = chosen.astype(BF16)
    total = None
    for part in three_parts(leaving):
        part = part.astype(F32)
        spread = [jnp.where(at_rank, part[c : c + 1], 0.0) for c in range(7)]
        spread.append(jnp.zeros_like(spread[0]))
        term = lax.dot_general(
            chosen,
            jnp.concatenate(spread, axis=0).astype(BF16),
            (((1,), (1,)), ((), ())),
            preferred_element_type=F32,
        )
        total = term if total is None else total + term
    lane = lax.broadcasted_iota(jnp.int32, (owners, 128), 1)
    send_ref[:, 0, :] = total[:, :128]
    send_ref[:, 1, :] = jnp.where(lane >= MARK, mark_ref[...], total[:, 128:])


def micro_kernel(
    got_ref,
    stiff_ref,
    pre_ref,
    force_ref,
    couple_ref,
    products_ref,
    cols_ref,
    out_ref,
    marks_ref,
    points_ref,
):
    tile = pl.program_id(0)
    owners = got_ref.shape[0]

    @pl.when(tile == 0)
    def _():
        points_ref[:128] = got_ref[:, 0, :].T
        second = got_ref[:, 1, :]
        points_ref[128:] = second.T
        marks_ref[...] = jnp.sum(second, axis=0, keepdims=True)

    stiff = stiff_ref[...]
    pre = pre_ref[...]
    halves = 4
    parts, loads, modes, sweeps = [], [], [], []
    for h in range(halves):
        part = jnp.concatenate(
            [points_ref[pl.ds(tile * 16 + h * 4 + k, 8, stride=32), :] for k in range(4)], axis=1
        )
        parts.append(part)
        loads.append(jnp.dot(force_ref[...], part.astype(BF16), preferred_element_type=F32))
        sweeps.append(part[6:7])
    for h in range(halves):
        modes.append(OMEGA * jnp.dot(pre, loads[h].astype(BF16), preferred_element_type=F32))
    for sweep in range(1, ITMAX):
        misfits = []
        for h in range(halves):
            misfit = (
                jnp.dot(stiff, modes[h].astype(BF16), preferred_element_type=F32)
                + BETA * jnp.tanh(modes[h])
                - loads[h]
            )
            misfits.append(misfit.astype(BF16))
        for h in range(halves):
            update = modes[h] - OMEGA * jnp.dot(pre, misfits[h], preferred_element_type=F32)
            modes[h] = jnp.where(sweeps[h] > sweep, update, modes[h])
    couple = couple_ref[...]
    products = products_ref[...]
    high = products.astype(BF16)
    low = (products - high.astype(F32)).astype(BF16)
    both = jnp.concatenate([high, low], axis=0)
    cols = cols_ref[...]
    for h in range(halves):
        bent = jnp.tanh(modes[h])
        slope = 1.0 - bent * bent
        slope_high = slope.astype(BF16)
        slope_low = (slope - slope_high.astype(F32)).astype(BF16)
        curved = jnp.dot(both, slope_high, preferred_element_type=F32)
        rows = (
            jnp.dot(couple, modes[h].astype(BF16), preferred_element_type=F32)
            + curved[:32]
            + curved[32:]
            + jnp.dot(high, slope_low, preferred_element_type=F32)
            + cols[:, 0:1]
        )
        part = parts[h]
        trace = part[0:1] + part[1:2] + part[2:3]
        elastic = cols[:8, 1:2] * trace + cols[:8, 2:3] * part
        rows = jnp.concatenate([rows[:8] + elastic, rows[8:]], axis=0)
        turned = []
        for k in range(2):
            pair = rows[:, k * 2 * owners : (k + 1) * 2 * owners].T
            turned += [pair[:owners], pair[owners:]]
        out_ref[:, pl.ds(tile * 4 + h, 1), :] = jnp.concatenate(turned, axis=1)[:, None, :]


def micro_solve(got, stiffness, precond, forcing, coupling, lame_first, lame_shear):
    modes = stiffness.shape[0]
    owners = got.shape[0]
    force = jnp.pad(forcing, ((0, 2), (0, 0))).T
    wide = coupling.astype(F32).T
    products = jnp.pad(jnp.stack([wide[i] * wide[j] for i, j in PAIRS]), ((6, 5), (0, 0)))
    couple = jnp.pad(coupling.T, ((0, 26), (0, 0)))
    base_first = [0.0] * 6 + [float(i < 3 and j < 3) for i, j in PAIRS] + [0.0] * 5
    base_shear = (
        [0.0] * 6
        + [2.0 * float(i == j and i < 3) + float(i == j and i >= 3) for i, j in PAIRS]
        + [0.0] * 5
    )
    on_trace = [1.0] * 3 + [0.0] * 29
    on_strain = [2.0] * 3 + [1.0] * 3 + [0.0] * 26
    firsts = np.zeros((32, 8), np.float32)
    shears = np.zeros((32, 8), np.float32)
    firsts[:, 0], firsts[:, 1] = base_first, on_trace
    shears[:, 0], shears[:, 2] = base_shear, on_strain
    cols = lame_first * firsts + lame_shear * shears
    whole = lambda *shape: pl.BlockSpec(shape, lambda step: (0,) * len(shape))
    return pl.pallas_call(
        micro_kernel,
        grid=(2,),
        in_specs=[
            whole(owners, 2, 128),
            whole(modes, modes),
            whole(modes, modes),
            whole(modes, 8),
            whole(32, modes),
            whole(32, modes),
            whole(32, 8),
        ],
        out_specs=[whole(owners, 8, 128), whole(1, 128)],
        out_shape=[
            jax.ShapeDtypeStruct((owners, 8, 128), F32),
            jax.ShapeDtypeStruct((1, 128), F32),
        ],
        scratch_shapes=[pltpu.VMEM((256, owners), F32)],
        compiler_params=pltpu.CompilerParams(vmem_limit_bytes=48 * 1024 * 1024),
        name="micro_solve",
    )(got, stiffness, precond, force, couple, products, cols)


def pick_kernel(back_ref, place_ref, load_ref, out_ref):
    owners = back_ref.shape[0]
    depth = out_ref.shape[3]
    owner = place_ref[0:1]
    rank = place_ref[1:2]
    chosen = jnp.where(hot_rows(owners, owner), 1.0, 0.0).astype(BF16)
    chosen = jnp.concatenate([chosen] * 3, axis=0)
    total = jnp.zeros((32, owner.shape[1]), F32)
    for s in range(8):
        turned = back_ref[:, s, :].T
        split = jnp.concatenate(three_parts(turned), axis=1)
        candidates = jnp.dot(split, chosen, preferred_element_type=F32)
        for k in range(4):
            total = total + jnp.where(
                rank == s * 4 + k, candidates[k * 32 : (k + 1) * 32], 0.0
            )
    for x in range(2):
        for y in range(2):
            at = (x * 2 + y) * depth
            out_ref[:ROWS, y, x, :] = total[:ROWS, at : at + depth]
            out_ref[ROWS:, y, x, :] = load_ref[:, x, y, :]


def shifts(shape):
    plane = lax.broadcasted_iota(jnp.int32, shape, 0)
    column = lax.broadcasted_iota(jnp.int32, shape, 1)
    planes, columns = shape

    def next_x(v):
        return jnp.where(plane == planes - 1, 0.0, pltpu.roll(v, planes - 1, 0))

    def prev_x(v):
        return jnp.where(plane == 0, 0.0, pltpu.roll(v, 1, 0))

    def next_z(v):
        return jnp.where(column == columns - 1, 0.0, pltpu.roll(v, columns - 1, 1))

    def prev_z(v):
        return jnp.where(column == 0, 0.0, pltpu.roll(v, 1, 1))

    return next_x, prev_x, next_z, prev_z


def strain_rows(nodes, lower, upper, moves):
    next_x, _, next_z, _ = moves
    sums, diffs = {}, {}
    for y in range(lower, upper + 2):
        for c in range(3):
            v = nodes[y][c]
            w = next_z(v)
            sums[y, c] = v + w
            diffs[y, c] = w - v
    strain = {}
    for y in range(lower, upper + 1):
        grad = []
        for c in range(3):
            both = sums[y, c] + sums[y + 1, c]
            rise = sums[y + 1, c] - sums[y, c]
            turn = diffs[y, c] + diffs[y + 1, c]
            grad.append(
                (
                    0.25 * (next_x(both) - both),
                    0.25 * (next_x(rise) + rise),
                    0.25 * (next_x(turn) + turn),
                )
            )
        strain[y] = (
            grad[0][0],
            grad[1][1],
            grad[2][2],
            grad[1][2] + grad[2][1],
            grad[0][2] + grad[2][0],
            grad[0][1] + grad[1][0],
        )
    return strain


def force_rows(stress, lower, upper, moves):
    _, prev_x, _, prev_z = moves
    xs = {}
    for y in range(lower - 1, upper + 1):
        for c in range(3):
            a, b, d = (stress[y][VOIGT[c][k]] for k in range(3))
            xs[y, c] = (prev_x(a) - a, prev_x(b) + b, prev_x(d) + d)
    force = {}
    for y in range(lower, upper + 1):
        parts = []
        for c in range(3):
            a0, b0, d0 = xs[y - 1, c]
            a1, b1, d1 = xs[y, c]
            flat = (a0 + a1) + (b0 - b1)
            deep = d0 + d1
            parts.append(0.25 * (prev_z(flat + deep) + (flat - deep)))
        force[y] = tuple(parts)
    return force


def apply_rows(nodes, tangent, lower, upper, moves):
    strain = strain_rows(nodes, lower - 1, upper, moves)
    stress = {}
    for y in range(lower - 1, upper + 1):
        rows = []
        for i in range(6):
            total = tangent(y, TANGENT[i, 0]) * strain[y][0]
            for j in range(1, 6):
                total = total + tangent(y, TANGENT[i, j]) * strain[y][j]
            rows.append(total)
        stress[y] = tuple(rows)
    force = force_rows(stress, lower, upper, moves)
    return {
        y: tuple(MASS * nodes[y][c] + force[y][c] for c in range(3))
        for y in range(lower, upper + 1)
    }


def value_reader(low_ref, own_ref, high_ref):
    def read(y, c):
        if y < 0:
            return low_ref[c, y + 2]
        if y < 2:
            return own_ref[c, y]
        return high_ref[c, y - 2]

    return read


def read_rows(ref, lower, count):
    return {lower + k: tuple(ref[c, k] for c in range(3)) for k in range(count)}


def inside(rows, y, last_ref):
    keep = jnp.where(last_ref[0] == 1, 0.0, 1.0)
    rows[y] = tuple(v * keep for v in rows[y])


def write_rows(ref, rows, lower, count):
    for k in range(count):
        for c in range(3):
            ref[c, k] = rows[lower + k][c]


def row_dot(first, second):
    total = None
    for y in (0, 1):
        for c in range(3):
            term = first[y][c] * second[y][c]
            total = term if total is None else total + term
    return total


def pack_dots(ref, products):
    lane = lax.broadcasted_iota(jnp.int32, (1, DOTS), 1)
    packed = jnp.zeros((1, DOTS), F32)
    for k, product in enumerate(products):
        total = jnp.sum(jnp.sum(product, axis=0, keepdims=True), axis=1, keepdims=True)
        packed = packed + jnp.where(lane == k, total, 0.0)
    ref[...] = jnp.broadcast_to(packed[None], ref.shape)


def unpack_dots(ref, count):
    row = jnp.sum(ref[...].reshape(-1, DOTS), axis=0, keepdims=True)
    lane = lax.broadcasted_iota(jnp.int32, (1, DOTS), 1)
    return [
        jnp.sum(jnp.where(lane == k, row, 0.0), axis=1, keepdims=True) for k in range(count)
    ]


def basis_steps(marks_ref):
    lane = lax.broadcasted_iota(jnp.int32, (1, DOTS), 1)
    mark = jnp.sum(jnp.where(lane == MARK, marks_ref[...], 0.0), axis=1, keepdims=True)
    reach = 0.5 * BASIS * mark
    return MASS + reach, reach


def chebyshev(image, now, before, center, half):
    scale = 2.0 / half
    return {
        y: tuple((image[y][c] - center * now[y][c]) * scale - before[y][c] for c in range(3))
        for y in image
    }


def first_kernel(flags_ref, marks_ref, low_ref, own_ref, high_ref, v0_ref, v1_ref):
    read = value_reader(low_ref, own_ref, high_ref)
    moves = shifts(own_ref.shape[2:])
    center, half = basis_steps(marks_ref)
    stress = {y: tuple(read(y, i) for i in range(6)) for y in range(-2, 3)}
    force = force_rows(stress, -1, 2, moves)
    v0 = {y: tuple(read(y, LOAD + c) - force[y][c] for c in range(3)) for y in range(-1, 3)}
    inside(v0, 2, flags_ref)
    image = apply_rows(v0, read, 0, 1, moves)
    scale = 1.0 / half
    v1 = {y: tuple((image[y][c] - center * v0[y][c]) * scale for c in range(3)) for y in (0, 1)}
    write_rows(v0_ref, v0, -1, 4)
    write_rows(v1_ref, v1, 0, 2)


def next_two(flags_ref, marks_ref, read, moves, before, low_ref, own_ref, high_ref):
    center, half = basis_steps(marks_ref)
    now = read_rows(low_ref, -2, 2) | read_rows(own_ref, 0, 2) | read_rows(high_ref, 2, 2)
    after = chebyshev(apply_rows(now, read, -1, 2, moves), now, before, center, half)
    inside(after, 2, flags_ref)
    last = chebyshev(apply_rows(after, read, 0, 1, moves), after, now, center, half)
    return now, after, last


def second_kernel(
    flags_ref,
    marks_ref,
    low_ref,
    own_ref,
    high_ref,
    v0_ref,
    v1_low_ref,
    v1_ref,
    v1_high_ref,
    v2_ref,
    v3_ref,
):
    read = value_reader(low_ref, own_ref, high_ref)
    moves = shifts(own_ref.shape[2:])
    _, v2, v3 = next_two(
        flags_ref,
        marks_ref,
        read,
        moves,
        read_rows(v0_ref, -1, 4),
        v1_low_ref,
        v1_ref,
        v1_high_ref,
    )
    write_rows(v2_ref, v2, -1, 4)
    write_rows(v3_ref, v3, 0, 2)


def basis_pairs():
    return [(i, j) for i in range(6) for j in range(i, 6)]


def third_kernel(
    flags_ref,
    marks_ref,
    low_ref,
    own_ref,
    high_ref,
    v0_ref,
    v1_ref,
    v2_ref,
    v3_low_ref,
    v3_ref,
    v3_high_ref,
    v4_ref,
    v5_ref,
    dots_ref,
):
    read = value_reader(low_ref, own_ref, high_ref)
    moves = shifts(own_ref.shape[2:])
    v2 = read_rows(v2_ref, -1, 4)
    v3, v4, v5 = next_two(
        flags_ref, marks_ref, read, moves, v2, v3_low_ref, v3_ref, v3_high_ref
    )
    write_rows(v4_ref, v4, 0, 2)
    write_rows(v5_ref, v5, 0, 2)
    basis = [read_rows(v0_ref, -1, 4), read_rows(v1_ref, 0, 2), v2, v3, v4, v5]
    pack_dots(dots_ref, [row_dot(basis[i], basis[j]) for i, j in basis_pairs()])


def total_of(terms):
    total = None
    for term in terms:
        total = term if total is None else total + term
    return total


def place_planes(increment_ref, residual_ref, solved, left, basis, rows_ref, first):
    for ref, weights in ((increment_ref, solved), (residual_ref, left)):
        for y in (0, 1):
            for c in range(3):
                rows_ref[...] = total_of(w * basis[k][y][c] for k, w in enumerate(weights))
                for x in (0, 1):
                    ref[c, x, pl.ds(y, 1), :] = rows_ref[pl.ds(first + x, 1), :]


def fourth_kernel(
    flags_ref,
    marks_ref,
    sums_ref,
    v0_ref,
    v1_ref,
    v2_ref,
    v3_ref,
    v4_ref,
    v5_ref,
    increment_ref,
    residual_ref,
    trust_ref,
    rows_ref,
):
    center, half = basis_steps(marks_ref)
    dots = unpack_dots(sums_ref, 21)
    gram = {}
    for k, (i, j) in enumerate(basis_pairs()):
        gram[i, j] = gram[j, i] = dots[k]

    def image_of(p):
        count = len(p)
        image = []
        for i in range(count + 1):
            terms = []
            if i < count:
                terms.append(center * p[i])
            if i > 0:
                terms.append((half if i == 1 else 0.5 * half) * p[i - 1])
            if i + 1 < count:
                terms.append(0.5 * half * p[i + 1])
            image.append(total_of(terms))
        return image

    def product(p, q):
        return total_of(
            p[i] * total_of(gram[i, j] * q[j] for j in range(len(q))) for i in range(len(p))
        )

    def size(p, q):
        return total_of(
            jnp.abs(p[i]) * total_of(jnp.abs(gram[i, j]) * jnp.abs(q[j]) for j in range(len(q)))
            for i in range(len(p))
        )

    def combine(p, factor, q):
        longer = max(len(p), len(q))
        return [
            (p[k] + factor * q[k] if k < len(p) else factor * q[k]) if k < len(q) else p[k]
            for k in range(longer)
        ]

    solved = []
    left = [jnp.ones((1, 1), F32)]
    course = left
    norm = gram[0, 0]
    for step in range(5):
        image = image_of(course)
        bend = product(course, image)
        if step == 4:
            spread = size(course, image) / bend
            trusted = jnp.where((spread > 0.0) & (spread < TRUST) & trusted, 1, 0)
        alpha = norm / bend
        solved = combine(solved, alpha, course)
        left = combine(left, -alpha, image)
        if step < 4:
            fresh = product(left, left)
            if step == 3:
                spread = size(left, left) / fresh
                trusted = (spread > 0.0) & (spread < TRUST)
            course = combine(left, fresh / norm, course)
            norm = fresh
    basis = [
        read_rows(v0_ref, -1, 4),
        read_rows(v1_ref, 0, 2),
        read_rows(v2_ref, -1, 4),
        read_rows(v3_ref, 0, 2),
        read_rows(v4_ref, 0, 2),
        read_rows(v5_ref, 0, 2),
    ]
    trust_ref[...] = trusted
    place_planes(increment_ref, residual_ref, solved, left, basis, rows_ref, flags_ref[1])


def careful_first(low_ref, own_ref, high_ref, v0_ref, v1_ref):
    read = value_reader(low_ref, own_ref, high_ref)
    moves = shifts(own_ref.shape[2:])
    write_rows(v1_ref, apply_rows(read_rows(v0_ref, -1, 4), read, 0, 1, moves), 0, 2)


def careful_second(
    last_ref, low_ref, own_ref, high_ref, v0_ref, v1_low_ref, v1_ref, v1_high_ref, v2_ref, dots_ref
):
    read = value_reader(low_ref, own_ref, high_ref)
    moves = shifts(own_ref.shape[2:])
    v1 = read_rows(v1_low_ref, -2, 2) | read_rows(v1_ref, 0, 2) | read_rows(v1_high_ref, 2, 2)
    v2 = apply_rows(v1, read, -1, 2, moves)
    inside(v2, 2, last_ref)
    v0 = read_rows(v0_ref, -1, 4)
    write_rows(v2_ref, v2, -1, 4)
    pack_dots(
        dots_ref,
        [
            row_dot(a, b)
            for a, b in ((v0, v0), (v0, v1), (v0, v2), (v1, v1), (v1, v2))
        ],
    )


def careful_third(
    low_ref,
    own_ref,
    high_ref,
    v0_ref,
    v1_low_ref,
    v1_ref,
    v1_high_ref,
    v2_ref,
    sums_ref,
    r1_ref,
    r2_ref,
    w3_ref,
    coef_ref,
):
    read = value_reader(low_ref, own_ref, high_ref)
    moves = shifts(own_ref.shape[2:])
    m00, m01, m02, m11, m12 = unpack_dots(sums_ref, 5)
    a0 = m00 / m01
    n1 = m00 - 2.0 * a0 * m01 + a0 * a0 * m11
    b0 = n1 / m00
    e = 1.0 + b0
    a1 = n1 / (e * e * m01 - e * a0 * (m02 + m11) + a0 * a0 * m12)
    center = 0.5 * (1.0 / a0 + 1.0 / a1 + b0 / a0)
    v0 = read_rows(v0_ref, -1, 4)
    v1 = read_rows(v1_low_ref, -2, 2) | read_rows(v1_ref, 0, 2) | read_rows(v1_high_ref, 2, 2)
    v2 = read_rows(v2_ref, -1, 4)
    along, twice = a0 + a1 * e, a1 * a0
    r2 = {
        y: tuple(v0[y][c] - along * v1[y][c] + twice * v2[y][c] for c in range(3))
        for y in range(-1, 3)
    }
    image = apply_rows(r2, read, 0, 1, moves)
    scale = 1.0 / center
    w3 = {y: tuple(image[y][c] * scale - r2[y][c] for c in range(3)) for y in (0, 1)}
    r1 = {y: tuple(v0[y][c] - a0 * v1[y][c] for c in range(3)) for y in (0, 1)}
    write_rows(r1_ref, r1, 0, 2)
    write_rows(r2_ref, r2, 0, 2)
    write_rows(w3_ref, w3, 0, 2)
    lane = lax.broadcasted_iota(jnp.int32, (1, DOTS), 1)
    packed = jnp.zeros((1, DOTS), F32)
    for k, value in enumerate((a0, b0, a1, n1, center)):
        packed = packed + jnp.where(lane == k, value, 0.0)
    coef_ref[...] = packed


def careful_fourth(
    last_ref,
    low_ref,
    own_ref,
    high_ref,
    coef_ref,
    v0_ref,
    r1_ref,
    r2_ref,
    w3_low_ref,
    w3_ref,
    w3_high_ref,
    w4_ref,
    w5_ref,
    dots_ref,
):
    read = value_reader(low_ref, own_ref, high_ref)
    moves = shifts(own_ref.shape[2:])
    scale = 1.0 / unpack_dots(coef_ref, 5)[4]
    w3 = read_rows(w3_low_ref, -2, 2) | read_rows(w3_ref, 0, 2) | read_rows(w3_high_ref, 2, 2)
    image = apply_rows(w3, read, -1, 2, moves)
    w4 = {y: tuple(image[y][c] * scale - w3[y][c] for c in range(3)) for y in range(-1, 3)}
    inside(w4, 2, last_ref)
    image = apply_rows(w4, read, 0, 1, moves)
    w5 = {y: tuple(image[y][c] * scale - w4[y][c] for c in range(3)) for y in (0, 1)}
    write_rows(w4_ref, w4, 0, 2)
    write_rows(w5_ref, w5, 0, 2)
    v0 = read_rows(v0_ref, -1, 4)
    basis = [v0, read_rows(r1_ref, 0, 2), read_rows(r2_ref, 0, 2), w3, w4, w5]
    pack_dots(dots_ref, [row_dot(basis[i], basis[j]) for i, j in basis_pairs()])


def careful_fifth(
    flags_ref,
    coef_ref,
    sums_ref,
    v0_ref,
    r1_ref,
    r2_ref,
    w3_ref,
    w4_ref,
    w5_ref,
    increment_ref,
    residual_ref,
    rows_ref,
):
    a0, b0, a1, n1, center = unpack_dots(coef_ref, 5)
    dots = unpack_dots(sums_ref, 21)
    gram = {}
    for k, (i, j) in enumerate(basis_pairs()):
        gram[i, j] = gram[j, i] = dots[k]
    zero = jnp.zeros((1, 1), F32)
    one = jnp.ones((1, 1), F32)
    i0, i1 = 1.0 / a0, 1.0 / a1

    def image_of(p):
        return [
            i0 * p[0] - b0 * i0 * p[1],
            (i1 + b0 * i0) * p[1] - i0 * p[0],
            center * p[2] - i1 * p[1],
            center * (p[2] + p[3]),
            center * (p[3] + p[4]),
            center * p[4],
        ]

    def product(p, q):
        return total_of(
            p[i] * total_of(gram[i, j] * q[j] for j in range(6)) for i in range(6)
        )

    solved = [a0 + a1 * b0, a1, zero, zero, zero, zero]
    left = [zero, zero, one, zero, zero, zero]
    norm = gram[2, 2]
    ratio = norm / n1
    course = [ratio * b0, ratio, one, zero, zero, zero]
    for step in range(3):
        image = image_of(course)
        alpha = norm / product(course, image)
        solved = [s + alpha * p for s, p in zip(solved, course)]
        left = [r - alpha * q for r, q in zip(left, image)]
        if step < 2:
            fresh = product(left, left)
            ratio = fresh / norm
            course = [r + ratio * p for r, p in zip(left, course)]
            norm = fresh
    v0 = read_rows(v0_ref, -1, 4)
    basis = [v0] + [read_rows(ref, 0, 2) for ref in (r1_ref, r2_ref, w3_ref, w4_ref, w5_ref)]
    place_planes(increment_ref, residual_ref, solved, left, basis, rows_ref, flags_ref[1])


def local_call(kernel, outs, name, *args, flags=None, scratch=()):
    typed = [out if isinstance(out[0], tuple) else (out, F32) for out in outs]
    specs = [pl.BlockSpec(memory_space=pltpu.VMEM)] * len(args)
    if flags is not None:
        specs = [pl.BlockSpec(memory_space=pltpu.SMEM)] + specs
        args = (flags,) + args
    return pl.pallas_call(
        kernel,
        in_specs=specs,
        out_specs=[pl.BlockSpec(memory_space=pltpu.VMEM)] * len(outs),
        out_shape=[jax.ShapeDtypeStruct(*out) for out in typed],
        scratch_shapes=scratch,
        compiler_params=pltpu.CompilerParams(vmem_limit_bytes=48 * 1024 * 1024),
        name=name,
    )(*args)


def up_and_down(up, down):
    count = lax.axis_size(MICRO)
    forward = [(k, k + 1) for k in range(count - 1)]
    backward = [(k + 1, k) for k in range(count - 1)]
    return lax.ppermute(up, MICRO, forward), lax.ppermute(down, MICRO, backward)


def swapped(block):
    return lax.all_to_all(block, MICRO, split_axis=0, concat_axis=0, tiled=True)


def gather_planes(block):
    count = lax.axis_size("macro")
    pieces = [block] + [
        lax.ppermute(block, "macro", [(k, (k - shift) % count) for k in range(count)])
        for shift in range(1, count)
    ]
    planes = block.shape[2]
    twice = jnp.concatenate(pieces + pieces[:-1], axis=2)
    start = (count - lax.axis_index("macro")) % count * planes
    return lax.dynamic_slice_in_dim(twice, start, count * planes, axis=2)


def shards(
    displacement,
    load,
    routes,
    counts,
    stiffness,
    precond,
    forcing,
    coupling,
    lame_first,
    lame_shear,
):
    planes, width, depth = displacement.shape[1:]
    points = planes * width * depth
    rows_x = lax.axis_size("macro")
    owners = lax.axis_size(MICRO)
    right = lax.ppermute(displacement, "macro", [(a + 1, a) for a in range(rows_x - 1)])
    above = lax.ppermute(displacement, MICRO, [(b + 1, b) for b in range(owners - 1)])
    corner = lax.ppermute(
        displacement,
        ("macro",) + MICRO,
        [
            ((a + 1) * owners + b + 1, a * owners + b)
            for a in range(rows_x - 1)
            for b in range(owners - 1)
        ],
    )
    place, mark, kept = local_call(
        functools.partial(rank_kernel, owners),
        (((8, points), jnp.int32), (1, 1), displacement.shape),
        "rank",
        lame_first.reshape(1, 1),
        lame_shear.reshape(1, 1),
        coupling[0].T,
        routes.reshape(1, points),
        counts.reshape(1, points),
        displacement,
    )
    (send,) = local_call(
        dispatch_kernel,
        ((owners, 2, 128),),
        "dispatch",
        place,
        mark,
        kept,
        right,
        above,
        corner,
    )
    send, forcing, coupling = lax.optimization_barrier((send, forcing, coupling))
    back, marks = micro_solve(
        swapped(send),
        stiffness[0],
        precond[0],
        forcing[0],
        coupling[0],
        lame_first[0],
        lame_shear[0],
    )
    (values,) = local_call(
        pick_kernel, ((FIELDS, width, planes, depth),), "pick", swapped(back), place, load
    )
    own = gather_planes(values)
    low, high = up_and_down(own, own[:, :1])
    flags = jnp.stack(
        [
            (lax.axis_index(MICRO) == owners - 1).astype(jnp.int32),
            (lax.axis_index("macro") * planes).astype(jnp.int32),
        ]
    )
    sets = (marks, low, own, high)
    whole = own.shape[2]
    two = (3, 2, whole, depth)
    four = (3, 4, whole, depth)
    v0, v1 = local_call(first_kernel, (four, two), "first_rows", *sets, flags=flags)
    v1_low, v1_high = up_and_down(v1, v1)
    v2, v3 = local_call(
        second_kernel, (four, two), "second_rows", *sets, v0, v1_low, v1, v1_high, flags=flags
    )
    v3_low, v3_high = up_and_down(v3, v3)
    v4, v5, dots = local_call(
        third_kernel,
        (two, two, (owners, 1, DOTS)),
        "third_rows",
        *sets,
        v0,
        v1,
        v2,
        v3_low,
        v3,
        v3_high,
        flags=flags,
    )
    mine = (3, planes, width, depth)
    scratch = [pltpu.VMEM((whole, depth), F32)]
    increment, residual, trust = local_call(
        fourth_kernel,
        (mine, mine, ((1, 1), jnp.int32)),
        "fourth_rows",
        marks,
        swapped(dots),
        v0,
        v1,
        v2,
        v3,
        v4,
        v5,
        flags=flags,
        scratch=scratch,
    )

    def careful():
        sets = (low, own, high)
        line = (1, DOTS)
        (u1,) = local_call(careful_first, (two,), "careful_first", *sets, v0)
        u1_low, u1_high = up_and_down(u1, u1)
        u2, dots = local_call(
            careful_second,
            (four, (owners, 1, DOTS)),
            "careful_second",
            *sets,
            v0,
            u1_low,
            u1,
            u1_high,
            flags=flags,
        )
        r1, r2, w3, coef = local_call(
            careful_third,
            (two, two, two, line),
            "careful_third",
            *sets,
            v0,
            u1_low,
            u1,
            u1_high,
            u2,
            swapped(dots),
        )
        w3_low, w3_high = up_and_down(w3, w3)
        w4, w5, dots = local_call(
            careful_fourth,
            (two, two, (owners, 1, DOTS)),
            "careful_fourth",
            *sets,
            coef,
            v0,
            r1,
            r2,
            w3_low,
            w3,
            w3_high,
            flags=flags,
        )
        return tuple(
            local_call(
                careful_fifth,
                (mine, mine),
                "careful_fifth",
                coef,
                swapped(dots),
                v0,
                r1,
                r2,
                w3,
                w4,
                w5,
                flags=flags,
                scratch=scratch,
            )
        )

    return lax.cond(trust[0, 0] == 1, lambda: (increment, residual), careful)


def solution(mesh):
    split = Mesh(
        mesh.devices.reshape(mesh.shape["macro"], 4, 8, 2),
        ("macro", "micro_0", "micro_1", "micro_2"),
    )
    placed = (
        P(None, "macro", MICRO, None),
        P(None, "macro", MICRO, None),
        P("macro", MICRO, None, None),
        P("macro", MICRO, None),
        P(MICRO, None, None),
        P(MICRO, None, None),
        P(MICRO, None, None),
        P(MICRO, None, None),
        P(MICRO),
        P(MICRO),
    )
    return jax.shard_map(
        shards,
        mesh=split,
        in_specs=placed,
        out_specs=(P(None, "macro", MICRO, None), P(None, "macro", MICRO, None)),
        check_vma=False,
    )
```

```python
import functools

import jax
import jax.numpy as jnp
import numpy as np
from jax import lax
from jax.experimental import pallas as pl
from jax.experimental.pallas import tpu as pltpu
from jax.sharding import Mesh
from jax.sharding import PartitionSpec as P

ITMAX = 4
MICRO = ("micro_0", "micro_1", "micro_2")

BETA = 0.1
OMEGA = 0.8
MASS = 0.1
VOIGT = ((0, 5, 4), (5, 1, 3), (4, 3, 2))
PAIRS = tuple((i, j) for i in range(6) for j in range(i, 6))
TANGENT = {}
for number, (i, j) in enumerate(PAIRS):
    TANGENT[i, j] = TANGENT[j, i] = 6 + number
ROWS = 27
LOAD = 27
FIELDS = 30
DOTS = 128
BASIS = 3.5
TRUST = 2e4
MARK = 7 * 32 - 128
F32 = jnp.float32
BF16 = jnp.bfloat16


def three_parts(value):
    high = value.astype(BF16)
    rest = value - high.astype(F32)
    middle = rest.astype(BF16)
    return high, middle, (rest - middle.astype(F32)).astype(BF16)


def hot_rows(count, index):
    return lax.broadcasted_iota(jnp.int32, (count, index.shape[1]), 0) == index


def rank_kernel(
    owners, first_ref, shear_ref, couple_ref, routes_ref, counts_ref, here_ref, place_ref, mark_ref, own_ref
):
    depth = here_ref.shape[3]
    own_ref[...] = here_ref[...]
    owner = routes_ref[...]
    chosen = jnp.where(hot_rows(owners, owner), 1.0, 0.0)
    pieces = [chosen[:, k * depth : (k + 1) * depth] for k in range(4)]
    earlier = lax.broadcasted_iota(jnp.int32, (depth, depth), 0) < lax.broadcasted_iota(
        jnp.int32, (depth, depth), 1
    )
    within = jnp.dot(
        jnp.concatenate(pieces, axis=0).astype(BF16),
        jnp.where(earlier, 1.0, 0.0).astype(BF16),
        preferred_element_type=F32,
    )
    running = jnp.zeros((owners, 1), F32)
    ranks = []
    for k in range(4):
        seen = within[k * owners : (k + 1) * owners] + running
        ranks.append(jnp.sum(pieces[k] * seen, axis=0, keepdims=True))
        running = running + jnp.sum(pieces[k], axis=1, keepdims=True)
    rank = jnp.concatenate(ranks, axis=1).astype(jnp.int32)
    place_ref[0:1] = owner
    place_ref[1:2] = rank
    place_ref[2:3] = counts_ref[...]
    axial = couple_ref[...].astype(F32)[:3]
    stretch = jnp.sum(jnp.sum(axial * axial, axis=0, keepdims=True), axis=1, keepdims=True)
    mark = (first_ref[...] + 2.0 * shear_ref[...] + stretch / 6.0) / owners
    mark_ref[...] = mark


def dispatch_kernel(
    place_ref, mark_ref, own_ref, right_ref, above_ref, corner_ref, send_ref
):
    owners = send_ref.shape[0]
    depth = own_ref.shape[3]
    capacity = 32
    column = lax.broadcasted_iota(jnp.int32, (3, depth), 1)
    sums, diffs = {}, {}
    for x in range(3):
        for y in range(3):
            ref = ((own_ref, above_ref), (right_ref, corner_ref))[x // 2][y // 2]
            node = ref[:, x % 2, y % 2, :]
            after = jnp.where(column == depth - 1, 0.0, pltpu.roll(node, depth - 1, 1))
            sums[x, y] = node + after
            diffs[x, y] = after - node
    blocks = []
    for x in range(2):
        for y in range(2):
            s00, s01, s10, s11 = sums[x, y], sums[x, y + 1], sums[x + 1, y], sums[x + 1, y + 1]
            grad_x = 0.25 * ((s10 + s11) - (s00 + s01))
            grad_y = 0.25 * ((s01 + s11) - (s00 + s10))
            grad_z = 0.25 * (
                (diffs[x, y] + diffs[x, y + 1]) + (diffs[x + 1, y] + diffs[x + 1, y + 1])
            )
            blocks.append(
                jnp.concatenate(
                    [
                        grad_x[0:1],
                        grad_y[1:2],
                        grad_z[2:3],
                        grad_z[1:2] + grad_y[2:3],
                        grad_z[0:1] + grad_x[2:3],
                        grad_y[0:1] + grad_x[1:2],
                    ],
                    axis=0,
                )
            )
    values = jnp.concatenate(blocks, axis=1)
    chosen = jnp.where(hot_rows(owners, place_ref[0:1]), 1.0, 0.0)
    rank = place_ref[1:2]
    at_rank = hot_rows(capacity, rank)
    leaving = jnp.concatenate([values, place_ref[2:3].astype(F32)], axis=0)
    chosen = chosen.astype(BF16)
    total = None
    for part in three_parts(leaving):
        part = part.astype(F32)
        spread = [jnp.where(at_rank, part[c : c + 1], 0.0) for c in range(7)]
        spread.append(jnp.zeros_like(spread[0]))
        term = lax.dot_general(
            chosen,
            jnp.concatenate(spread, axis=0).astype(BF16),
            (((1,), (1,)), ((), ())),
            preferred_element_type=F32,
        )
        total = term if total is None else total + term
    lane = lax.broadcasted_iota(jnp.int32, (owners, 128), 1)
    send_ref[:, 0, :] = total[:, :128]
    send_ref[:, 1, :] = jnp.where(lane >= MARK, mark_ref[...], total[:, 128:])


def micro_kernel(
    got_ref,
    stiff_ref,
    pre_ref,
    force_ref,
    couple_ref,
    products_ref,
    cols_ref,
    out_ref,
    marks_ref,
    points_ref,
):
    tile = pl.program_id(0)
    owners = got_ref.shape[0]

    @pl.when(tile == 0)
    def _():
        points_ref[:128] = got_ref[:, 0, :].T
        second = got_ref[:, 1, :]
        points_ref[128:] = second.T
        marks_ref[...] = jnp.sum(second, axis=0, keepdims=True)

    stiff = stiff_ref[...]
    pre = pre_ref[...]
    halves = 4
    parts, loads, modes, sweeps = [], [], [], []
    for h in range(halves):
        part = jnp.concatenate(
            [points_ref[pl.ds(tile * 16 + h * 4 + k, 8, stride=32), :] for k in range(4)], axis=1
        )
        parts.append(part)
        loads.append(jnp.dot(force_ref[...], part.astype(BF16), preferred_element_type=F32))
        sweeps.append(part[6:7])
    for h in range(halves):
        modes.append(OMEGA * jnp.dot(pre, loads[h].astype(BF16), preferred_element_type=F32))
    for sweep in range(1, ITMAX):
        misfits = []
        for h in range(halves):
            misfit = (
                jnp.dot(stiff, modes[h].astype(BF16), preferred_element_type=F32)
                + BETA * jnp.tanh(modes[h])
                - loads[h]
            )
            misfits.append(misfit.astype(BF16))
        for h in range(halves):
            update = modes[h] - OMEGA * jnp.dot(pre, misfits[h], preferred_element_type=F32)
            modes[h] = jnp.where(sweeps[h] > sweep, update, modes[h])
    couple = couple_ref[...]
    products = products_ref[...]
    high = products.astype(BF16)
    low = (products - high.astype(F32)).astype(BF16)
    both = jnp.concatenate([high, low], axis=0)
    cols = cols_ref[...]
    for h in range(halves):
        bent = jnp.tanh(modes[h])
        slope = 1.0 - bent * bent
        slope_high = slope.astype(BF16)
        slope_low = (slope - slope_high.astype(F32)).astype(BF16)
        curved = jnp.dot(both, slope_high, preferred_element_type=F32)
        rows = (
            jnp.dot(couple, modes[h].astype(BF16), preferred_element_type=F32)
            + curved[:32]
            + curved[32:]
            + jnp.dot(high, slope_low, preferred_element_type=F32)
            + cols[:, 0:1]
        )
        part = parts[h]
        trace = part[0:1] + part[1:2] + part[2:3]
        elastic = cols[:8, 1:2] * trace + cols[:8, 2:3] * part
        rows = jnp.concatenate([rows[:8] + elastic, rows[8:]], axis=0)
        turned = []
        for k in range(2):
            pair = rows[:, k * 2 * owners : (k + 1) * 2 * owners].T
            turned += [pair[:owners], pair[owners:]]
        out_ref[:, pl.ds(tile * 4 + h, 1), :] = jnp.concatenate(turned, axis=1)[:, None, :]


def micro_solve(got, stiffness, precond, forcing, coupling, lame_first, lame_shear):
    modes = stiffness.shape[0]
    owners = got.shape[0]
    force = jnp.pad(forcing, ((0, 2), (0, 0))).T
    wide = coupling.astype(F32).T
    products = jnp.pad(jnp.stack([wide[i] * wide[j] for i, j in PAIRS]), ((6, 5), (0, 0)))
    couple = jnp.pad(coupling.T, ((0, 26), (0, 0)))
    base_first = [0.0] * 6 + [float(i < 3 and j < 3) for i, j in PAIRS] + [0.0] * 5
    base_shear = (
        [0.0] * 6
        + [2.0 * float(i == j and i < 3) + float(i == j and i >= 3) for i, j in PAIRS]
        + [0.0] * 5
    )
    on_trace = [1.0] * 3 + [0.0] * 29
    on_strain = [2.0] * 3 + [1.0] * 3 + [0.0] * 26
    firsts = np.zeros((32, 8), np.float32)
    shears = np.zeros((32, 8), np.float32)
    firsts[:, 0], firsts[:, 1] = base_first, on_trace
    shears[:, 0], shears[:, 2] = base_shear, on_strain
    cols = lame_first * firsts + lame_shear * shears
    whole = lambda *shape: pl.BlockSpec(shape, lambda step: (0,) * len(shape))
    return pl.pallas_call(
        micro_kernel,
        grid=(2,),
        in_specs=[
            whole(owners, 2, 128),
            whole(modes, modes),
            whole(modes, modes),
            whole(modes, 8),
            whole(32, modes),
            whole(32, modes),
            whole(32, 8),
        ],
        out_specs=[whole(owners, 8, 128), whole(1, 128)],
        out_shape=[
            jax.ShapeDtypeStruct((owners, 8, 128), F32),
            jax.ShapeDtypeStruct((1, 128), F32),
        ],
        scratch_shapes=[pltpu.VMEM((256, owners), F32)],
        compiler_params=pltpu.CompilerParams(vmem_limit_bytes=48 * 1024 * 1024),
        name="micro_solve",
    )(got, stiffness, precond, force, couple, products, cols)


def pick_kernel(back_ref, place_ref, load_ref, out_ref):
    owners = back_ref.shape[0]
    depth = out_ref.shape[3]
    owner = place_ref[0:1]
    rank = place_ref[1:2]
    chosen = jnp.where(hot_rows(owners, owner), 1.0, 0.0).astype(BF16)
    chosen = jnp.concatenate([chosen] * 3, axis=0)
    total = jnp.zeros((32, owner.shape[1]), F32)
    for s in range(8):
        turned = back_ref[:, s, :].T
        split = jnp.concatenate(three_parts(turned), axis=1)
        candidates = jnp.dot(split, chosen, preferred_element_type=F32)
        for k in range(4):
            total = total + jnp.where(
                rank == s * 4 + k, candidates[k * 32 : (k + 1) * 32], 0.0
            )
    for x in range(2):
        for y in range(2):
            at = (x * 2 + y) * depth
            out_ref[:ROWS, y, x, :] = total[:ROWS, at : at + depth]
            out_ref[ROWS:, y, x, :] = load_ref[:, x, y, :]


def shifts(shape):
    plane = lax.broadcasted_iota(jnp.int32, shape, 0)
    column = lax.broadcasted_iota(jnp.int32, shape, 1)
    planes, columns = shape

    def next_x(v):
        return jnp.where(plane == planes - 1, 0.0, pltpu.roll(v, planes - 1, 0))

    def prev_x(v):
        return jnp.where(plane == 0, 0.0, pltpu.roll(v, 1, 0))

    def next_z(v):
        return jnp.where(column == columns - 1, 0.0, pltpu.roll(v, columns - 1, 1))

    def prev_z(v):
        return jnp.where(column == 0, 0.0, pltpu.roll(v, 1, 1))

    return next_x, prev_x, next_z, prev_z


def strain_rows(nodes, lower, upper, moves):
    next_x, _, next_z, _ = moves
    sums, diffs = {}, {}
    for y in range(lower, upper + 2):
        for c in range(3):
            v = nodes[y][c]
            w = next_z(v)
            sums[y, c] = v + w
            diffs[y, c] = w - v
    strain = {}
    for y in range(lower, upper + 1):
        grad = []
        for c in range(3):
            both = sums[y, c] + sums[y + 1, c]
            rise = sums[y + 1, c] - sums[y, c]
            turn = diffs[y, c] + diffs[y + 1, c]
            grad.append(
                (
                    0.25 * (next_x(both) - both),
                    0.25 * (next_x(rise) + rise),
                    0.25 * (next_x(turn) + turn),
                )
            )
        strain[y] = (
            grad[0][0],
            grad[1][1],
            grad[2][2],
            grad[1][2] + grad[2][1],
            grad[0][2] + grad[2][0],
            grad[0][1] + grad[1][0],
        )
    return strain


def force_rows(stress, lower, upper, moves):
    _, prev_x, _, prev_z = moves
    xs = {}
    for y in range(lower - 1, upper + 1):
        for c in range(3):
            a, b, d = (stress[y][VOIGT[c][k]] for k in range(3))
            xs[y, c] = (prev_x(a) - a, prev_x(b) + b, prev_x(d) + d)
    force = {}
    for y in range(lower, upper + 1):
        parts = []
        for c in range(3):
            a0, b0, d0 = xs[y - 1, c]
            a1, b1, d1 = xs[y, c]
            flat = (a0 + a1) + (b0 - b1)
            deep = d0 + d1
            parts.append(0.25 * (prev_z(flat + deep) + (flat - deep)))
        force[y] = tuple(parts)
    return force


def apply_rows(nodes, tangent, lower, upper, moves):
    strain = strain_rows(nodes, lower - 1, upper, moves)
    stress = {}
    for y in range(lower - 1, upper + 1):
        rows = []
        for i in range(6):
            total = tangent(y, TANGENT[i, 0]) * strain[y][0]
            for j in range(1, 6):
                total = total + tangent(y, TANGENT[i, j]) * strain[y][j]
            rows.append(total)
        stress[y] = tuple(rows)
    force = force_rows(stress, lower, upper, moves)
    return {
        y: tuple(MASS * nodes[y][c] + force[y][c] for c in range(3))
        for y in range(lower, upper + 1)
    }


def value_reader(low_ref, own_ref, high_ref):
    def read(y, c):
        if y < 0:
            return low_ref[c, y + 2]
        if y < 2:
            return own_ref[c, y]
        return high_ref[c, y - 2]

    return read


def read_rows(ref, lower, count):
    return {lower + k: tuple(ref[c, k] for c in range(3)) for k in range(count)}


def inside(rows, y, last_ref):
    keep = jnp.where(last_ref[0] == 1, 0.0, 1.0)
    rows[y] = tuple(v * keep for v in rows[y])


def write_rows(ref, rows, lower, count):
    for k in range(count):
        for c in range(3):
            ref[c, k] = rows[lower + k][c]


def row_dot(first, second):
    total = None
    for y in (0, 1):
        for c in range(3):
            term = first[y][c] * second[y][c]
            total = term if total is None else total + term
    return total


def pack_dots(ref, products):
    lane = lax.broadcasted_iota(jnp.int32, (1, DOTS), 1)
    packed = jnp.zeros((1, DOTS), F32)
    for k, product in enumerate(products):
        total = jnp.sum(jnp.sum(product, axis=0, keepdims=True), axis=1, keepdims=True)
        packed = packed + jnp.where(lane == k, total, 0.0)
    ref[...] = jnp.broadcast_to(packed[None], ref.shape)


def unpack_dots(ref, count):
    row = jnp.sum(ref[...].reshape(-1, DOTS), axis=0, keepdims=True)
    lane = lax.broadcasted_iota(jnp.int32, (1, DOTS), 1)
    return [
        jnp.sum(jnp.where(lane == k, row, 0.0), axis=1, keepdims=True) for k in range(count)
    ]


def basis_steps(marks_ref):
    lane = lax.broadcasted_iota(jnp.int32, (1, DOTS), 1)
    mark = jnp.sum(jnp.where(lane == MARK, marks_ref[...], 0.0), axis=1, keepdims=True)
    reach = 0.5 * BASIS * mark
    return MASS + reach, reach


def chebyshev(image, now, before, center, half):
    scale = 2.0 / half
    return {
        y: tuple((image[y][c] - center * now[y][c]) * scale - before[y][c] for c in range(3))
        for y in image
    }


def first_kernel(flags_ref, marks_ref, low_ref, own_ref, high_ref, v0_ref, v1_ref):
    read = value_reader(low_ref, own_ref, high_ref)
    moves = shifts(own_ref.shape[2:])
    center, half = basis_steps(marks_ref)
    stress = {y: tuple(read(y, i) for i in range(6)) for y in range(-2, 3)}
    force = force_rows(stress, -1, 2, moves)
    v0 = {y: tuple(read(y, LOAD + c) - force[y][c] for c in range(3)) for y in range(-1, 3)}
    inside(v0, 2, flags_ref)
    image = apply_rows(v0, read, 0, 1, moves)
    scale = 1.0 / half
    v1 = {y: tuple((image[y][c] - center * v0[y][c]) * scale for c in range(3)) for y in (0, 1)}
    write_rows(v0_ref, v0, -1, 4)
    write_rows(v1_ref, v1, 0, 2)


def next_two(flags_ref, marks_ref, read, moves, before, low_ref, own_ref, high_ref):
    center, half = basis_steps(marks_ref)
    now = read_rows(low_ref, -2, 2) | read_rows(own_ref, 0, 2) | read_rows(high_ref, 2, 2)
    after = chebyshev(apply_rows(now, read, -1, 2, moves), now, before, center, half)
    inside(after, 2, flags_ref)
    last = chebyshev(apply_rows(after, read, 0, 1, moves), after, now, center, half)
    return now, after, last


def second_kernel(
    flags_ref,
    marks_ref,
    low_ref,
    own_ref,
    high_ref,
    v0_ref,
    v1_low_ref,
    v1_ref,
    v1_high_ref,
    v2_ref,
    v3_ref,
):
    read = value_reader(low_ref, own_ref, high_ref)
    moves = shifts(own_ref.shape[2:])
    _, v2, v3 = next_two(
        flags_ref,
        marks_ref,
        read,
        moves,
        read_rows(v0_ref, -1, 4),
        v1_low_ref,
        v1_ref,
        v1_high_ref,
    )
    write_rows(v2_ref, v2, -1, 4)
    write_rows(v3_ref, v3, 0, 2)


def basis_pairs():
    return [(i, j) for i in range(6) for j in range(i, 6)]


def third_kernel(
    flags_ref,
    marks_ref,
    low_ref,
    own_ref,
    high_ref,
    v0_ref,
    v1_ref,
    v2_ref,
    v3_low_ref,
    v3_ref,
    v3_high_ref,
    v4_ref,
    v5_ref,
    dots_ref,
):
    read = value_reader(low_ref, own_ref, high_ref)
    moves = shifts(own_ref.shape[2:])
    v2 = read_rows(v2_ref, -1, 4)
    v3, v4, v5 = next_two(
        flags_ref, marks_ref, read, moves, v2, v3_low_ref, v3_ref, v3_high_ref
    )
    write_rows(v4_ref, v4, 0, 2)
    write_rows(v5_ref, v5, 0, 2)
    basis = [read_rows(v0_ref, -1, 4), read_rows(v1_ref, 0, 2), v2, v3, v4, v5]
    pack_dots(dots_ref, [row_dot(basis[i], basis[j]) for i, j in basis_pairs()])


def total_of(terms):
    total = None
    for term in terms:
        total = term if total is None else total + term
    return total


def place_planes(increment_ref, residual_ref, solved, left, basis, rows_ref, first):
    for ref, weights in ((increment_ref, solved), (residual_ref, left)):
        for y in (0, 1):
            for c in range(3):
                rows_ref[...] = total_of(w * basis[k][y][c] for k, w in enumerate(weights))
                for x in (0, 1):
                    ref[c, x, pl.ds(y, 1), :] = rows_ref[pl.ds(first + x, 1), :]


def fourth_kernel(
    flags_ref,
    marks_ref,
    sums_ref,
    v0_ref,
    v1_ref,
    v2_ref,
    v3_ref,
    v4_ref,
    v5_ref,
    increment_ref,
    residual_ref,
    trust_ref,
    rows_ref,
):
    center, half = basis_steps(marks_ref)
    dots = unpack_dots(sums_ref, 21)
    gram = {}
    for k, (i, j) in enumerate(basis_pairs()):
        gram[i, j] = gram[j, i] = dots[k]

    def image_of(p):
        count = len(p)
        image = []
        for i in range(count + 1):
            terms = []
            if i < count:
                terms.append(center * p[i])
            if i > 0:
                terms.append((half if i == 1 else 0.5 * half) * p[i - 1])
            if i + 1 < count:
                terms.append(0.5 * half * p[i + 1])
            image.append(total_of(terms))
        return image

    def product(p, q):
        return total_of(
            p[i] * total_of(gram[i, j] * q[j] for j in range(len(q))) for i in range(len(p))
        )

    def size(p, q):
        return total_of(
            jnp.abs(p[i]) * total_of(jnp.abs(gram[i, j]) * jnp.abs(q[j]) for j in range(len(q)))
            for i in range(len(p))
        )

    def combine(p, factor, q):
        longer = max(len(p), len(q))
        return [
            (p[k] + factor * q[k] if k < len(p) else factor * q[k]) if k < len(q) else p[k]
            for k in range(longer)
        ]

    solved = []
    left = [jnp.ones((1, 1), F32)]
    course = left
    norm = gram[0, 0]
    for step in range(5):
        image = image_of(course)
        bend = product(course, image)
        if step == 4:
            spread = size(course, image) / bend
            trusted = jnp.where((spread > 0.0) & (spread < TRUST) & trusted, 1, 0)
        alpha = norm / bend
        solved = combine(solved, alpha, course)
        left = combine(left, -alpha, image)
        if step < 4:
            fresh = product(left, left)
            if step == 3:
                spread = size(left, left) / fresh
                trusted = (spread > 0.0) & (spread < TRUST)
            course = combine(left, fresh / norm, course)
            norm = fresh
    basis = [
        read_rows(v0_ref, -1, 4),
        read_rows(v1_ref, 0, 2),
        read_rows(v2_ref, -1, 4),
        read_rows(v3_ref, 0, 2),
        read_rows(v4_ref, 0, 2),
        read_rows(v5_ref, 0, 2),
    ]
    trust_ref[...] = trusted
    place_planes(increment_ref, residual_ref, solved, left, basis, rows_ref, flags_ref[1])


def careful_first(low_ref, own_ref, high_ref, v0_ref, v1_ref):
    read = value_reader(low_ref, own_ref, high_ref)
    moves = shifts(own_ref.shape[2:])
    write_rows(v1_ref, apply_rows(read_rows(v0_ref, -1, 4), read, 0, 1, moves), 0, 2)


def careful_second(
    last_ref, low_ref, own_ref, high_ref, v0_ref, v1_low_ref, v1_ref, v1_high_ref, v2_ref, dots_ref
):
    read = value_reader(low_ref, own_ref, high_ref)
    moves = shifts(own_ref.shape[2:])
    v1 = read_rows(v1_low_ref, -2, 2) | read_rows(v1_ref, 0, 2) | read_rows(v1_high_ref, 2, 2)
    v2 = apply_rows(v1, read, -1, 2, moves)
    inside(v2, 2, last_ref)
    v0 = read_rows(v0_ref, -1, 4)
    write_rows(v2_ref, v2, -1, 4)
    pack_dots(
        dots_ref,
        [
            row_dot(a, b)
            for a, b in ((v0, v0), (v0, v1), (v0, v2), (v1, v1), (v1, v2))
        ],
    )


def careful_third(
    low_ref,
    own_ref,
    high_ref,
    v0_ref,
    v1_low_ref,
    v1_ref,
    v1_high_ref,
    v2_ref,
    sums_ref,
    r1_ref,
    r2_ref,
    w3_ref,
    coef_ref,
):
    read = value_reader(low_ref, own_ref, high_ref)
    moves = shifts(own_ref.shape[2:])
    m00, m01, m02, m11, m12 = unpack_dots(sums_ref, 5)
    a0 = m00 / m01
    n1 = m00 - 2.0 * a0 * m01 + a0 * a0 * m11
    b0 = n1 / m00
    e = 1.0 + b0
    a1 = n1 / (e * e * m01 - e * a0 * (m02 + m11) + a0 * a0 * m12)
    center = 0.5 * (1.0 / a0 + 1.0 / a1 + b0 / a0)
    v0 = read_rows(v0_ref, -1, 4)
    v1 = read_rows(v1_low_ref, -2, 2) | read_rows(v1_ref, 0, 2) | read_rows(v1_high_ref, 2, 2)
    v2 = read_rows(v2_ref, -1, 4)
    along, twice = a0 + a1 * e, a1 * a0
    r2 = {
        y: tuple(v0[y][c] - along * v1[y][c] + twice * v2[y][c] for c in range(3))
        for y in range(-1, 3)
    }
    image = apply_rows(r2, read, 0, 1, moves)
    scale = 1.0 / center
    w3 = {y: tuple(image[y][c] * scale - r2[y][c] for c in range(3)) for y in (0, 1)}
    r1 = {y: tuple(v0[y][c] - a0 * v1[y][c] for c in range(3)) for y in (0, 1)}
    write_rows(r1_ref, r1, 0, 2)
    write_rows(r2_ref, r2, 0, 2)
    write_rows(w3_ref, w3, 0, 2)
    lane = lax.broadcasted_iota(jnp.int32, (1, DOTS), 1)
    packed = jnp.zeros((1, DOTS), F32)
    for k, value in enumerate((a0, b0, a1, n1, center)):
        packed = packed + jnp.where(lane == k, value, 0.0)
    coef_ref[...] = packed


def careful_fourth(
    last_ref,
    low_ref,
    own_ref,
    high_ref,
    coef_ref,
    v0_ref,
    r1_ref,
    r2_ref,
    w3_low_ref,
    w3_ref,
    w3_high_ref,
    w4_ref,
    w5_ref,
    dots_ref,
):
    read = value_reader(low_ref, own_ref, high_ref)
    moves = shifts(own_ref.shape[2:])
    scale = 1.0 / unpack_dots(coef_ref, 5)[4]
    w3 = read_rows(w3_low_ref, -2, 2) | read_rows(w3_ref, 0, 2) | read_rows(w3_high_ref, 2, 2)
    image = apply_rows(w3, read, -1, 2, moves)
    w4 = {y: tuple(image[y][c] * scale - w3[y][c] for c in range(3)) for y in range(-1, 3)}
    inside(w4, 2, last_ref)
    image = apply_rows(w4, read, 0, 1, moves)
    w5 = {y: tuple(image[y][c] * scale - w4[y][c] for c in range(3)) for y in (0, 1)}
    write_rows(w4_ref, w4, 0, 2)
    write_rows(w5_ref, w5, 0, 2)
    v0 = read_rows(v0_ref, -1, 4)
    basis = [v0, read_rows(r1_ref, 0, 2), read_rows(r2_ref, 0, 2), w3, w4, w5]
    pack_dots(dots_ref, [row_dot(basis[i], basis[j]) for i, j in basis_pairs()])


def careful_fifth(
    flags_ref,
    coef_ref,
    sums_ref,
    v0_ref,
    r1_ref,
    r2_ref,
    w3_ref,
    w4_ref,
    w5_ref,
    increment_ref,
    residual_ref,
    rows_ref,
):
    a0, b0, a1, n1, center = unpack_dots(coef_ref, 5)
    dots = unpack_dots(sums_ref, 21)
    gram = {}
    for k, (i, j) in enumerate(basis_pairs()):
        gram[i, j] = gram[j, i] = dots[k]
    zero = jnp.zeros((1, 1), F32)
    one = jnp.ones((1, 1), F32)
    i0, i1 = 1.0 / a0, 1.0 / a1

    def image_of(p):
        return [
            i0 * p[0] - b0 * i0 * p[1],
            (i1 + b0 * i0) * p[1] - i0 * p[0],
            center * p[2] - i1 * p[1],
            center * (p[2] + p[3]),
            center * (p[3] + p[4]),
            center * p[4],
        ]

    def product(p, q):
        return total_of(
            p[i] * total_of(gram[i, j] * q[j] for j in range(6)) for i in range(6)
        )

    solved = [a0 + a1 * b0, a1, zero, zero, zero, zero]
    left = [zero, zero, one, zero, zero, zero]
    norm = gram[2, 2]
    ratio = norm / n1
    course = [ratio * b0, ratio, one, zero, zero, zero]
    for step in range(3):
        image = image_of(course)
        alpha = norm / product(course, image)
        solved = [s + alpha * p for s, p in zip(solved, course)]
        left = [r - alpha * q for r, q in zip(left, image)]
        if step < 2:
            fresh = product(left, left)
            ratio = fresh / norm
            course = [r + ratio * p for r, p in zip(left, course)]
            norm = fresh
    v0 = read_rows(v0_ref, -1, 4)
    basis = [v0] + [read_rows(ref, 0, 2) for ref in (r1_ref, r2_ref, w3_ref, w4_ref, w5_ref)]
    place_planes(increment_ref, residual_ref, solved, left, basis, rows_ref, flags_ref[1])


def local_call(kernel, outs, name, *args, flags=None, scratch=()):
    typed = [out if isinstance(out[0], tuple) else (out, F32) for out in outs]
    specs = [pl.BlockSpec(memory_space=pltpu.VMEM)] * len(args)
    if flags is not None:
        specs = [pl.BlockSpec(memory_space=pltpu.SMEM)] + specs
        args = (flags,) + args
    return pl.pallas_call(
        kernel,
        in_specs=specs,
        out_specs=[pl.BlockSpec(memory_space=pltpu.VMEM)] * len(outs),
        out_shape=[jax.ShapeDtypeStruct(*out) for out in typed],
        scratch_shapes=scratch,
        compiler_params=pltpu.CompilerParams(vmem_limit_bytes=48 * 1024 * 1024),
        name=name,
    )(*args)


def up_and_down(up, down):
    count = lax.axis_size(MICRO)
    forward = [(k, k + 1) for k in range(count - 1)]
    backward = [(k + 1, k) for k in range(count - 1)]
    return lax.ppermute(up, MICRO, forward), lax.ppermute(down, MICRO, backward)


def swapped(block):
    return lax.all_to_all(block, MICRO, split_axis=0, concat_axis=0, tiled=True)


def order_kernel(flags_ref, piece_0, piece_1, piece_2, piece_3, own_ref, edge_ref):
    pieces = [ref[...] for ref in (piece_0, piece_1, piece_2, piece_3)]
    for turn in range(4):

        @pl.when(flags_ref[1] == 2 * turn)
        def _():
            whole = jnp.concatenate([pieces[(k - turn) % 4] for k in range(4)], axis=2)
            own_ref[...] = whole
            edge_ref[...] = whole[:, :1]


def from_ring(block):
    count = lax.axis_size("macro")
    return [block] + [
        lax.ppermute(block, "macro", [(k, (k - shift) % count) for k in range(count)])
        for shift in range(1, count)
    ]


def shards(
    displacement,
    load,
    routes,
    counts,
    stiffness,
    precond,
    forcing,
    coupling,
    lame_first,
    lame_shear,
):
    planes, width, depth = displacement.shape[1:]
    points = planes * width * depth
    rows_x = lax.axis_size("macro")
    owners = lax.axis_size(MICRO)
    right = lax.ppermute(displacement, "macro", [(a + 1, a) for a in range(rows_x - 1)])
    above = lax.ppermute(displacement, MICRO, [(b + 1, b) for b in range(owners - 1)])
    corner = lax.ppermute(
        displacement,
        ("macro",) + MICRO,
        [
            ((a + 1) * owners + b + 1, a * owners + b)
            for a in range(rows_x - 1)
            for b in range(owners - 1)
        ],
    )
    place, mark, kept = local_call(
        functools.partial(rank_kernel, owners),
        (((8, points), jnp.int32), (1, 1), displacement.shape),
        "rank",
        lame_first.reshape(1, 1),
        lame_shear.reshape(1, 1),
        coupling[0].T,
        routes.reshape(1, points),
        counts.reshape(1, points),
        displacement,
    )
    (send,) = local_call(
        dispatch_kernel,
        ((owners, 2, 128),),
        "dispatch",
        place,
        mark,
        kept,
        right,
        above,
        corner,
    )
    send, forcing, coupling = lax.optimization_barrier((send, forcing, coupling))
    back, marks = micro_solve(
        swapped(send),
        stiffness[0],
        precond[0],
        forcing[0],
        coupling[0],
        lame_first[0],
        lame_shear[0],
    )
    (values,) = local_call(
        pick_kernel, ((FIELDS, width, planes, depth),), "pick", swapped(back), place, load
    )
    flags = jnp.stack(
        [
            (lax.axis_index(MICRO) == owners - 1).astype(jnp.int32),
            (lax.axis_index("macro") * planes).astype(jnp.int32),
        ]
    )
    whole = planes * rows_x
    own, edge = local_call(
        order_kernel,
        ((FIELDS, width, whole, depth), (FIELDS, 1, whole, depth)),
        "order",
        *from_ring(values),
        flags=flags,
    )
    low, high = up_and_down(own, edge)
    sets = (marks, low, own, high)
    two = (3, 2, whole, depth)
    four = (3, 4, whole, depth)
    v0, v1 = local_call(first_kernel, (four, two), "first_rows", *sets, flags=flags)
    v1_low, v1_high = up_and_down(v1, v1)
    v2, v3 = local_call(
        second_kernel, (four, two), "second_rows", *sets, v0, v1_low, v1, v1_high, flags=flags
    )
    v3_low, v3_high = up_and_down(v3, v3)
    v4, v5, dots = local_call(
        third_kernel,
        (two, two, (owners, 1, DOTS)),
        "third_rows",
        *sets,
        v0,
        v1,
        v2,
        v3_low,
        v3,
        v3_high,
        flags=flags,
    )
    mine = (3, planes, width, depth)
    scratch = [pltpu.VMEM((whole, depth), F32)]
    increment, residual, trust = local_call(
        fourth_kernel,
        (mine, mine, ((1, 1), jnp.int32)),
        "fourth_rows",
        marks,
        swapped(dots),
        v0,
        v1,
        v2,
        v3,
        v4,
        v5,
        flags=flags,
        scratch=scratch,
    )

    def careful():
        sets = (low, own, high)
        line = (1, DOTS)
        (u1,) = local_call(careful_first, (two,), "careful_first", *sets, v0)
        u1_low, u1_high = up_and_down(u1, u1)
        u2, dots = local_call(
            careful_second,
            (four, (owners, 1, DOTS)),
            "careful_second",
            *sets,
            v0,
            u1_low,
            u1,
            u1_high,
            flags=flags,
        )
        r1, r2, w3, coef = local_call(
            careful_third,
            (two, two, two, line),
            "careful_third",
            *sets,
            v0,
            u1_low,
            u1,
            u1_high,
            u2,
            swapped(dots),
        )
        w3_low, w3_high = up_and_down(w3, w3)
        w4, w5, dots = local_call(
            careful_fourth,
            (two, two, (owners, 1, DOTS)),
            "careful_fourth",
            *sets,
            coef,
            v0,
            r1,
            r2,
            w3_low,
            w3,
            w3_high,
            flags=flags,
        )
        return tuple(
            local_call(
                careful_fifth,
                (mine, mine),
                "careful_fifth",
                coef,
                swapped(dots),
                v0,
                r1,
                r2,
                w3,
                w4,
                w5,
                flags=flags,
                scratch=scratch,
            )
        )

    return lax.cond(trust[0, 0] == 1, lambda: (increment, residual), careful)


def solution(mesh):
    split = Mesh(
        mesh.devices.reshape(mesh.shape["macro"], 4, 8, 2),
        ("macro", "micro_0", "micro_1", "micro_2"),
    )
    placed = (
        P(None, "macro", MICRO, None),
        P(None, "macro", MICRO, None),
        P("macro", MICRO, None, None),
        P("macro", MICRO, None),
        P(MICRO, None, None),
        P(MICRO, None, None),
        P(MICRO, None, None),
        P(MICRO, None, None),
        P(MICRO),
        P(MICRO),
    )
    return jax.shard_map(
        shards,
        mesh=split,
        in_specs=placed,
        out_specs=(P(None, "macro", MICRO, None), P(None, "macro", MICRO, None)),
        check_vma=False,
    )
```
